32 devices in a mesh: dp: 8 (over z, x), tensor: 4 (over y, core).
Axes of the slice: x: 2, y: 2, z: 4, core: 2. Of those that a mesh axis runs over, the one named last changes fastest.
Arguments:
- tokens: bfloat16 [32768, 1024], P('dp', 'tensor'), may hold values from -6 to 6
- lengths: int32 [16], P('dp'), may hold values from 512 to 2048, as said below
- grad_out: bfloat16 [32768, 1024], P('dp', 'tensor'), may hold values from -6 to 6
- norm_gain: bfloat16 [1024], P('dp'), may hold values from 0.099609375 to 1.8984375
- w_gate: bfloat16 [1024, 2048], P('dp', 'tensor'), may hold values from -0.1875 to 0.1875
- w_value: bfloat16 [1024, 2048], P('dp', 'tensor'), may hold values from -0.1875 to 0.1875
- w_bc: bfloat16 [1024, 256], P('dp'), may hold values from -0.1875 to 0.1875
- w_dt: bfloat16 [1024, 32], P('dp', 'tensor'), may hold values from -0.1875 to 0.1875
- conv_x: float32 [5, 2048], P(None, 'tensor'), may hold values from -3 to 3
- conv_bc: float32 [5, 256], replicated, may hold values from -3 to 3
- dt_bias: float32 [32], P('tensor'), may hold values from -7 to -2.5
- a_log: float32 [32], P('tensor'), may hold values from 0 to 2.77
- skip_d: float32 [32], P('tensor'), may hold values from 0.35 to 2.75
- gate_gain: float32 [2048], P('tensor'), may hold values from 0.1 to 1.9
- w_out: bfloat16 [1024, 2048], P('dp', 'tensor'), may hold values from -0.125 to 0.125
Outputs:
- out: bfloat16 [32768, 1024], P('dp', 'tensor')
- grad_tokens: float32 [32768, 1024], P('dp', 'tensor')
- grad_norm_gain: float32 [1024], P(('dp', 'tensor'))
- grad_w_gate: float32 [1024, 2048], P('dp', 'tensor')
- grad_w_value: float32 [1024, 2048], P('dp', 'tensor')
- grad_w_bc: float32 [1024, 256], P(('dp', 'tensor'))
- grad_w_dt: float32 [1024, 32], P('dp', 'tensor')
- grad_conv_x: float32 [5, 2048], P(None, 'tensor')
- grad_conv_bc: float32 [5, 256], replicated
- grad_dt_bias: float32 [32], P('tensor')
- grad_a_log: float32 [32], P('tensor')
- grad_skip_d: float32 [32], P('tensor')
- grad_gate_gain: float32 [2048], P('tensor')
- grad_w_out: float32 [1024, 2048], P('dp', 'tensor')
The draws below stay inside these ranges and needn't reach their ends.
Inputs may be any that keep to these rules, and one draw needn't show every extreme that they name: Sequence i occupies the first lengths[i] of its 2048 slots; the rest is padding. Sequence 0 is full.
All inputs are finite; a program needn't handle non-finite values.
Results may differ from the reference program's by a relative error of at most 0.0085.
Values may be sent and summed in bfloat16 or wider, within the bound.
No kernel may reach another device: no remote copies, remote signals or barrier semaphores. Data moves between devices by JAX's collectives and lax.ppermute only.
A program may use at most 192 MiB of HBM per device.

```python
import jax
import jax.numpy as jnp
from jax import lax

D = 1024
HEADS = 32
STATE = 128
CONV = 4
GROUP = 256
SEQ_LEN = 2048
INNER = 2048
SEQS = 16
TOKENS = 32768


def draw_lengths(key, part):
    drawn = jax.random.randint(key, (SEQS,), SEQ_LEN // 4, SEQ_LEN + 1)
    return drawn.at[0].set(SEQ_LEN).astype(jnp.int32)


def draw_skip_d(key, part):
    ramp = 0.5 + 1.5 * jnp.arange(HEADS, dtype=jnp.float32) / (HEADS - 1)
    jitter = jnp.exp(0.15 * jnp.clip(jax.random.normal(key, (HEADS,), jnp.float32), -2.0, 2.0))
    return (ramp * jitter).astype(jnp.float32)


def strengthened(array, stream_key, source, target, parts, factor):
    owner, partner = [(jnp.arange(array.shape[dim]) // (array.shape[dim] // parts)).reshape([-1 if axis == dim else 1 for axis in range(array.ndim)]) for dim in (source, target)]
    chosen = jax.random.permutation(stream_key, parts)[partner]
    strong = (owner == chosen) | (owner == (partner + parts // 2) % parts)
    return jnp.where(strong, factor * array, array)


def levels(stream_key, extent, split, smallest, top_value):
    factor_of = 1.0
    for position, blocks in split:
        steps = jax.random.uniform(jax.random.fold_in(jax.random.fold_in(stream_key, 6), position), (blocks,), jnp.float32, smallest / len(split), top_value / len(split))
        factor_of = factor_of * jnp.repeat(jnp.exp(steps), extent[position] // blocks).reshape((-1,) + (1,) * (len(extent) - 1 - position))
    return factor_of


def noise(stream_key, shape, spread, reach, pieces=(), kind=jnp.bfloat16):
    entries = spread * jax.random.normal(stream_key, shape, jnp.float32)
    if pieces:
        entries = entries * levels(stream_key, shape, pieces, -0.22, 0.18)
    return jnp.clip(entries, -reach, reach).astype(kind)


def heavy_noise(own_key, shape, width, limit, shards, heavy, kind=jnp.bfloat16):
    values = width * jax.random.normal(own_key, shape, jnp.float32)
    if shards:
        values = values * levels(own_key, shape, shards, -0.22, 0.18)
    return jnp.clip(strengthened(values, jax.random.fold_in(own_key, 3), *heavy), -limit, limit).astype(kind)


def setup_inputs(seed: int = 0) -> dict:
    splits = jax.random.split(jax.random.key(seed), 16)
    return {
        "tokens": noise(splits[0], (TOKENS, D), 1.0, 6.0, ((0, 8), (1, 4))),
        "lengths": draw_lengths(jax.random.fold_in(splits[15], 71), 0),
        "grad_out": heavy_noise(splits[2], (TOKENS, D), 1.0, 6.0, ((0, 8), (1, 4)), (0, 1, 8, 2.0)),
        "norm_gain": jnp.clip(1.0 + 0.18 * jax.random.normal(splits[3], (D,), jnp.float32), 0.099609375, 1.8984375).astype(jnp.bfloat16),
        "w_gate": noise(splits[4], (D, INNER), D ** -0.5, 0.1875, ((0, 8), (1, 4))),
        "w_value": noise(splits[5], (D, INNER), D ** -0.5, 0.1875, ((0, 8), (1, 4))),
        "w_bc": noise(splits[6], (D, 2 * STATE), D ** -0.5, 0.1875, ((0, 8),)),
        "w_dt": noise(splits[7], (D, HEADS), D ** -0.5, 0.1875, ((0, 8), (1, 4))),
        "conv_x": noise(splits[8], (CONV + 1, INNER), CONV ** -0.5, 3.0, ((1, 4),), jnp.float32),
        "conv_bc": noise(splits[9], (CONV + 1, 2 * STATE), CONV ** -0.5, 3.0, (), jnp.float32),
        "dt_bias": jnp.clip(-7.0 + 4.5 * jax.random.uniform(splits[10], (HEADS,), jnp.float32) ** levels(splits[10], (HEADS,), ((0, 4),), -0.2, 0.2), -7.0, -2.5),
        "a_log": jnp.clip(2.77 * jax.random.uniform(splits[11], (HEADS,), jnp.float32) ** levels(splits[11], (HEADS,), ((0, 4),), -0.2, 0.2), 0.0, 2.77),
        "skip_d": draw_skip_d(jax.random.fold_in(splits[15], 71), 0),
        "gate_gain": jnp.clip(1.0 + 0.18 * jax.random.normal(splits[13], (INNER,), jnp.float32), 0.1, 1.9),
        "w_out": noise(splits[14], (D, INNER), INNER ** -0.5, 0.125, ((0, 8), (1, 4))),
    }


@jax.custom_vjp
def low(v):
    return lax.optimization_barrier(v.astype(jnp.bfloat16)).astype(jnp.float32)

@jax.custom_vjp
def low_back(v):
    return v

def low_keep(v):
    return (low(v), None)

def low_pass(kept, grad):
    return (grad,)

def back_keep(v):
    return (v, None)

def back_low(kept, grad):
    return (low(grad),)
low.defvjp(low_keep, low_pass)
low_back.defvjp(back_keep, back_low)
epsilon = 1e-05

def matmul(left, right):
    return jnp.dot(left, right, precision=lax.Precision.HIGHEST)

def causal_conv(signal, kernel):
    window = kernel.shape[0] - 1
    length = signal.shape[0]
    padded = jnp.concatenate([jnp.zeros((window - 1, signal.shape[1]), jnp.float32), signal], 0)
    summed = jnp.broadcast_to(kernel[window], signal.shape)
    for offset in range(window):
        summed = summed + kernel[offset] * padded[offset:offset + length]
    return summed

def group_scan(values, step_sizes, decay_rates, inputs_b, inputs_c):
    length, head_count, head_width = values.shape
    blocks = length // GROUP
    values = values.reshape(blocks, GROUP, head_count, head_width)
    step_sizes = step_sizes.reshape(blocks, GROUP, head_count)
    inputs_b = inputs_b.reshape(blocks, GROUP, -1)
    inputs_c = inputs_c.reshape(blocks, GROUP, -1)
    log_decay = jnp.transpose(step_sizes * decay_rates, (0, 2, 1))
    running = jnp.cumsum(log_decay, axis=2)
    causal = jnp.arange(GROUP)[:, None] >= jnp.arange(GROUP)[None, :]
    decay_grid = jnp.exp(jnp.where(causal, running[..., :, None] - running[..., None, :], -jnp.inf))
    intersection = jnp.einsum('bqn,bsn->bqs', inputs_c, inputs_b, precision=lax.Precision.HIGHEST)
    weighted = values * step_sizes[..., None]
    inner_part = jnp.einsum('bhqs,bshp->bqhp', intersection[:, None] * decay_grid, weighted, precision=lax.Precision.HIGHEST)
    to_end = jnp.exp(running[..., -1:] - running)
    states = jnp.einsum('bsn,bhs,bshp->bhpn', inputs_b, to_end, weighted, precision=lax.Precision.HIGHEST)
    totals = running[..., -1]
    through = jnp.cumsum(totals, axis=0)
    before = through - totals
    earlier = jnp.arange(blocks)[:, None] > jnp.arange(blocks)[None, :]
    carry_weights = jnp.exp(jnp.where(earlier[..., None], before[:, None, :] - through[None, :, :], -jnp.inf))
    incoming = jnp.einsum('cdh,dhpn->chpn', carry_weights, states, precision=lax.Precision.HIGHEST)
    outer_part = jnp.einsum('bqn,bhpn,bhq->bqhp', inputs_c, incoming, jnp.exp(running), precision=lax.Precision.HIGHEST)
    return (inner_part + outer_part).reshape(length, head_count, head_width)

def mixer(gate_in, value_in, shared_in, step_in, conv_value, conv_shared, step_bias, log_rate, skip_gain):
    length = value_in.shape[0]
    head_count = step_in.shape[1]
    state_size = shared_in.shape[1] // 2
    convolved = jax.nn.silu(causal_conv(value_in, conv_value))
    shared = jax.nn.silu(causal_conv(shared_in, conv_shared))
    step_sizes = jax.nn.softplus(step_in + step_bias)
    decay_rates = -jnp.exp(log_rate)
    values = convolved.reshape(length, head_count, -1)
    scanned = group_scan(values, step_sizes, decay_rates, shared[:, :state_size], shared[:, state_size:])
    mixed_out = scanned + skip_gain[:, None] * values
    return mixed_out.reshape(length, -1) * jax.nn.silu(gate_in)

def branch(sequence, params):
    norm_gain, w_gate, w_value, w_bc, w_dt, conv_x, conv_bc, dt_bias, a_log, skip_d, gate_gain, w_out = params
    inverse_rms = lax.rsqrt(lax.optimization_barrier(jnp.mean(sequence * sequence, -1, keepdims=True)) + epsilon)
    normed = low(sequence * inverse_rms * norm_gain)
    gate_proj = low_back(matmul(normed, w_gate))
    value_proj = low_back(matmul(normed, w_value))
    shared_in = low_back(matmul(normed, w_bc))
    step_in = low_back(matmul(normed, w_dt))
    mixed_out = mixer(gate_proj, value_proj, shared_in, step_in, conv_x, conv_bc, dt_bias, a_log, skip_d)
    inverse_gate = lax.rsqrt(lax.optimization_barrier(jnp.mean(mixed_out * mixed_out, -1, keepdims=True)) + epsilon)
    normed_out = low(mixed_out * inverse_gate * gate_gain)
    return matmul(normed_out, w_out.T)

def reference(tokens, lengths, grad_out, norm_gain, w_gate, w_value, w_bc, w_dt, conv_x, conv_bc, dt_bias, a_log, skip_d, gate_gain, w_out):
    params = tuple((item.astype(jnp.float32) for item in (norm_gain, w_gate, w_value, w_bc, w_dt, conv_x, conv_bc, dt_bias, a_log, skip_d, gate_gain, w_out)))
    inputs = tokens.astype(jnp.float32).reshape(SEQS, SEQ_LEN, D)
    validity = (jnp.arange(SEQ_LEN)[None, :] < lengths[:, None]).astype(jnp.float32)[..., None]

    def forward(inputs, params):

        def single_sequence(packed):
            sequence, keeper = packed
            return sequence + keeper * branch(sequence, params)
        return lax.map(jax.checkpoint(single_sequence), (inputs, validity))
    outputs, pullback = jax.vjp(forward, inputs, params)
    cotangent = grad_out.astype(jnp.float32).reshape(SEQS, SEQ_LEN, D) * validity
    grad_inputs, grad_params = pullback(cotangent)
    return (outputs.reshape(TOKENS, D).astype(jnp.bfloat16), grad_inputs.reshape(TOKENS, D), grad_params[0], grad_params[1], grad_params[2], grad_params[3], grad_params[4], grad_params[5], grad_params[6], grad_params[7], grad_params[8], grad_params[9], grad_params[10], grad_params[11])
```

```python
import functools

import jax
import jax.numpy as jnp
from jax import lax
from jax.experimental import pallas as pl
from jax.experimental.pallas import tpu as pltpu
from jax.sharding import PartitionSpec as P

SEQ_LEN = 2048
Q = 256
HALF = 128
F32 = jnp.float32
BF16 = jnp.bfloat16
epsilon = 1e-05
NEG = -1e30


def nn(a, b):
    return lax.dot_general(a, b, (((1,), (0,)), ((), ())), preferred_element_type=F32)


def nt(a, b):
    return lax.dot_general(a, b, (((1,), (1,)), ((), ())), preferred_element_type=F32)


def split3(a):
    high = a.astype(BF16)
    rest = a - high.astype(F32)
    mid = rest.astype(BF16)
    low = (rest - mid.astype(F32)).astype(BF16)
    return high, mid, low


def times_ones(a, ones):
    rows = a.shape[0]
    got = nn(jnp.concatenate(split3(a), 0), ones)
    return got[:rows] + got[rows : 2 * rows] + got[2 * rows :]


def twice(a):
    return jnp.concatenate([a, a], 1)


def fold(a):
    return a[:, :HALF] + a[:, HALF:]


def triangle(keep):
    row = lax.broadcasted_iota(jnp.int32, (Q, Q), 0)
    col = lax.broadcasted_iota(jnp.int32, (Q, Q), 1)
    return jnp.where(keep(row, col), 1.0, 0.0).astype(BF16)


def conv(raw, tail, taps):
    ext = jnp.concatenate([tail, raw], 1)
    total = twice(taps[4]) + twice(taps[3]) * raw
    for k in range(1, 4):
        total = total + twice(taps[3 - k]) * pltpu.roll(ext, k, 1)[:, HALF:]
    return total


def conv_back(grad, head, taps):
    ext = jnp.concatenate([grad, head], 1)
    shifted = [grad] + [pltpu.roll(ext, 3 * HALF - k, 1)[:, :Q] for k in range(1, 4)]
    total = twice(taps[3]) * grad
    for k in range(1, 4):
        total = total + twice(taps[3 - k]) * shifted[k]
    return total, shifted


def decay_blocks(run_row, run_col, upper):
    early, late = run_row[:, :HALF], run_row[:, HALF:]
    col_early = jnp.broadcast_to(run_col[:HALF], (HALF, HALF))
    col_late = jnp.broadcast_to(run_col[HALF:], (HALF, HALF))
    first = jnp.exp(jnp.where(upper, early - col_early, NEG))
    cross = jnp.exp(late - col_early)
    second = jnp.exp(jnp.where(upper, late - col_late, NEG))
    return first, cross, second


def stack_blocks(first, cross, second):
    zero = jnp.zeros((HALF, HALF), first.dtype)
    return jnp.concatenate(
        [jnp.concatenate([first, cross], 1), jnp.concatenate([zero, second], 1)], 0
    )


def intersection(b_rows, c_rows):
    b_time = jnp.transpose(b_rows)
    b_high = b_time.astype(BF16)
    b_low = (b_time - b_high.astype(F32)).astype(BF16)
    c_high = c_rows.astype(BF16)
    c_low = (c_rows - c_high.astype(F32)).astype(BF16)
    return nn(
        jnp.concatenate([b_high, b_low, b_high], 1), jnp.concatenate([c_high, c_high, c_low], 0)
    )


def rms_scale(xs, width):
    total = xs[0] * xs[0]
    for x in xs[1:]:
        total = total + x * x
    return lax.rsqrt(jnp.sum(total, -1, keepdims=True) / width + epsilon)


def gain_row(wt_ref, base, heads):
    return wt_ref[base : base + 16, :].astype(F32)[heads : heads + 1]


def softplus(a):
    return jnp.maximum(a, 0.0) + jnp.log1p(jnp.exp(-jnp.abs(a)))


def upper_half():
    row = lax.broadcasted_iota(jnp.int32, (HALF, HALF), 0)
    return row <= lax.broadcasted_iota(jnp.int32, (HALF, HALF), 1)


def valid_row(block, length):
    pos = block * Q + lax.broadcasted_iota(jnp.int32, (1, Q), 1)
    return jnp.where(pos < length, 1.0, 0.0)


def forward_kernel(len_ref, *refs, seq, inner, heads, width, aliased):
    x_refs, (wt_ref, chan_ref, bcc_ref, headc_ref) = refs[:4], refs[4:8]
    refs = refs[8 + aliased :]
    (norm_ref, gate_ref, val_ref, z_ref, y_ref, m_ref, bc_ref, bcz_ref) = refs[:8]
    (step_ref, run_ref, state_ref, stat_ref, proj, vtail, btail, state) = refs[8:]
    block = pl.program_id(0)
    length = len_ref[seq]
    per = inner // heads
    part = width // 4
    states = bc_ref.shape[0] // 2

    @pl.when(block == 0)
    def _():
        vtail[...] = jnp.zeros_like(vtail)
        btail[...] = jnp.zeros_like(btail)
        state[...] = jnp.zeros_like(state)

    @pl.when(block * Q >= length)
    def _():
        norm_ref[...] = jnp.zeros_like(norm_ref)
        stat_ref[...] = jnp.zeros_like(stat_ref)

    @pl.when(block * Q < length)
    def _():
        base = 2 * inner + 2 * states
        gain = gain_row(wt_ref, base, heads)
        xs = [ref[...].astype(F32) for ref in x_refs]
        inv = rms_scale(xs, width)
        for k in range(4):
            cols = slice(k * part, (k + 1) * part)
            norm_ref[:, cols] = (xs[k] * inv * gain[:, cols]).astype(BF16)
        proj[...] = nt(wt_ref[: base + 16, :], norm_ref[...])

        raw = proj[2 * inner : base, :]
        bc_ref[...] = raw
        bcz = conv(raw, btail[...], [bcc_ref[j] for j in range(5)])
        btail[...] = raw[:, HALF:]
        bcz_ref[...] = bcz
        shared = bcz * jax.nn.sigmoid(bcz)
        b_rows, c_rows = shared[:states], shared[states:]
        cb = intersection(b_rows, c_rows)
        cb_blocks = (cb[:HALF, :HALF], cb[:HALF, HALF:], cb[HALF:, HALF:])
        b_low, c_low = b_rows.astype(BF16), c_rows.astype(BF16)

        step_raw = proj[base : base + heads, :] + twice(headc_ref[0])
        step_ref[...] = step_raw
        steps = softplus(step_raw)
        running = times_ones(steps * twice(headc_ref[1]), triangle(lambda s, t: s <= t))
        run_ref[...] = running
        run_cols = jnp.transpose(running)
        ends = running[:, Q - 1 :]
        grow = jnp.exp(running)
        to_end = jnp.exp(ends - running)
        whole = jnp.exp(ends)
        upper = upper_half()

        state_ref[...] = state[...]
        squares = jnp.zeros((1, Q), F32)
        for h in range(heads):
            rows = slice(h * per, (h + 1) * per)
            raw_v = proj[inner + h * per : inner + (h + 1) * per, :]
            gate = proj[rows, :]
            val_ref[rows, :] = raw_v
            gate_ref[rows, :] = gate
            z = conv(raw_v, vtail[rows, :], [chan_ref[j, rows, :] for j in range(5)])
            vtail[rows, :] = raw_v[:, HALF:]
            z_ref[rows, :] = z
            v = z * jax.nn.sigmoid(z)
            w = v * steps[h : h + 1]
            decays = decay_blocks(running[h : h + 1], run_cols[:, h : h + 1], upper)
            grid = stack_blocks(*[(d * g).astype(BF16) for d, g in zip(decays, cb_blocks)])
            old = state[rows, :]
            y = nn(w.astype(BF16), grid) + nn(old.astype(BF16), c_low) * grow[h : h + 1]
            y_ref[rows, :] = y
            fresh = nt((w * to_end[h : h + 1]).astype(BF16), b_low)
            state[rows, :] = old * whole[h : h + 1] + fresh
            u = y + twice(chan_ref[6, rows, :]) * v
            m = u * gate * jax.nn.sigmoid(gate)
            m_ref[rows, :] = m
            squares = squares + jnp.sum(m * m, 0, keepdims=True)
        stat_ref[...] = squares


def middle_kernel(
    len_ref, c0, c1, c2, c3, wo_ref, chan_ref, m_ref, sq_ref,
    nout_ref, b0, b1, b2, b3, gno_ref, stat_ref, gain_acc, nout, *, inner, inner_all, width,
):
    seq, block = pl.program_id(0), pl.program_id(1)
    length = len_ref[seq]
    part = width // 4

    @pl.when((seq == 0) & (block == 0))
    def _():
        gain_acc[...] = jnp.zeros_like(gain_acc)

    @pl.when(block * Q >= length)
    def _():
        nout_ref[...] = jnp.zeros_like(nout_ref)
        stat_ref[...] = jnp.zeros_like(stat_ref)
        for ref in (b0, b1, b2, b3):
            ref[...] = jnp.zeros_like(ref)

    @pl.when(block * Q < length)
    def _():
        valid = valid_row(block, length)
        scale = lax.rsqrt(sq_ref[...] / inner_all + epsilon) * valid
        cot = jnp.concatenate([ref[...] for ref in (c0, c1, c2, c3)], 1)
        gno_ref[...] = nt(wo_ref[...], cot) * valid
        inners = jnp.zeros((1, Q), F32)
        for lo in range(0, inner, 64):
            rows = slice(lo, lo + 64)
            gain = twice(chan_ref[5, rows, :])
            m = m_ref[rows, :]
            gno = gno_ref[rows, :]
            nout[rows, :] = (m * scale * gain).astype(BF16)
            inners = inners + jnp.sum(gno * gain * m, 0, keepdims=True)
            gain_acc[rows, :] += fold(gno * m * scale)
        stat_ref[...] = inners
        nout_time = jnp.transpose(nout[...])
        nout_ref[...] = nout_time
        branch = nn(nout_time, wo_ref[...])
        for k, ref in enumerate((b0, b1, b2, b3)):
            ref[...] = branch[:, k * part : (k + 1) * part].astype(BF16)


def backward_kernel(len_ref, *refs, seq, inner, inner_all, heads, width, blocks):
    x_refs, (wt_ref, chan_ref, bcc_ref, headc_ref) = refs[:4], refs[4:8]
    (gate_ref, val_ref, z_ref, y_ref, gno_ref, bc_ref, bcz_ref) = refs[8:15]
    (step_ref, run_ref, state_ref, sq_ref, stat_ref) = refs[15:20]
    low_ref, g_refs, (chan_acc, bc_acc, head_acc, norm_acc) = refs[20], refs[21:25], refs[25:29]
    low, gstate, vhead, bhead, dcb, wdec, gudec = refs[29:]
    step = pl.program_id(0)
    block = blocks - 1 - step
    length = len_ref[seq]
    per = inner // heads
    part = width // 4
    states = bc_ref.shape[0] // 2
    base = 2 * inner + 2 * states

    @pl.when(step == 0)
    def _():
        chan_acc[...] = jnp.zeros_like(chan_acc)
        bc_acc[...] = jnp.zeros_like(bc_acc)
        head_acc[...] = jnp.zeros_like(head_acc)
        norm_acc[...] = jnp.zeros_like(norm_acc)
        low[base:, :] = jnp.zeros_like(low[base:, :])
        gstate[...] = jnp.zeros_like(gstate)
        vhead[...] = jnp.zeros_like(vhead)
        bhead[...] = jnp.zeros_like(bhead)

    @pl.when(block * Q >= length)
    def _():
        low_ref[...] = jnp.zeros_like(low_ref)
        for ref in g_refs:
            ref[...] = jnp.zeros_like(ref)

    @pl.when(block * Q < length)
    def _():
        inv_gate = lax.rsqrt(sq_ref[...] / inner_all + epsilon)
        pull = inv_gate * inv_gate * inv_gate * stat_ref[...] / inner_all

        bcz = bcz_ref[...]
        sig = jax.nn.sigmoid(bcz)
        shared = bcz * sig
        shared_slope = sig * (1.0 + bcz * (1.0 - sig))
        b_rows, c_rows = shared[:states], shared[states:]
        cb = intersection(b_rows, c_rows)
        cb_blocks = (cb[:HALF, :HALF], cb[:HALF, HALF:], cb[HALF:, HALF:])
        b_low, c_low = b_rows.astype(BF16), c_rows.astype(BF16)

        step_raw = step_ref[...]
        steps = softplus(step_raw)
        running = run_ref[...]
        run_cols = jnp.transpose(running)
        ends = running[:, Q - 1 :]
        grow = jnp.exp(running)
        to_end = jnp.exp(ends - running)
        whole = jnp.exp(ends)
        upper = upper_half()

        direct, both, after, through = [], [], [], []
        for h in range(heads):
            rows = slice(h * per, (h + 1) * per)
            gate, z, y, gno = gate_ref[rows, :], z_ref[rows, :], y_ref[rows, :], gno_ref[rows, :]
            gain = twice(chan_ref[5, rows, :])
            skip = twice(chan_ref[6, rows, :])
            sig_g = jax.nn.sigmoid(gate)
            silu_g = gate * sig_g
            sig_z = jax.nn.sigmoid(z)
            v = z * sig_z
            u = y + skip * v
            m = u * silu_g
            gm = inv_gate * gain * gno - m * pull
            low[rows, :] = (gm * u * (sig_g * (1.0 + gate * (1.0 - sig_g)))).astype(BF16)
            gu = gm * silu_g
            chan_acc[5, rows, :] += fold(gu * v)
            w = v * steps[h : h + 1]
            w_low, gu_low = w.astype(BF16), gu.astype(BF16)
            decays = decay_blocks(running[h : h + 1], run_cols[:, h : h + 1], upper)
            grid = stack_blocks(*[(d * g).astype(BF16) for d, g in zip(decays, cb_blocks)])
            gw_in = nt(gu_low, grid)
            pair = nn(jnp.transpose(w_low), gu_low)
            pieces = (pair[:HALF, :HALF], pair[:HALF, HALF:], pair[HALF:, HALF:])
            for i in range(3):
                if h == 0:
                    dcb[i] = decays[i] * pieces[i]
                else:
                    dcb[i] += decays[i] * pieces[i]
            gs = gstate[rows, :]
            gs_low = gs.astype(BF16)
            gw_out = nn(gs_low, b_low) * to_end[h : h + 1]
            gw = gw_in + gw_out
            direct.append(jnp.sum(gw * v, 0, keepdims=True))
            both.append(
                jnp.sum(gu_low.astype(F32) * y - gw_in * w_low.astype(F32), 0, keepdims=True)
            )
            after.append(jnp.sum(gw_out * w, 0, keepdims=True))
            through.append(
                jnp.sum(gs * state_ref[rows, :], 0, keepdims=True) * whole[h : h + 1]
            )
            gud = (gu * grow[h : h + 1]).astype(BF16)
            gudec[rows, :] = gud
            wdec[rows, :] = (w * to_end[h : h + 1]).astype(BF16)
            gz = (skip * gu + gw * steps[h : h + 1]) * (sig_z * (1.0 + z * (1.0 - sig_z)))
            taps = [chan_ref[j, rows, :] for j in range(4)]
            gv, shifted = conv_back(gz, vhead[rows, :], taps)
            vhead[rows, :] = gz[:, :HALF]
            raw_v = val_ref[rows, :]
            for k in range(4):
                chan_acc[3 - k, rows, :] += fold(shifted[k] * raw_v)
            chan_acc[4, rows, :] += fold(gz)
            low[inner + h * per : inner + (h + 1) * per, :] = gv.astype(BF16)

        direct = jnp.concatenate(direct, 0)
        both = jnp.concatenate(both, 0)
        after = jnp.concatenate(after, 0)
        through = jnp.sum(jnp.concatenate(through, 0), -1, keepdims=True)
        g_decay = (
            times_ones(both, triangle(lambda t, r: t >= r))
            + times_ones(after, triangle(lambda s, r: s < r))
            + through
        )
        head_acc[1] += fold(steps * g_decay)
        g_step = (direct + twice(headc_ref[1]) * g_decay) * jax.nn.sigmoid(step_raw)
        head_acc[0] += fold(g_step)
        low[base : base + 16, :] = jnp.concatenate(
            [g_step, jnp.zeros((16 - heads, Q), F32)], 0
        ).astype(BF16)

        dcb_low = stack_blocks(*[dcb[i].astype(BF16) for i in range(3)])
        gud, wd = gudec[...], wdec[...]
        gs_old = gstate[...]
        g_c = nn(b_low, dcb_low) + nn(jnp.transpose(state_ref[...]).astype(BF16), gud)
        g_b = nt(c_low, dcb_low) + nn(jnp.transpose(gs_old).astype(BF16), wd)
        fresh = nt(gud, c_low)
        for h in range(heads):
            rows = slice(h * per, (h + 1) * per)
            gstate[rows, :] = gs_old[rows] * whole[h : h + 1] + fresh[rows]
        gbcz = jnp.concatenate([g_b, g_c], 0) * shared_slope
        gbc, shifted = conv_back(gbcz, bhead[...], [bcc_ref[j] for j in range(4)])
        bhead[...] = gbcz[:, :HALF]
        raw = bc_ref[...]
        for k in range(4):
            bc_acc[3 - k] += fold(shifted[k] * raw)
        bc_acc[4] += fold(gbcz)
        low[2 * inner : base, :] = gbc.astype(BF16)

        lows = jnp.transpose(low[...])
        low_ref[...] = lows
        g_norm = nn(lows, wt_ref[...])
        gain = gain_row(wt_ref, base, heads)
        xs = [ref[...].astype(F32) for ref in x_refs]
        inv = rms_scale(xs, width)
        prod = None
        for k in range(4):
            cols = slice(k * part, (k + 1) * part)
            here = g_norm[:, cols] * xs[k]
            norm_acc[:, cols] += jnp.sum((here * inv).reshape(Q // 8, 8, part), 0)
            weighted = here * gain[:, cols]
            prod = weighted if prod is None else prod + weighted
        pull_x = inv * inv * inv * (jnp.sum(prod, -1, keepdims=True) / width)
        for k in range(4):
            cols = slice(k * part, (k + 1) * part)
            g_refs[k][...] = (inv * gain[:, cols] * g_norm[:, cols] - xs[k] * pull_x).astype(BF16)


def shape(dims, kind=F32):
    return jax.ShapeDtypeStruct(dims, kind)


def params(count):
    return pltpu.CompilerParams(
        dimension_semantics=("arbitrary",) * count, vmem_limit_bytes=60 << 20
    )


def fixed(array):
    rank = array.ndim
    return pl.BlockSpec(array.shape, lambda *_: (0,) * rank, pipeline_mode=pl.Buffered(1))


def run_forward(seq, seqs, lengths, xs, wt, chan, bcc, headc, before):
    part = xs[0].shape[1]
    width = 4 * part
    inner, heads, states2 = chan.shape[1], headc.shape[1], bcc.shape[1]
    blocks = SEQ_LEN // Q
    rows = seqs * SEQ_LEN
    at = lambda c: seq * blocks + c
    col = lambda n: pl.BlockSpec((n, Q), lambda c, lens: (0, at(c)))
    out_shape = [
        shape((rows, width), BF16),
        *[shape((inner, rows))] * 5,
        *[shape((states2, rows))] * 2,
        *[shape((heads, rows))] * 2,
        shape((seqs * blocks * inner, states2 // 2)),
        shape((1, SEQ_LEN)),
    ]
    out_specs = [
        pl.BlockSpec((Q, width), lambda c, lens: (at(c), 0)),
        *[col(inner)] * 5,
        *[col(states2)] * 2,
        *[col(heads)] * 2,
        pl.BlockSpec((inner, states2 // 2), lambda c, lens: (at(c), 0)),
        pl.BlockSpec((1, Q), lambda c, lens: (0, c)),
    ]
    consts = (wt, chan, bcc, headc)
    return pl.pallas_call(
        functools.partial(
            forward_kernel,
            seq=seq,
            inner=inner,
            heads=heads,
            width=width,
            aliased=len(before),
        ),
        out_shape=out_shape,
        grid_spec=pltpu.PrefetchScalarGridSpec(
            num_scalar_prefetch=1,
            grid=(blocks,),
            in_specs=[
                *[pl.BlockSpec((Q, part), lambda c, lens: (c, 0))] * 4,
                *[fixed(array) for array in consts],
                *[pl.BlockSpec(memory_space=pl.ANY)] * len(before),
            ],
            out_specs=out_specs,
            scratch_shapes=[
                pltpu.VMEM((2 * inner + states2 + 16, Q), F32),
                pltpu.VMEM((inner, HALF), F32),
                pltpu.VMEM((states2, HALF), F32),
                pltpu.VMEM((inner, states2 // 2), F32),
            ],
        ),
        input_output_aliases={9 + i: i for i in range(len(before))},
        compiler_params=params(1),
        name="mixer_forward",
    )(lengths, *xs, *consts, *before)


def run_middle(lengths, cots, wo, chan, m, squares, inner_all):
    rows, part = cots[0].shape
    width = 4 * part
    inner = wo.shape[0]
    blocks = SEQ_LEN // Q
    at = lambda q, c: q * blocks + c
    piece = pl.BlockSpec((Q, part), lambda q, c, lens: (at(q, c), 0))
    col = lambda n: pl.BlockSpec((n, Q), lambda q, c, lens: (0, at(q, c)))
    return pl.pallas_call(
        functools.partial(middle_kernel, inner=inner, inner_all=inner_all, width=width),
        out_shape=[
            shape((rows, inner), BF16),
            *[shape((rows, part), BF16)] * 4,
            shape((inner, rows)),
            shape((1, rows)),
            shape((inner, HALF)),
        ],
        grid_spec=pltpu.PrefetchScalarGridSpec(
            num_scalar_prefetch=1,
            grid=(rows // SEQ_LEN, blocks),
            in_specs=[*[piece] * 4, fixed(wo), fixed(chan), col(inner), col(1)],
            out_specs=[
                pl.BlockSpec((Q, inner), lambda q, c, lens: (at(q, c), 0)),
                *[piece] * 4,
                col(inner),
                col(1),
                pl.BlockSpec((inner, HALF), lambda q, c, lens: (0, 0)),
            ],
            scratch_shapes=[pltpu.VMEM((inner, Q), BF16)],
        ),
        compiler_params=params(2),
        name="mixer_middle",
    )(lengths, *cots, wo, chan, m, squares)


def run_backward(seq, lengths, xs, wt, chan, bcc, headc, saved, squares, stat, inner_all):
    part = xs[0].shape[1]
    width = 4 * part
    inner, heads, states2 = chan.shape[1], headc.shape[1], bcc.shape[1]
    blocks = SEQ_LEN // Q
    back = lambda c: blocks - 1 - c
    at = lambda c: seq * blocks + back(c)
    col = lambda n: pl.BlockSpec((n, Q), lambda c, lens: (0, at(c)))
    piece = pl.BlockSpec((Q, part), lambda c, lens: (back(c), 0))
    consts = (wt, chan, bcc, headc)
    accs = [(6, inner, HALF), (5, states2, HALF), (2, heads, HALF), (8, width)]
    keep = lambda dims: pl.BlockSpec(dims, lambda c, lens: (0,) * len(dims))
    return pl.pallas_call(
        functools.partial(
            backward_kernel,
            seq=seq,
            inner=inner,
            inner_all=inner_all,
            heads=heads,
            width=width,
            blocks=blocks,
        ),
        out_shape=[
            shape((SEQ_LEN, wt.shape[0]), BF16),
            *[shape((SEQ_LEN, part), BF16)] * 4,
            *[shape(dims) for dims in accs],
        ],
        grid_spec=pltpu.PrefetchScalarGridSpec(
            num_scalar_prefetch=1,
            grid=(blocks,),
            in_specs=[
                *[piece] * 4,
                *[fixed(array) for array in consts],
                *[col(inner)] * 5,
                *[col(states2)] * 2,
                *[col(heads)] * 2,
                pl.BlockSpec((inner, states2 // 2), lambda c, lens: (at(c), 0)),
                *[col(1)] * 2,
            ],
            out_specs=[
                pl.BlockSpec((Q, wt.shape[0]), lambda c, lens: (back(c), 0)),
                *[piece] * 4,
                *[keep(dims) for dims in accs],
            ],
            scratch_shapes=[
                pltpu.VMEM((wt.shape[0], Q), BF16),
                pltpu.VMEM((inner, states2 // 2), F32),
                pltpu.VMEM((inner, HALF), F32),
                pltpu.VMEM((states2, HALF), F32),
                pltpu.VMEM((3, HALF, HALF), F32),
                pltpu.VMEM((inner, Q), BF16),
                pltpu.VMEM((inner, Q), BF16),
            ],
        ),
        compiler_params=params(1),
        name="mixer_backward",
    )(lengths, *xs, *consts, *saved, squares, stat)


def exchange(a, axis, bit):
    return lax.ppermute(a, axis, [(i, i ^ bit) for i in range(lax.axis_size(axis))])


def exchange_sum(a, axis):
    bit = 1
    while bit < lax.axis_size(axis):
        a = a + exchange(a, axis, bit)
        bit *= 2
    return a


def gather_pieces(a):
    across = exchange(a, "tensor", 2)
    return a, exchange(a, "tensor", 1), across, exchange(across, "tensor", 1)


def reduce_pieces(pieces, kind=BF16):
    own, beside, across, corner = pieces
    send = jnp.concatenate([beside, corner], 0).astype(kind)
    got = exchange(send, "tensor", 1).astype(F32)
    count = own.shape[0]
    onward = (across.astype(F32) + got[count:]).astype(kind)
    return own.astype(F32) + got[:count] + exchange(onward, "tensor", 2).astype(F32)


def line_shift(a, up, senders):
    move = 2 if up else -2
    return lax.ppermute(a, "dp", [(2 * z + x, 2 * z + x + move) for z in senders for x in (0, 1)])


def place():
    index = lax.axis_index("dp")
    return index // 2, index % 2


def line_gather(a):
    z, _ = place()
    ups, downs = [a], [a]
    for k in range(1, 4):
        ups.append(line_shift(ups[-1], True, range(k - 1, 3)))
        downs.append(line_shift(downs[-1], False, range(1, 5 - k)))
    blocks = [jnp.where(z + r < 4, downs[r], ups[4 - r]) for r in range(1, 4)]
    return jnp.stack([a] + blocks)


def line_reduce(pick):
    z, _ = place()
    total = pick(z)
    for up in (True, False):
        got = None
        for k in range(1, 4):
            send = pick((z + 4 - k) % 4 if up else (z + k) % 4)
            if got is not None:
                send = send + got
            senders = range(0, k) if up else range(4 - k, 4)
            got = line_shift(send.astype(BF16), up, senders).astype(F32)
        total = total + got
    return total


def round_to(count, tile):
    return count // tile * tile


def weight_columns(a):
    tensor = lax.axis_index("tensor")
    cols, part = a.shape
    count = lax.axis_size("dp")
    if count != 8:
        whole = jnp.transpose(lax.all_gather(jnp.transpose(a), "dp", axis=0, tiled=True))
        blocks = whole.reshape(cols, 4, -1)
        return jnp.concatenate(
            [lax.dynamic_index_in_dim(blocks, tensor ^ m, 1, keepdims=False) for m in range(4)], 1
        )
    z, x = place()
    cut = round_to(cols * 2 // 3, 16)
    first, second = a[:cut], a[cut:]
    pair = jnp.stack([second, exchange(second, "dp", 1)])
    beside = exchange(first, "dp", 1)
    mine = line_gather(first)
    other = jnp.concatenate([beside[None], exchange(mine[1:], "dp", 1)], 0)
    both = line_gather(pair)
    out = []
    for m in range(4):
        r = ((tensor ^ m) - z) % 4
        top = [lax.dynamic_index_in_dim(b, r, 0, keepdims=False) for b in (mine, other)]
        low = lax.dynamic_index_in_dim(both, r, 0, keepdims=False)
        for side in (0, 1):
            own = x == side
            out.append(
                jnp.concatenate(
                    [jnp.where(own, top[0], top[1]), jnp.where(own, low[0], low[1])], 0
                )
            )
    return jnp.concatenate(out, 1)


def weight_rows(a):
    tensor = lax.axis_index("tensor")
    width, cols = a.shape
    count = lax.axis_size("dp")
    if count != 8:
        blocks = a.reshape(4, -1, cols)
        ordered = jnp.concatenate(
            [lax.dynamic_index_in_dim(blocks, tensor ^ m, 0, keepdims=False) for m in range(4)], 0
        )
        return lax.psum_scatter(ordered, "dp", scatter_dimension=0, tiled=True)
    _, x = place()
    blocks = a.reshape(4, 2, width // 8, cols)
    cut = round_to(cols * 5 // 8, HALF)
    first, second = blocks[..., :cut], blocks[..., cut:]
    take = lambda b, i, dim: lax.dynamic_index_in_dim(b, i, dim, keepdims=False)
    got = exchange(take(first, 1 - x, 1).astype(BF16), "dp", 1).astype(F32)
    halves = take(first, x, 1) + got
    pairs = line_reduce(lambda z: take(second, z ^ tensor, 0))
    late = exchange(take(pairs, 1 - x, 0).astype(BF16), "dp", 1).astype(F32)
    early = line_reduce(lambda z: take(halves, z ^ tensor, 0))
    return jnp.concatenate([early, take(pairs, x, 0) + late], 1)


def over_rows(left, right):
    return lax.dot_general(
        left, right, (((0,), (0,)), ((), ())), preferred_element_type=F32
    )


def lanes(a):
    return jnp.broadcast_to(a[..., None], a.shape + (HALF,))


def small_constants(conv_x, conv_bc, dt_bias, a_log, skip_d, gate_gain):
    per = conv_x.shape[1] // skip_d.shape[0]
    chan = lanes(jnp.concatenate([conv_x, gate_gain[None], jnp.repeat(skip_d, per)[None]], 0))
    return chan, lanes(conv_bc), lanes(jnp.stack([dt_bias, -jnp.exp(a_log)], 0))


def per_device(
    tokens,
    lengths,
    grad_out,
    norm_gain,
    w_gate,
    w_value,
    w_bc,
    w_dt,
    conv_x,
    conv_bc,
    dt_bias,
    a_log,
    skip_d,
    gate_gain,
    w_out,
):
    tensor_count = lax.axis_size("tensor")
    tensor = lax.axis_index("tensor")
    rows, part = tokens.shape
    seqs = rows // SEQ_LEN
    inner = w_gate.shape[1]
    inner_all = inner * tensor_count
    heads = w_dt.shape[1]
    states2 = w_bc.shape[1]
    base = 2 * inner + states2

    local = jnp.concatenate(
        [
            w_gate,
            w_value,
            w_bc,
            w_dt,
            norm_gain[:, None],
            jnp.zeros((w_gate.shape[0], 15 - heads), BF16),
        ],
        1,
    )
    xs = [gather_pieces(tokens[q * SEQ_LEN : (q + 1) * SEQ_LEN]) for q in range(seqs)]
    cots = gather_pieces(grad_out)
    wt = jnp.pad(weight_columns(jnp.transpose(local)), ((0, HALF - 16), (0, 0)))
    wo = weight_columns(jnp.transpose(w_out))
    chan, bcc, headc = small_constants(conv_x, conv_bc, dt_bias, a_log, skip_d, gate_gain)

    saved, squares = [], []
    for q in range(seqs):
        *saved, here = run_forward(q, seqs, lengths, xs[q], wt, chan, bcc, headc, saved)
        squares.append(exchange_sum(here, "tensor"))
    squares = jnp.concatenate(squares, 1)
    normed, gate, val, z, y, m, *shared = saved
    nout, *branch, gno, stat, gain_acc = run_middle(
        lengths, cots, wo, chan, m, squares, inner_all
    )
    stat = exchange_sum(stat, "tensor")
    g_out = jnp.concatenate([over_rows(cot, nout) for cot in cots], 0)
    out_rows = (tokens.astype(F32) + reduce_pieces(branch)).astype(BF16)
    grad_out_rows = weight_rows(g_out)

    grad_rows, accs, g_all = [], None, None
    kept = (gate, val, z, y, gno, *shared)
    for q in range(seqs):
        lows, *rest = run_backward(
            q, lengths, xs[q], wt, chan, bcc, headc, kept, squares, stat, inner_all
        )
        gin, here = rest[:4], rest[4:]
        accs = here if accs is None else [a + b for a, b in zip(accs, here)]
        grad_rows.append(reduce_pieces(gin))
        here = over_rows(normed[q * SEQ_LEN : (q + 1) * SEQ_LEN], lows)
        g_all = here if g_all is None else g_all + here
    valid = (jnp.arange(SEQ_LEN)[None] < lengths[:, None]).reshape(rows)[:, None]
    grad_rows = jnp.concatenate(grad_rows, 0) + jnp.where(valid, grad_out.astype(F32), 0.0)

    chan_acc, bc_acc, head_acc, norm_acc = accs
    column = jnp.arange(g_all.shape[1]) == base + heads
    g_all = jnp.where(column[None], jnp.sum(norm_acc, 0)[:, None], g_all)
    grads = weight_rows(g_all)
    rest = grads[:, 2 * inner :].reshape(tensor_count, -1, states2 + HALF)
    rest = reduce_pieces(
        [lax.dynamic_index_in_dim(rest, tensor ^ i, 0, keepdims=False) for i in range(4)], F32
    )
    sizes = [5 * inner, inner, inner, 2 * heads, 5 * states2]
    flat = jnp.concatenate(
        [
            jnp.sum(chan_acc, -1).reshape(-1),
            jnp.sum(gain_acc, -1),
            jnp.sum(head_acc, -1).reshape(-1),
            jnp.sum(bc_acc, -1).reshape(-1),
        ]
    )
    flat = exchange_sum(flat, "dp")
    cuts = [sum(sizes[: i + 1]) for i in range(4)]
    g_conv, g_skip, g_gain, g_head, g_conv_bc = jnp.split(flat, cuts)
    g_conv_bc = exchange_sum(g_conv_bc, "tensor")
    return (
        out_rows,
        grad_rows,
        rest[:, states2 + heads],
        grads[:, :inner],
        grads[:, inner : 2 * inner],
        rest[:, :states2],
        grads[:, base : base + heads],
        g_conv.reshape(5, inner),
        g_conv_bc.reshape(5, states2),
        g_head[:heads],
        g_head[heads:] * -jnp.exp(a_log),
        jnp.sum(g_skip.reshape(heads, -1), -1),
        g_gain,
        grad_out_rows,
    )


def solution(mesh):
    both = ("dp", "tensor")
    return jax.shard_map(
        per_device,
        mesh=mesh,
        in_specs=(
            P("dp", "tensor"),
            P("dp"),
            P("dp", "tensor"),
            P("dp"),
            P("dp", "tensor"),
            P("dp", "tensor"),
            P("dp", None),
            P("dp", "tensor"),
            P(None, "tensor"),
            P(),
            P("tensor"),
            P("tensor"),
            P("tensor"),
            P("tensor"),
            P("dp", "tensor"),
        ),
        out_specs=(
            P("dp", "tensor"),
            P("dp", "tensor"),
            P(both),
            P("dp", "tensor"),
            P("dp", "tensor"),
            P(both, None),
            P("dp", "tensor"),
            P(None, "tensor"),
            P(),
            P("tensor"),
            P("tensor"),
            P("tensor"),
            P("tensor"),
            P("dp", "tensor"),
        ),
        check_vma=False,
    )
```

```python
import functools

import jax
import jax.numpy as jnp
from jax import lax
from jax.experimental import pallas as pl
from jax.experimental.pallas import tpu as pltpu
from jax.sharding import PartitionSpec as P


SEQ_LEN = 2048
Q = 256
HALF = 128
F32 = jnp.float32
BF16 = jnp.bfloat16
epsilon = 1e-05
NEG = -1e30


def nn(a, b):
    return lax.dot_general(a, b, (((1,), (0,)), ((), ())), preferred_element_type=F32)


def nt(a, b):
    return lax.dot_general(a, b, (((1,), (1,)), ((), ())), preferred_element_type=F32)


def split3(a):
    high = a.astype(BF16)
    rest = a - high.astype(F32)
    mid = rest.astype(BF16)
    low = (rest - mid.astype(F32)).astype(BF16)
    return high, mid, low


def times_ones(a, ones):
    rows = a.shape[0]
    got = nn(jnp.concatenate(split3(a), 0), ones)
    return got[:rows] + got[rows : 2 * rows] + got[2 * rows :]


def twice(a):
    return jnp.concatenate([a, a], 1)


def fold(a):
    return a[:, :HALF] + a[:, HALF:]


def triangle(keep):
    row = lax.broadcasted_iota(jnp.int32, (Q, Q), 0)
    col = lax.broadcasted_iota(jnp.int32, (Q, Q), 1)
    return jnp.where(keep(row, col), 1.0, 0.0).astype(BF16)


def conv(raw, tail, taps):
    ext = jnp.concatenate([tail, raw], 1)
    total = twice(taps[4]) + twice(taps[3]) * raw
    for k in range(1, 4):
        total = total + twice(taps[3 - k]) * pltpu.roll(ext, k, 1)[:, HALF:]
    return total


def conv_back(grad, head, taps):
    ext = jnp.concatenate([grad, head], 1)
    shifted = [grad] + [pltpu.roll(ext, 3 * HALF - k, 1)[:, :Q] for k in range(1, 4)]
    total = twice(taps[3]) * grad
    for k in range(1, 4):
        total = total + twice(taps[3 - k]) * shifted[k]
    return total, shifted


def decay_blocks(run_row, run_col, upper):
    early, late = run_row[:, :HALF], run_row[:, HALF:]
    col_early = jnp.broadcast_to(run_col[:HALF], (HALF, HALF))
    col_late = jnp.broadcast_to(run_col[HALF:], (HALF, HALF))
    first = jnp.exp(jnp.where(upper, early - col_early, NEG))
    cross = jnp.exp(late - col_early)
    second = jnp.exp(jnp.where(upper, late - col_late, NEG))
    return first, cross, second


def stack_blocks(first, cross, second):
    zero = jnp.zeros((HALF, HALF), first.dtype)
    return jnp.concatenate(
        [jnp.concatenate([first, cross], 1), jnp.concatenate([zero, second], 1)], 0
    )


def intersection(b_rows, c_rows):
    b_time = jnp.transpose(b_rows)
    b_high = b_time.astype(BF16)
    b_low = (b_time - b_high.astype(F32)).astype(BF16)
    c_high = c_rows.astype(BF16)
    c_low = (c_rows - c_high.astype(F32)).astype(BF16)
    return nn(
        jnp.concatenate([b_high, b_low, b_high], 1), jnp.concatenate([c_high, c_high, c_low], 0)
    )


def rms_scale(xs, width):
    total = xs[0] * xs[0]
    for x in xs[1:]:
        total = total + x * x
    return lax.rsqrt(jnp.sum(total, -1, keepdims=True) / width + epsilon)


def gain_row(wt_ref, base, heads):
    return wt_ref[base : base + 16, :].astype(F32)[heads : heads + 1]


def softplus(a):
    return jnp.maximum(a, 0.0) + jnp.log1p(jnp.exp(-jnp.abs(a)))


def upper_half():
    row = lax.broadcasted_iota(jnp.int32, (HALF, HALF), 0)
    return row <= lax.broadcasted_iota(jnp.int32, (HALF, HALF), 1)


def valid_row(block, length):
    pos = block * Q + lax.broadcasted_iota(jnp.int32, (1, Q), 1)
    return jnp.where(pos < length, 1.0, 0.0)


def forward_kernel(len_ref, *refs, seq, inner, heads, width, aliased):
    x_refs, (wt_ref, chan_ref, bcc_ref, headc_ref) = refs[:4], refs[4:8]
    refs = refs[8 + aliased :]
    (norm_ref, gate_ref, val_ref, z_ref, y_ref, m_ref, bc_ref, bcz_ref) = refs[:8]
    (step_ref, run_ref, state_ref, stat_ref, proj, vtail, btail, state) = refs[8:]
    block = pl.program_id(0)
    length = len_ref[seq]
    per = inner // heads
    part = width // 4
    states = bc_ref.shape[0] // 2

    @pl.when(block == 0)
    def _():
        vtail[...] = jnp.zeros_like(vtail)
        btail[...] = jnp.zeros_like(btail)
        state[...] = jnp.zeros_like(state)

    @pl.when(block * Q >= length)
    def _():
        norm_ref[...] = jnp.zeros_like(norm_ref)
        stat_ref[...] = jnp.zeros_like(stat_ref)

    @pl.when(block * Q < length)
    def _():
        base = 2 * inner + 2 * states
        gain = gain_row(wt_ref, base, heads)
        xs = [ref[...].astype(F32) for ref in x_refs]
        inv = rms_scale(xs, width)
        for k in range(4):
            cols = slice(k * part, (k + 1) * part)
            norm_ref[:, cols] = (xs[k] * inv * gain[:, cols]).astype(BF16)
        proj[...] = nt(wt_ref[: base + 16, :], norm_ref[...])

        raw = proj[2 * inner : base, :]
        bc_ref[...] = raw
        bcz = conv(raw, btail[...], [bcc_ref[j] for j in range(5)])
        btail[...] = raw[:, HALF:]
        bcz_ref[...] = bcz
        shared = bcz * jax.nn.sigmoid(bcz)
        b_rows, c_rows = shared[:states], shared[states:]
        cb = intersection(b_rows, c_rows)
        cb_blocks = (cb[:HALF, :HALF], cb[:HALF, HALF:], cb[HALF:, HALF:])
        b_low, c_low = b_rows.astype(BF16), c_rows.astype(BF16)

        step_raw = proj[base : base + heads, :] + twice(headc_ref[0])
        step_ref[...] = step_raw
        steps = softplus(step_raw)
        running = times_ones(steps * twice(headc_ref[1]), triangle(lambda s, t: s <= t))
        run_ref[...] = running
        run_cols = jnp.transpose(running)
        ends = running[:, Q - 1 :]
        grow = jnp.exp(running)
        to_end = jnp.exp(ends - running)
        whole = jnp.exp(ends)
        upper = upper_half()

        state_ref[...] = state[...]
        squares = jnp.zeros((1, Q), F32)
        for h in range(heads):
            rows = slice(h * per, (h + 1) * per)
            raw_v = proj[inner + h * per : inner + (h + 1) * per, :]
            gate = proj[rows, :]
            val_ref[rows, :] = raw_v
            gate_ref[rows, :] = gate
            z = conv(raw_v, vtail[rows, :], [chan_ref[j, rows, :] for j in range(5)])
            vtail[rows, :] = raw_v[:, HALF:]
            z_ref[rows, :] = z
            v = z * jax.nn.sigmoid(z)
            w = v * steps[h : h + 1]
            decays = decay_blocks(running[h : h + 1], run_cols[:, h : h + 1], upper)
            grid = stack_blocks(*[(d * g).astype(BF16) for d, g in zip(decays, cb_blocks)])
            old = state[rows, :]
            y = nn(w.astype(BF16), grid) + nn(old.astype(BF16), c_low) * grow[h : h + 1]
            y_ref[rows, :] = y
            fresh = nt((w * to_end[h : h + 1]).astype(BF16), b_low)
            state[rows, :] = old * whole[h : h + 1] + fresh
            u = y + twice(chan_ref[6, rows, :]) * v
            m = u * gate * jax.nn.sigmoid(gate)
            m_ref[rows, :] = m
            squares = squares + jnp.sum(m * m, 0, keepdims=True)
        stat_ref[...] = squares


def middle_kernel(
    len_ref, c0, c1, c2, c3, wo_ref, chan_ref, m_ref, sq_ref,
    nout_ref, b0, b1, b2, b3, gno_ref, stat_ref, gain_acc, nout, *, inner, inner_all, width,
):
    seq, block = pl.program_id(0), pl.program_id(1)
    length = len_ref[seq]
    part = width // 4

    @pl.when((seq == 0) & (block == 0))
    def _():
        gain_acc[...] = jnp.zeros_like(gain_acc)

    @pl.when(block * Q >= length)
    def _():
        nout_ref[...] = jnp.zeros_like(nout_ref)
        stat_ref[...] = jnp.zeros_like(stat_ref)
        for ref in (b0, b1, b2, b3):
            ref[...] = jnp.zeros_like(ref)

    @pl.when(block * Q < length)
    def _():
        valid = valid_row(block, length)
        scale = lax.rsqrt(sq_ref[...] / inner_all + epsilon) * valid
        cot = jnp.concatenate([ref[...] for ref in (c0, c1, c2, c3)], 1)
        gno_ref[...] = nt(wo_ref[...], cot) * valid
        inners = jnp.zeros((1, Q), F32)
        for lo in range(0, inner, 64):
            rows = slice(lo, lo + 64)
            gain = twice(chan_ref[5, rows, :])
            m = m_ref[rows, :]
            gno = gno_ref[rows, :]
            nout[rows, :] = (m * scale * gain).astype(BF16)
            inners = inners + jnp.sum(gno * gain * m, 0, keepdims=True)
            gain_acc[rows, :] += fold(gno * m * scale)
        stat_ref[...] = inners
        nout_time = jnp.transpose(nout[...])
        nout_ref[...] = nout_time
        branch = nn(nout_time, wo_ref[...])
        for k, ref in enumerate((b0, b1, b2, b3)):
            ref[...] = branch[:, k * part : (k + 1) * part].astype(BF16)


def backward_kernel(len_ref, *refs, seq, inner, inner_all, heads, width, blocks):
    x_refs, (wt_ref, chan_ref, bcc_ref, headc_ref) = refs[:4], refs[4:8]
    (gate_ref, val_ref, z_ref, y_ref, gno_ref, bc_ref, bcz_ref) = refs[8:15]
    (step_ref, run_ref, state_ref, sq_ref, stat_ref) = refs[15:20]
    low_ref, g_refs, (chan_acc, bc_acc, head_acc, norm_acc) = refs[20], refs[21:25], refs[25:29]
    low, gstate, vhead, bhead, dcb, wdec, gudec = refs[29:]
    step = pl.program_id(0)
    block = blocks - 1 - step
    length = len_ref[seq]
    per = inner // heads
    part = width // 4
    states = bc_ref.shape[0] // 2
    base = 2 * inner + 2 * states

    @pl.when(step == 0)
    def _():
        chan_acc[...] = jnp.zeros_like(chan_acc)
        bc_acc[...] = jnp.zeros_like(bc_acc)
        head_acc[...] = jnp.zeros_like(head_acc)
        norm_acc[...] = jnp.zeros_like(norm_acc)
        low[base:, :] = jnp.zeros_like(low[base:, :])
        gstate[...] = jnp.zeros_like(gstate)
        vhead[...] = jnp.zeros_like(vhead)
        bhead[...] = jnp.zeros_like(bhead)

    @pl.when(block * Q >= length)
    def _():
        low_ref[...] = jnp.zeros_like(low_ref)
        for ref in g_refs:
            ref[...] = jnp.zeros_like(ref)

    @pl.when(block * Q < length)
    def _():
        inv_gate = lax.rsqrt(sq_ref[...] / inner_all + epsilon)
        pull = inv_gate * inv_gate * inv_gate * stat_ref[...] / inner_all

        bcz = bcz_ref[...]
        sig = jax.nn.sigmoid(bcz)
        shared = bcz * sig
        shared_slope = sig * (1.0 + bcz * (1.0 - sig))
        b_rows, c_rows = shared[:states], shared[states:]
        cb = intersection(b_rows, c_rows)
        cb_blocks = (cb[:HALF, :HALF], cb[:HALF, HALF:], cb[HALF:, HALF:])
        b_low, c_low = b_rows.astype(BF16), c_rows.astype(BF16)

        step_raw = step_ref[...]
        steps = softplus(step_raw)
        running = run_ref[...]
        run_cols = jnp.transpose(running)
        ends = running[:, Q - 1 :]
        grow = jnp.exp(running)
        to_end = jnp.exp(ends - running)
        whole = jnp.exp(ends)
        upper = upper_half()

        direct, both, after, through = [], [], [], []
        for h in range(heads):
            rows = slice(h * per, (h + 1) * per)
            gate, z, y, gno = gate_ref[rows, :], z_ref[rows, :], y_ref[rows, :], gno_ref[rows, :]
            gain = twice(chan_ref[5, rows, :])
            skip = twice(chan_ref[6, rows, :])
            sig_g = jax.nn.sigmoid(gate)
            silu_g = gate * sig_g
            sig_z = jax.nn.sigmoid(z)
            v = z * sig_z
            u = y + skip * v
            m = u * silu_g
            gm = inv_gate * gain * gno - m * pull
            low[rows, :] = (gm * u * (sig_g * (1.0 + gate * (1.0 - sig_g)))).astype(BF16)
            gu = gm * silu_g
            chan_acc[5, rows, :] += fold(gu * v)
            w = v * steps[h : h + 1]
            w_low, gu_low = w.astype(BF16), gu.astype(BF16)
            decays = decay_blocks(running[h : h + 1], run_cols[:, h : h + 1], upper)
            grid = stack_blocks(*[(d * g).astype(BF16) for d, g in zip(decays, cb_blocks)])
            gw_in = nt(gu_low, grid)
            pair = nn(jnp.transpose(w_low), gu_low)
            pieces = (pair[:HALF, :HALF], pair[:HALF, HALF:], pair[HALF:, HALF:])
            for i in range(3):
                if h == 0:
                    dcb[i] = decays[i] * pieces[i]
                else:
                    dcb[i] += decays[i] * pieces[i]
            gs = gstate[rows, :]
            gs_low = gs.astype(BF16)
            gw_out = nn(gs_low, b_low) * to_end[h : h + 1]
            gw = gw_in + gw_out
            direct.append(jnp.sum(gw * v, 0, keepdims=True))
            both.append(
                jnp.sum(gu_low.astype(F32) * y - gw_in * w_low.astype(F32), 0, keepdims=True)
            )
            after.append(jnp.sum(gw_out * w, 0, keepdims=True))
            through.append(
                jnp.sum(gs * state_ref[rows, :], 0, keepdims=True) * whole[h : h + 1]
            )
            gud = (gu * grow[h : h + 1]).astype(BF16)
            gudec[rows, :] = gud
            wdec[rows, :] = (w * to_end[h : h + 1]).astype(BF16)
            gz = (skip * gu + gw * steps[h : h + 1]) * (sig_z * (1.0 + z * (1.0 - sig_z)))
            taps = [chan_ref[j, rows, :] for j in range(4)]
            gv, shifted = conv_back(gz, vhead[rows, :], taps)
            vhead[rows, :] = gz[:, :HALF]
            raw_v = val_ref[rows, :]
            for k in range(4):
                chan_acc[3 - k, rows, :] += fold(shifted[k] * raw_v)
            chan_acc[4, rows, :] += fold(gz)
            low[inner + h * per : inner + (h + 1) * per, :] = gv.astype(BF16)

        direct = jnp.concatenate(direct, 0)
        both = jnp.concatenate(both, 0)
        after = jnp.concatenate(after, 0)
        through = jnp.sum(jnp.concatenate(through, 0), -1, keepdims=True)
        g_decay = (
            times_ones(both, triangle(lambda t, r: t >= r))
            + times_ones(after, triangle(lambda s, r: s < r))
            + through
        )
        head_acc[1] += fold(steps * g_decay)
        g_step = (direct + twice(headc_ref[1]) * g_decay) * jax.nn.sigmoid(step_raw)
        head_acc[0] += fold(g_step)
        low[base : base + 16, :] = jnp.concatenate(
            [g_step, jnp.zeros((16 - heads, Q), F32)], 0
        ).astype(BF16)

        dcb_low = stack_blocks(*[dcb[i].astype(BF16) for i in range(3)])
        gud, wd = gudec[...], wdec[...]
        gs_old = gstate[...]
        g_c = nn(b_low, dcb_low) + nn(jnp.transpose(state_ref[...]).astype(BF16), gud)
        g_b = nt(c_low, dcb_low) + nn(jnp.transpose(gs_old).astype(BF16), wd)
        fresh = nt(gud, c_low)
        for h in range(heads):
            rows = slice(h * per, (h + 1) * per)
            gstate[rows, :] = gs_old[rows] * whole[h : h + 1] + fresh[rows]
        gbcz = jnp.concatenate([g_b, g_c], 0) * shared_slope
        gbc, shifted = conv_back(gbcz, bhead[...], [bcc_ref[j] for j in range(4)])
        bhead[...] = gbcz[:, :HALF]
        raw = bc_ref[...]
        for k in range(4):
            bc_acc[3 - k] += fold(shifted[k] * raw)
        bc_acc[4] += fold(gbcz)
        low[2 * inner : base, :] = gbc.astype(BF16)

        lows = jnp.transpose(low[...])
        low_ref[...] = lows
        g_norm = nn(lows, wt_ref[...])
        gain = gain_row(wt_ref, base, heads)
        xs = [ref[...].astype(F32) for ref in x_refs]
        inv = rms_scale(xs, width)
        prod = None
        for k in range(4):
            cols = slice(k * part, (k + 1) * part)
            here = g_norm[:, cols] * xs[k]
            norm_acc[:, cols] += jnp.sum((here * inv).reshape(Q // 8, 8, part), 0)
            weighted = here * gain[:, cols]
            prod = weighted if prod is None else prod + weighted
        pull_x = inv * inv * inv * (jnp.sum(prod, -1, keepdims=True) / width)
        for k in range(4):
            cols = slice(k * part, (k + 1) * part)
            g_refs[k][...] = (inv * gain[:, cols] * g_norm[:, cols] - xs[k] * pull_x).astype(BF16)


def shape(dims, kind=F32):
    return jax.ShapeDtypeStruct(dims, kind)


def params(count):
    return pltpu.CompilerParams(
        dimension_semantics=("arbitrary",) * count, vmem_limit_bytes=60 << 20
    )


def fixed(array):
    rank = array.ndim
    return pl.BlockSpec(array.shape, lambda *_: (0,) * rank, pipeline_mode=pl.Buffered(1))


def run_forward(seq, seqs, lengths, xs, wt, chan, bcc, headc, before):
    part = xs[0].shape[1]
    width = 4 * part
    inner, heads, states2 = chan.shape[1], headc.shape[1], bcc.shape[1]
    blocks = SEQ_LEN // Q
    rows = seqs * SEQ_LEN
    at = lambda c: seq * blocks + c
    col = lambda n: pl.BlockSpec((n, Q), lambda c, lens: (0, at(c)))
    out_shape = [
        shape((rows, width), BF16),
        *[shape((inner, rows))] * 5,
        *[shape((states2, rows))] * 2,
        *[shape((heads, rows))] * 2,
        shape((seqs * blocks * inner, states2 // 2)),
        shape((1, SEQ_LEN)),
    ]
    out_specs = [
        pl.BlockSpec((Q, width), lambda c, lens: (at(c), 0)),
        *[col(inner)] * 5,
        *[col(states2)] * 2,
        *[col(heads)] * 2,
        pl.BlockSpec((inner, states2 // 2), lambda c, lens: (at(c), 0)),
        pl.BlockSpec((1, Q), lambda c, lens: (0, c)),
    ]
    consts = (wt, chan, bcc, headc)
    return pl.pallas_call(
        functools.partial(
            forward_kernel,
            seq=seq,
            inner=inner,
            heads=heads,
            width=width,
            aliased=len(before),
        ),
        out_shape=out_shape,
        grid_spec=pltpu.PrefetchScalarGridSpec(
            num_scalar_prefetch=1,
            grid=(blocks,),
            in_specs=[
                *[pl.BlockSpec((Q, part), lambda c, lens: (c, 0))] * 4,
                *[fixed(array) for array in consts],
                *[pl.BlockSpec(memory_space=pl.ANY)] * len(before),
            ],
            out_specs=out_specs,
            scratch_shapes=[
                pltpu.VMEM((2 * inner + states2 + 16, Q), F32),
                pltpu.VMEM((inner, HALF), F32),
                pltpu.VMEM((states2, HALF), F32),
                pltpu.VMEM((inner, states2 // 2), F32),
            ],
        ),
        input_output_aliases={9 + i: i for i in range(len(before))},
        compiler_params=params(1),
        name="mixer_forward",
    )(lengths, *xs, *consts, *before)


def run_middle(lengths, cots, wo, chan, m, squares, inner_all):
    rows, part = cots[0].shape
    width = 4 * part
    inner = wo.shape[0]
    blocks = SEQ_LEN // Q
    at = lambda q, c: q * blocks + c
    piece = pl.BlockSpec((Q, part), lambda q, c, lens: (at(q, c), 0))
    col = lambda n: pl.BlockSpec((n, Q), lambda q, c, lens: (0, at(q, c)))
    return pl.pallas_call(
        functools.partial(middle_kernel, inner=inner, inner_all=inner_all, width=width),
        out_shape=[
            shape((rows, inner), BF16),
            *[shape((rows, part), BF16)] * 4,
            shape((inner, rows)),
            shape((1, rows)),
            shape((inner, HALF)),
        ],
        grid_spec=pltpu.PrefetchScalarGridSpec(
            num_scalar_prefetch=1,
            grid=(rows // SEQ_LEN, blocks),
            in_specs=[*[piece] * 4, fixed(wo), fixed(chan), col(inner), col(1)],
            out_specs=[
                pl.BlockSpec((Q, inner), lambda q, c, lens: (at(q, c), 0)),
                *[piece] * 4,
                col(inner),
                col(1),
                pl.BlockSpec((inner, HALF), lambda q, c, lens: (0, 0)),
            ],
            scratch_shapes=[pltpu.VMEM((inner, Q), BF16)],
        ),
        compiler_params=params(2),
        name="mixer_middle",
    )(lengths, *cots, wo, chan, m, squares)


def run_backward(seq, lengths, xs, wt, chan, bcc, headc, saved, squares, stat, inner_all):
    part = xs[0].shape[1]
    width = 4 * part
    inner, heads, states2 = chan.shape[1], headc.shape[1], bcc.shape[1]
    blocks = SEQ_LEN // Q
    back = lambda c: blocks - 1 - c
    at = lambda c: seq * blocks + back(c)
    col = lambda n: pl.BlockSpec((n, Q), lambda c, lens: (0, at(c)))
    piece = pl.BlockSpec((Q, part), lambda c, lens: (back(c), 0))
    consts = (wt, chan, bcc, headc)
    accs = [(6, inner, HALF), (5, states2, HALF), (2, heads, HALF), (8, width)]
    keep = lambda dims: pl.BlockSpec(dims, lambda c, lens: (0,) * len(dims))
    return pl.pallas_call(
        functools.partial(
            backward_kernel,
            seq=seq,
            inner=inner,
            inner_all=inner_all,
            heads=heads,
            width=width,
            blocks=blocks,
        ),
        out_shape=[
            shape((SEQ_LEN, wt.shape[0]), BF16),
            *[shape((SEQ_LEN, part), BF16)] * 4,
            *[shape(dims) for dims in accs],
        ],
        grid_spec=pltpu.PrefetchScalarGridSpec(
            num_scalar_prefetch=1,
            grid=(blocks,),
            in_specs=[
                *[piece] * 4,
                *[fixed(array) for array in consts],
                *[col(inner)] * 5,
                *[col(states2)] * 2,
                *[col(heads)] * 2,
                pl.BlockSpec((inner, states2 // 2), lambda c, lens: (at(c), 0)),
                *[col(1)] * 2,
            ],
            out_specs=[
                pl.BlockSpec((Q, wt.shape[0]), lambda c, lens: (back(c), 0)),
                *[piece] * 4,
                *[keep(dims) for dims in accs],
            ],
            scratch_shapes=[
                pltpu.VMEM((wt.shape[0], Q), BF16),
                pltpu.VMEM((inner, states2 // 2), F32),
                pltpu.VMEM((inner, HALF), F32),
                pltpu.VMEM((states2, HALF), F32),
                pltpu.VMEM((3, HALF, HALF), F32),
                pltpu.VMEM((inner, Q), BF16),
                pltpu.VMEM((inner, Q), BF16),
            ],
        ),
        compiler_params=params(1),
        name="mixer_backward",
    )(lengths, *xs, *consts, *saved, squares, stat)


def exchange(a, axis, bit):
    return lax.ppermute(a, axis, [(i, i ^ bit) for i in range(lax.axis_size(axis))])


def exchange_sum(a, axis):
    bit = 1
    while bit < lax.axis_size(axis):
        a = a + exchange(a, axis, bit)
        bit *= 2
    return a


def gather_pieces(a):
    across = exchange(a, "tensor", 2)
    beside = exchange(a, "tensor", 1)
    return a, beside, across, exchange(across, "tensor", 1)


def reduce_pieces(pieces, kind=BF16):
    own, beside, across, corner = pieces
    got_corner = exchange(corner.astype(kind), "tensor", 1)
    got_beside = exchange(beside.astype(kind), "tensor", 1)
    onward = (across.astype(F32) + got_corner.astype(F32)).astype(kind)
    here = own.astype(F32) + got_beside.astype(F32)
    return here + exchange(onward, "tensor", 2).astype(F32)


def place():
    index = lax.axis_index("dp")
    return index // 2, index % 2


def take(a, index, dim):
    return lax.dynamic_index_in_dim(a, index, dim, keepdims=False)


def round_to(count, tile):
    return count // tile * tile


def weight_columns(a):
    tensor = lax.axis_index("tensor")
    cols = a.shape[0]
    if lax.axis_size("dp") != 8:
        whole = jnp.transpose(lax.all_gather(jnp.transpose(a), "dp", axis=0, tiled=True))
        blocks = whole.reshape(cols, 4, -1)
        return jnp.concatenate([take(blocks, tensor ^ m, 1) for m in range(4)], 1)
    z, x = place()
    cut = round_to(cols * 7 // 10, 16)
    first, second = a[:cut], a[cut:]
    beside = exchange(second, "dp", 1)
    mine = [first] + [exchange(first, "dp", 2 * j) for j in (3, 2, 1)]
    other = [exchange(first, "dp", 1)]
    pair = jnp.stack([second, beside])
    both = jnp.stack([pair] + [exchange(pair, "dp", 2 * j) for j in (3, 2, 1)])
    mine = jnp.stack(mine)
    other = jnp.concatenate([other[0][None], exchange(mine[1:], "dp", 1)], 0)
    out = []
    for m in range(4):
        step = (tensor ^ m) ^ z
        slot = (4 - step) % 4
        top = [take(mine, slot, 0), take(other, slot, 0)]
        low = take(both, slot, 0)
        for side in (0, 1):
            own = x == side
            out.append(
                jnp.concatenate(
                    [jnp.where(own, top[0], top[1]), jnp.where(own, low[0], low[1])], 0
                )
            )
    return jnp.concatenate(out, 1)


def along_z(pick):
    z, _ = place()
    total = pick(z)
    for j in (3, 2, 1):
        total = total + exchange(pick(z ^ j).astype(BF16), "dp", 2 * j).astype(F32)
    return total


def weight_rows(a):
    tensor = lax.axis_index("tensor")
    width, cols = a.shape
    if lax.axis_size("dp") != 8:
        blocks = a.reshape(4, -1, cols)
        ordered = jnp.concatenate([take(blocks, tensor ^ m, 0) for m in range(4)], 0)
        return lax.psum_scatter(ordered, "dp", scatter_dimension=0, tiled=True)
    _, x = place()
    blocks = a.reshape(4, 2, width // 8, cols)
    cut = round_to(cols * 2 // 3, HALF)
    first, second = blocks[..., :cut], blocks[..., cut:]
    got = exchange(take(first, 1 - x, 1).astype(BF16), "dp", 1).astype(F32)
    pairs = along_z(lambda z: take(second, z ^ tensor, 0))
    halves = take(first, x, 1) + got
    early = along_z(lambda z: take(halves, z ^ tensor, 0))
    late = exchange(take(pairs, 1 - x, 0).astype(BF16), "dp", 1).astype(F32)
    return jnp.concatenate([early, take(pairs, x, 0) + late], 1)


def over_rows(left, right):
    return lax.dot_general(
        left, right, (((0,), (0,)), ((), ())), preferred_element_type=F32
    )


def lanes(a):
    return jnp.broadcast_to(a[..., None], a.shape + (HALF,))


def small_constants(conv_x, conv_bc, dt_bias, a_log, skip_d, gate_gain):
    per = conv_x.shape[1] // skip_d.shape[0]
    chan = lanes(jnp.concatenate([conv_x, gate_gain[None], jnp.repeat(skip_d, per)[None]], 0))
    return chan, lanes(conv_bc), lanes(jnp.stack([dt_bias, -jnp.exp(a_log)], 0))


def per_device(
    tokens,
    lengths,
    grad_out,
    norm_gain,
    w_gate,
    w_value,
    w_bc,
    w_dt,
    conv_x,
    conv_bc,
    dt_bias,
    a_log,
    skip_d,
    gate_gain,
    w_out,
):
    tensor_count = lax.axis_size("tensor")
    tensor = lax.axis_index("tensor")
    rows, _ = tokens.shape
    seqs = rows // SEQ_LEN
    inner = w_gate.shape[1]
    inner_all = inner * tensor_count
    heads = w_dt.shape[1]
    states2 = w_bc.shape[1]
    base = 2 * inner + states2

    local = jnp.concatenate(
        [
            w_gate,
            w_value,
            w_bc,
            w_dt,
            norm_gain[:, None],
            jnp.zeros((w_gate.shape[0], 15 - heads), BF16),
        ],
        1,
    )
    xs = [gather_pieces(tokens[q * SEQ_LEN : (q + 1) * SEQ_LEN]) for q in range(seqs)]
    cots = gather_pieces(grad_out)
    wt = jnp.pad(weight_columns(jnp.transpose(local)), ((0, HALF - 16), (0, 0)))
    w_out, wt = lax.optimization_barrier((w_out, wt))
    wo = weight_columns(jnp.transpose(w_out))
    chan, bcc, headc = small_constants(conv_x, conv_bc, dt_bias, a_log, skip_d, gate_gain)

    saved, squares = [], []
    for q in range(seqs):
        *saved, here = run_forward(q, seqs, lengths, xs[q], wt, chan, bcc, headc, saved)
        squares.append(exchange_sum(here, "tensor"))
    squares = jnp.concatenate(squares, 1)
    normed, gate, val, z, y, m, *shared = saved
    nout, *branch, gno, stat, gain_acc = run_middle(lengths, cots, wo, chan, m, squares, inner_all)
    stat = exchange_sum(stat, "tensor")
    g_out = jnp.concatenate([over_rows(cot, nout) for cot in cots], 0)
    branch = reduce_pieces(branch)
    out_rows = (tokens.astype(F32) + branch).astype(BF16)
    grad_out_rows = weight_rows(g_out)

    grad_rows, accs, g_all = [], None, None
    kept = (gate, val, z, y, gno, *shared)
    for q in range(seqs):
        lows, *rest = run_backward(
            q, lengths, xs[q], wt, chan, bcc, headc, kept, squares, stat, inner_all
        )
        gin, here = rest[:4], rest[4:]
        accs = here if accs is None else [a + b for a, b in zip(accs, here)]
        grad_rows.append(reduce_pieces(gin))
        here = over_rows(normed[q * SEQ_LEN : (q + 1) * SEQ_LEN], lows)
        g_all = here if g_all is None else g_all + here
    valid = (jnp.arange(SEQ_LEN)[None] < lengths[:, None]).reshape(rows)[:, None]
    grad_rows = jnp.concatenate(grad_rows, 0) + jnp.where(valid, grad_out.astype(F32), 0.0)

    chan_acc, bc_acc, head_acc, norm_acc = accs
    column = jnp.arange(g_all.shape[1]) == base + heads
    g_all = jnp.where(column[None], jnp.sum(norm_acc, 0)[:, None], g_all)
    grads = weight_rows(g_all)
    rest = grads[:, 2 * inner :].reshape(tensor_count, -1, states2 + HALF)
    rest = reduce_pieces(
        [lax.dynamic_index_in_dim(rest, tensor ^ i, 0, keepdims=False) for i in range(4)], F32
    )
    sizes = [5 * inner, inner, inner, 2 * heads, 5 * states2]
    flat = jnp.concatenate(
        [
            jnp.sum(chan_acc, -1).reshape(-1),
            jnp.sum(gain_acc, -1),
            jnp.sum(head_acc, -1).reshape(-1),
            jnp.sum(bc_acc, -1).reshape(-1),
        ]
    )
    flat = exchange_sum(flat, "dp")
    cuts = [sum(sizes[: i + 1]) for i in range(4)]
    g_conv, g_skip, g_gain, g_head, g_conv_bc = jnp.split(flat, cuts)
    g_conv_bc = exchange_sum(g_conv_bc, "tensor")
    return (
        out_rows,
        grad_rows,
        rest[:, states2 + heads],
        grads[:, :inner],
        grads[:, inner : 2 * inner],
        rest[:, :states2],
        grads[:, base : base + heads],
        g_conv.reshape(5, inner),
        g_conv_bc.reshape(5, states2),
        g_head[:heads],
        g_head[heads:] * -jnp.exp(a_log),
        jnp.sum(g_skip.reshape(heads, -1), -1),
        g_gain,
        grad_out_rows,
    )


def solution(mesh):
    return mapped(mesh)


def mapped(mesh):
    both = ("dp", "tensor")
    return jax.shard_map(
        per_device,
        mesh=mesh,
        in_specs=(
            P("dp", "tensor"),
            P("dp"),
            P("dp", "tensor"),
            P("dp"),
            P("dp", "tensor"),
            P("dp", "tensor"),
            P("dp", None),
            P("dp", "tensor"),
            P(None, "tensor"),
            P(),
            P("tensor"),
            P("tensor"),
            P("tensor"),
            P("tensor"),
            P("dp", "tensor"),
        ),
        out_specs=(
            P("dp", "tensor"),
            P("dp", "tensor"),
            P(both),
            P("dp", "tensor"),
            P("dp", "tensor"),
            P(both, None),
            P("dp", "tensor"),
            P(None, "tensor"),
            P(),
            P("tensor"),
            P("tensor"),
            P("tensor"),
            P("tensor"),
            P("dp", "tensor"),
        ),
        check_vma=False,
    )
```

```python
import functools

import jax
import jax.numpy as jnp
from jax import lax
from jax.experimental import pallas as pl
from jax.experimental.pallas import tpu as pltpu
from jax.sharding import PartitionSpec as P


SEQ_LEN = 2048
Q = 256
HALF = 128
F32 = jnp.float32
BF16 = jnp.bfloat16
epsilon = 1e-05
NEG = -1e30


def nn(a, b):
    return lax.dot_general(a, b, (((1,), (0,)), ((), ())), preferred_element_type=F32)


def nt(a, b):
    return lax.dot_general(a, b, (((1,), (1,)), ((), ())), preferred_element_type=F32)


def split3(a):
    high = a.astype(BF16)
    rest = a - high.astype(F32)
    mid = rest.astype(BF16)
    low = (rest - mid.astype(F32)).astype(BF16)
    return high, mid, low


def times_ones(a, ones):
    rows = a.shape[0]
    got = nn(jnp.concatenate(split3(a), 0), ones)
    return got[:rows] + got[rows : 2 * rows] + got[2 * rows :]


def twice(a):
    return jnp.concatenate([a, a], 1)


def fold(a):
    return a[:, :HALF] + a[:, HALF:]


def triangle(keep):
    row = lax.broadcasted_iota(jnp.int32, (Q, Q), 0)
    col = lax.broadcasted_iota(jnp.int32, (Q, Q), 1)
    return jnp.where(keep(row, col), 1.0, 0.0).astype(BF16)


def conv(raw, tail, taps):
    ext = jnp.concatenate([tail, raw], 1)
    total = twice(taps[4]) + twice(taps[3]) * raw
    for k in range(1, 4):
        total = total + twice(taps[3 - k]) * pltpu.roll(ext, k, 1)[:, HALF:]
    return total


def conv_back(grad, head, taps):
    ext = jnp.concatenate([grad, head], 1)
    shifted = [grad] + [pltpu.roll(ext, 3 * HALF - k, 1)[:, :Q] for k in range(1, 4)]
    total = twice(taps[3]) * grad
    for k in range(1, 4):
        total = total + twice(taps[3 - k]) * shifted[k]
    return total, shifted


def decay_blocks(run_row, run_col, upper):
    early, late = run_row[:, :HALF], run_row[:, HALF:]
    col_early = jnp.broadcast_to(run_col[:HALF], (HALF, HALF))
    col_late = jnp.broadcast_to(run_col[HALF:], (HALF, HALF))
    first = jnp.exp(jnp.where(upper, early - col_early, NEG))
    cross = jnp.exp(late - col_early)
    second = jnp.exp(jnp.where(upper, late - col_late, NEG))
    return first, cross, second


def stack_blocks(first, cross, second):
    zero = jnp.zeros((HALF, HALF), first.dtype)
    return jnp.concatenate(
        [jnp.concatenate([first, cross], 1), jnp.concatenate([zero, second], 1)], 0
    )


def intersection(b_rows, c_rows):
    b_time = jnp.transpose(b_rows)
    b_high = b_time.astype(BF16)
    b_low = (b_time - b_high.astype(F32)).astype(BF16)
    c_high = c_rows.astype(BF16)
    c_low = (c_rows - c_high.astype(F32)).astype(BF16)
    return nn(
        jnp.concatenate([b_high, b_low, b_high], 1), jnp.concatenate([c_high, c_high, c_low], 0)
    )


def rms_scale(xs, width):
    total = xs[0] * xs[0]
    for x in xs[1:]:
        total = total + x * x
    return lax.rsqrt(jnp.sum(total, -1, keepdims=True) / width + epsilon)


def gain_row(wt_ref, base, heads):
    return wt_ref[base : base + 16, :].astype(F32)[heads : heads + 1]


def softplus(a):
    return jnp.maximum(a, 0.0) + jnp.log1p(jnp.exp(-jnp.abs(a)))


def upper_half():
    row = lax.broadcasted_iota(jnp.int32, (HALF, HALF), 0)
    return row <= lax.broadcasted_iota(jnp.int32, (HALF, HALF), 1)


def valid_row(block, length):
    pos = block * Q + lax.broadcasted_iota(jnp.int32, (1, Q), 1)
    return jnp.where(pos < length, 1.0, 0.0)


def forward_kernel(len_ref, *refs, seq, inner, heads, width, aliased):
    x_refs, (wt_ref, chan_ref, bcc_ref, headc_ref) = refs[:4], refs[4:8]
    refs = refs[8 + aliased :]
    (norm_ref, gate_ref, val_ref, z_ref, y_ref, m_ref, bc_ref, bcz_ref) = refs[:8]
    (step_ref, run_ref, state_ref, stat_ref, proj, vtail, btail, state) = refs[8:]
    block = pl.program_id(0)
    length = len_ref[seq]
    per = inner // heads
    part = width // 4
    states = bc_ref.shape[0] // 2

    @pl.when(block == 0)
    def _():
        vtail[...] = jnp.zeros_like(vtail)
        btail[...] = jnp.zeros_like(btail)
        state[...] = jnp.zeros_like(state)

    @pl.when(block * Q >= length)
    def _():
        norm_ref[...] = jnp.zeros_like(norm_ref)
        stat_ref[...] = jnp.zeros_like(stat_ref)

    @pl.when(block * Q < length)
    def _():
        base = 2 * inner + 2 * states
        gain = gain_row(wt_ref, base, heads)
        xs = [ref[...].astype(F32) for ref in x_refs]
        inv = rms_scale(xs, width)
        for k in range(4):
            cols = slice(k * part, (k + 1) * part)
            norm_ref[:, cols] = (xs[k] * inv * gain[:, cols]).astype(BF16)
        proj[...] = nt(wt_ref[: base + 16, :], norm_ref[...])

        raw = proj[2 * inner : base, :]
        bc_ref[...] = raw
        bcz = conv(raw, btail[...], [bcc_ref[j] for j in range(5)])
        btail[...] = raw[:, HALF:]
        bcz_ref[...] = bcz
        shared = bcz * jax.nn.sigmoid(bcz)
        b_rows, c_rows = shared[:states], shared[states:]
        cb = intersection(b_rows, c_rows)
        cb_blocks = (cb[:HALF, :HALF], cb[:HALF, HALF:], cb[HALF:, HALF:])
        b_low, c_low = b_rows.astype(BF16), c_rows.astype(BF16)

        step_raw = proj[base : base + heads, :] + twice(headc_ref[0])
        step_ref[...] = step_raw
        steps = softplus(step_raw)
        running = times_ones(steps * twice(headc_ref[1]), triangle(lambda s, t: s <= t))
        run_ref[...] = running
        run_cols = jnp.transpose(running)
        ends = running[:, Q - 1 :]
        grow = jnp.exp(running)
        to_end = jnp.exp(ends - running)
        whole = jnp.exp(ends)
        upper = upper_half()

        state_ref[...] = state[...]
        squares = jnp.zeros((1, Q), F32)
        for h in range(heads):
            rows = slice(h * per, (h + 1) * per)
            raw_v = proj[inner + h * per : inner + (h + 1) * per, :]
            gate = proj[rows, :]
            val_ref[rows, :] = raw_v
            gate_ref[rows, :] = gate
            z = conv(raw_v, vtail[rows, :], [chan_ref[j, rows, :] for j in range(5)])
            vtail[rows, :] = raw_v[:, HALF:]
            z_ref[rows, :] = z
            v = z * jax.nn.sigmoid(z)
            w = v * steps[h : h + 1]
            decays = decay_blocks(running[h : h + 1], run_cols[:, h : h + 1], upper)
            grid = stack_blocks(*[(d * g).astype(BF16) for d, g in zip(decays, cb_blocks)])
            old = state[rows, :]
            y = nn(w.astype(BF16), grid) + nn(old.astype(BF16), c_low) * grow[h : h + 1]
            y_ref[rows, :] = y
            fresh = nt((w * to_end[h : h + 1]).astype(BF16), b_low)
            state[rows, :] = old * whole[h : h + 1] + fresh
            u = y + twice(chan_ref[6, rows, :]) * v
            m = u * gate * jax.nn.sigmoid(gate)
            m_ref[rows, :] = m
            squares = squares + jnp.sum(m * m, 0, keepdims=True)
        stat_ref[...] = squares


def middle_kernel(
    len_ref, c0, c1, c2, c3, wo_ref, chan_ref, m_ref, sq_ref,
    nout_ref, b0, b1, b2, b3, gno_ref, stat_ref, gain_acc, nout, *, inner, inner_all, width,
):
    seq, block = pl.program_id(0), pl.program_id(1)
    length = len_ref[seq]
    part = width // 4

    @pl.when((seq == 0) & (block == 0))
    def _():
        gain_acc[...] = jnp.zeros_like(gain_acc)

    @pl.when(block * Q >= length)
    def _():
        nout_ref[...] = jnp.zeros_like(nout_ref)
        stat_ref[...] = jnp.zeros_like(stat_ref)
        for ref in (b0, b1, b2, b3):
            ref[...] = jnp.zeros_like(ref)

    @pl.when(block * Q < length)
    def _():
        valid = valid_row(block, length)
        scale = lax.rsqrt(sq_ref[...] / inner_all + epsilon) * valid
        cot = jnp.concatenate([ref[...] for ref in (c0, c1, c2, c3)], 1)
        gno_ref[...] = nt(wo_ref[...], cot) * valid
        inners = jnp.zeros((1, Q), F32)
        for lo in range(0, inner, 64):
            rows = slice(lo, lo + 64)
            gain = twice(chan_ref[5, rows, :])
            m = m_ref[rows, :]
            gno = gno_ref[rows, :]
            nout[rows, :] = (m * scale * gain).astype(BF16)
            inners = inners + jnp.sum(gno * gain * m, 0, keepdims=True)
            gain_acc[rows, :] += fold(gno * m * scale)
        stat_ref[...] = inners
        nout_time = jnp.transpose(nout[...])
        nout_ref[...] = nout_time
        branch = nn(nout_time, wo_ref[...])
        for k, ref in enumerate((b0, b1, b2, b3)):
            ref[...] = branch[:, k * part : (k + 1) * part].astype(BF16)


def backward_kernel(len_ref, *refs, seq, inner, inner_all, heads, width, blocks):
    x_refs, (wt_ref, chan_ref, bcc_ref, headc_ref) = refs[:4], refs[4:8]
    (gate_ref, val_ref, z_ref, y_ref, gno_ref, bc_ref, bcz_ref) = refs[8:15]
    (step_ref, run_ref, state_ref, sq_ref, stat_ref) = refs[15:20]
    low_refs, g_refs, (chan_acc, bc_acc, head_acc, norm_acc) = refs[20:22], refs[22:26], refs[26:30]
    low, gstate, vhead, bhead, dcb, wdec, gudec = refs[30:]
    step = pl.program_id(0)
    block = blocks - 1 - step
    length = len_ref[seq]
    per = inner // heads
    part = width // 4
    states = bc_ref.shape[0] // 2
    base = 2 * inner + 2 * states

    @pl.when(step == 0)
    def _():
        chan_acc[...] = jnp.zeros_like(chan_acc)
        bc_acc[...] = jnp.zeros_like(bc_acc)
        head_acc[...] = jnp.zeros_like(head_acc)
        norm_acc[...] = jnp.zeros_like(norm_acc)
        low[base:, :] = jnp.zeros_like(low[base:, :])
        gstate[...] = jnp.zeros_like(gstate)
        vhead[...] = jnp.zeros_like(vhead)
        bhead[...] = jnp.zeros_like(bhead)

    @pl.when(block * Q >= length)
    def _():
        for ref in (*low_refs, *g_refs):
            ref[...] = jnp.zeros_like(ref)

    @pl.when(block * Q < length)
    def _():
        inv_gate = lax.rsqrt(sq_ref[...] / inner_all + epsilon)
        pull = inv_gate * inv_gate * inv_gate * stat_ref[...] / inner_all

        bcz = bcz_ref[...]
        sig = jax.nn.sigmoid(bcz)
        shared = bcz * sig
        shared_slope = sig * (1.0 + bcz * (1.0 - sig))
        b_rows, c_rows = shared[:states], shared[states:]
        cb = intersection(b_rows, c_rows)
        cb_blocks = (cb[:HALF, :HALF], cb[:HALF, HALF:], cb[HALF:, HALF:])
        b_low, c_low = b_rows.astype(BF16), c_rows.astype(BF16)

        step_raw = step_ref[...]
        steps = softplus(step_raw)
        running = run_ref[...]
        run_cols = jnp.transpose(running)
        ends = running[:, Q - 1 :]
        grow = jnp.exp(running)
        to_end = jnp.exp(ends - running)
        whole = jnp.exp(ends)
        upper = upper_half()

        direct, both, after, through = [], [], [], []
        for h in range(heads):
            rows = slice(h * per, (h + 1) * per)
            gate, z, y, gno = gate_ref[rows, :], z_ref[rows, :], y_ref[rows, :], gno_ref[rows, :]
            gain = twice(chan_ref[5, rows, :])
            skip = twice(chan_ref[6, rows, :])
            sig_g = jax.nn.sigmoid(gate)
            silu_g = gate * sig_g
            sig_z = jax.nn.sigmoid(z)
            v = z * sig_z
            u = y + skip * v
            m = u * silu_g
            gm = inv_gate * gain * gno - m * pull
            low[rows, :] = (gm * u * (sig_g * (1.0 + gate * (1.0 - sig_g)))).astype(BF16)
            gu = gm * silu_g
            chan_acc[5, rows, :] += fold(gu * v)
            w = v * steps[h : h + 1]
            w_low, gu_low = w.astype(BF16), gu.astype(BF16)
            decays = decay_blocks(running[h : h + 1], run_cols[:, h : h + 1], upper)
            grid = stack_blocks(*[(d * g).astype(BF16) for d, g in zip(decays, cb_blocks)])
            gw_in = nt(gu_low, grid)
            pair = nn(jnp.transpose(w_low), gu_low)
            pieces = (pair[:HALF, :HALF], pair[:HALF, HALF:], pair[HALF:, HALF:])
            for i in range(3):
                if h == 0:
                    dcb[i] = decays[i] * pieces[i]
                else:
                    dcb[i] += decays[i] * pieces[i]
            gs = gstate[rows, :]
            gs_low = gs.astype(BF16)
            gw_out = nn(gs_low, b_low) * to_end[h : h + 1]
            gw = gw_in + gw_out
            direct.append(jnp.sum(gw * v, 0, keepdims=True))
            both.append(
                jnp.sum(gu_low.astype(F32) * y - gw_in * w_low.astype(F32), 0, keepdims=True)
            )
            after.append(jnp.sum(gw_out * w, 0, keepdims=True))
            through.append(
                jnp.sum(gs * state_ref[rows, :], 0, keepdims=True) * whole[h : h + 1]
            )
            gud = (gu * grow[h : h + 1]).astype(BF16)
            gudec[rows, :] = gud
            wdec[rows, :] = (w * to_end[h : h + 1]).astype(BF16)
            gz = (skip * gu + gw * steps[h : h + 1]) * (sig_z * (1.0 + z * (1.0 - sig_z)))
            taps = [chan_ref[j, rows, :] for j in range(4)]
            gv, shifted = conv_back(gz, vhead[rows, :], taps)
            vhead[rows, :] = gz[:, :HALF]
            raw_v = val_ref[rows, :]
            for k in range(4):
                chan_acc[3 - k, rows, :] += fold(shifted[k] * raw_v)
            chan_acc[4, rows, :] += fold(gz)
            low[inner + h * per : inner + (h + 1) * per, :] = gv.astype(BF16)

        direct = jnp.concatenate(direct, 0)
        both = jnp.concatenate(both, 0)
        after = jnp.concatenate(after, 0)
        through = jnp.sum(jnp.concatenate(through, 0), -1, keepdims=True)
        g_decay = (
            times_ones(both, triangle(lambda t, r: t >= r))
            + times_ones(after, triangle(lambda s, r: s < r))
            + through
        )
        head_acc[1] += fold(steps * g_decay)
        g_step = (direct + twice(headc_ref[1]) * g_decay) * jax.nn.sigmoid(step_raw)
        head_acc[0] += fold(g_step)
        low[base : base + 16, :] = jnp.concatenate(
            [g_step, jnp.zeros((16 - heads, Q), F32)], 0
        ).astype(BF16)

        dcb_low = stack_blocks(*[dcb[i].astype(BF16) for i in range(3)])
        gud, wd = gudec[...], wdec[...]
        gs_old = gstate[...]
        g_c = nn(b_low, dcb_low) + nn(jnp.transpose(state_ref[...]).astype(BF16), gud)
        g_b = nt(c_low, dcb_low) + nn(jnp.transpose(gs_old).astype(BF16), wd)
        fresh = nt(gud, c_low)
        for h in range(heads):
            rows = slice(h * per, (h + 1) * per)
            gstate[rows, :] = gs_old[rows] * whole[h : h + 1] + fresh[rows]
        gbcz = jnp.concatenate([g_b, g_c], 0) * shared_slope
        gbc, shifted = conv_back(gbcz, bhead[...], [bcc_ref[j] for j in range(4)])
        bhead[...] = gbcz[:, :HALF]
        raw = bc_ref[...]
        for k in range(4):
            bc_acc[3 - k] += fold(shifted[k] * raw)
        bc_acc[4] += fold(gbcz)
        low[2 * inner : base, :] = gbc.astype(BF16)

        lows = jnp.transpose(low[...])
        cut = low_refs[0].shape[1]
        low_refs[0][...] = lows[:, :cut]
        low_refs[1][...] = lows[:, cut:]
        g_norm = nn(lows, wt_ref[...])
        gain = gain_row(wt_ref, base, heads)
        xs = [ref[...].astype(F32) for ref in x_refs]
        inv = rms_scale(xs, width)
        prod = None
        for k in range(4):
            cols = slice(k * part, (k + 1) * part)
            here = g_norm[:, cols] * xs[k]
            norm_acc[:, cols] += jnp.sum((here * inv).reshape(Q // 8, 8, part), 0)
            weighted = here * gain[:, cols]
            prod = weighted if prod is None else prod + weighted
        pull_x = inv * inv * inv * (jnp.sum(prod, -1, keepdims=True) / width)
        for k in range(4):
            cols = slice(k * part, (k + 1) * part)
            g_refs[k][...] = (inv * gain[:, cols] * g_norm[:, cols] - xs[k] * pull_x).astype(BF16)


def shape(dims, kind=F32):
    return jax.ShapeDtypeStruct(dims, kind)


def params(count):
    return pltpu.CompilerParams(
        dimension_semantics=("arbitrary",) * count, vmem_limit_bytes=44 << 20
    )


def fixed(array):
    rank = array.ndim
    return pl.BlockSpec(array.shape, lambda *_: (0,) * rank, pipeline_mode=pl.Buffered(1))


def run_forward(seq, seqs, lengths, xs, wt, chan, bcc, headc, before):
    part = xs[0].shape[1]
    width = 4 * part
    inner, heads, states2 = chan.shape[1], headc.shape[1], bcc.shape[1]
    blocks = SEQ_LEN // Q
    rows = seqs * SEQ_LEN
    at = lambda c: seq * blocks + c
    col = lambda n: pl.BlockSpec((n, Q), lambda c, lens: (0, at(c)))
    out_shape = [
        shape((rows, width), BF16),
        *[shape((inner, rows))] * 5,
        *[shape((states2, rows))] * 2,
        *[shape((heads, rows))] * 2,
        shape((seqs * blocks * inner, states2 // 2)),
        shape((1, SEQ_LEN)),
    ]
    out_specs = [
        pl.BlockSpec((Q, width), lambda c, lens: (at(c), 0)),
        *[col(inner)] * 5,
        *[col(states2)] * 2,
        *[col(heads)] * 2,
        pl.BlockSpec((inner, states2 // 2), lambda c, lens: (at(c), 0)),
        pl.BlockSpec((1, Q), lambda c, lens: (0, c)),
    ]
    consts = (wt, chan, bcc, headc)
    return pl.pallas_call(
        functools.partial(
            forward_kernel,
            seq=seq,
            inner=inner,
            heads=heads,
            width=width,
            aliased=len(before),
        ),
        out_shape=out_shape,
        grid_spec=pltpu.PrefetchScalarGridSpec(
            num_scalar_prefetch=1,
            grid=(blocks,),
            in_specs=[
                *[pl.BlockSpec((Q, part), lambda c, lens: (c, 0))] * 4,
                *[fixed(array) for array in consts],
                *[pl.BlockSpec(memory_space=pl.ANY)] * len(before),
            ],
            out_specs=out_specs,
            scratch_shapes=[
                pltpu.VMEM((2 * inner + states2 + 16, Q), F32),
                pltpu.VMEM((inner, HALF), F32),
                pltpu.VMEM((states2, HALF), F32),
                pltpu.VMEM((inner, states2 // 2), F32),
            ],
        ),
        input_output_aliases={9 + i: i for i in range(len(before))},
        compiler_params=params(1),
        name="mixer_forward",
    )(lengths, *xs, *consts, *before)


def run_middle(lengths, cots, wo, chan, m, squares, inner_all):
    rows, part = cots[0].shape
    width = 4 * part
    inner = wo.shape[0]
    blocks = SEQ_LEN // Q
    at = lambda q, c: q * blocks + c
    piece = pl.BlockSpec((Q, part), lambda q, c, lens: (at(q, c), 0))
    col = lambda n: pl.BlockSpec((n, Q), lambda q, c, lens: (0, at(q, c)))
    return pl.pallas_call(
        functools.partial(middle_kernel, inner=inner, inner_all=inner_all, width=width),
        out_shape=[
            shape((rows, inner), BF16),
            *[shape((rows, part), BF16)] * 4,
            shape((inner, rows)),
            shape((1, rows)),
            shape((inner, HALF)),
        ],
        grid_spec=pltpu.PrefetchScalarGridSpec(
            num_scalar_prefetch=1,
            grid=(rows // SEQ_LEN, blocks),
            in_specs=[*[piece] * 4, fixed(wo), fixed(chan), col(inner), col(1)],
            out_specs=[
                pl.BlockSpec((Q, inner), lambda q, c, lens: (at(q, c), 0)),
                *[piece] * 4,
                col(inner),
                col(1),
                pl.BlockSpec((inner, HALF), lambda q, c, lens: (0, 0)),
            ],
            scratch_shapes=[pltpu.VMEM((inner, Q), BF16)],
        ),
        compiler_params=params(2),
        name="mixer_middle",
    )(lengths, *cots, wo, chan, m, squares)


def run_backward(seq, lengths, xs, wt, chan, bcc, headc, saved, squares, stat, inner_all):
    part = xs[0].shape[1]
    width = 4 * part
    inner, heads, states2 = chan.shape[1], headc.shape[1], bcc.shape[1]
    blocks = SEQ_LEN // Q
    back = lambda c: blocks - 1 - c
    at = lambda c: seq * blocks + back(c)
    col = lambda n: pl.BlockSpec((n, Q), lambda c, lens: (0, at(c)))
    piece = pl.BlockSpec((Q, part), lambda c, lens: (back(c), 0))
    consts = (wt, chan, bcc, headc)
    cut = inner + inner // 2
    sets = (cut, wt.shape[0] - cut)
    accs = [(6, inner, HALF), (5, states2, HALF), (2, heads, HALF), (8, width)]
    keep = lambda dims: pl.BlockSpec(dims, lambda c, lens: (0,) * len(dims))
    return pl.pallas_call(
        functools.partial(
            backward_kernel,
            seq=seq,
            inner=inner,
            inner_all=inner_all,
            heads=heads,
            width=width,
            blocks=blocks,
        ),
        out_shape=[
            *[shape((SEQ_LEN, count), BF16) for count in sets],
            *[shape((SEQ_LEN, part), BF16)] * 4,
            *[shape(dims) for dims in accs],
        ],
        grid_spec=pltpu.PrefetchScalarGridSpec(
            num_scalar_prefetch=1,
            grid=(blocks,),
            in_specs=[
                *[piece] * 4,
                *[fixed(array) for array in consts],
                *[col(inner)] * 5,
                *[col(states2)] * 2,
                *[col(heads)] * 2,
                pl.BlockSpec((inner, states2 // 2), lambda c, lens: (at(c), 0)),
                *[col(1)] * 2,
            ],
            out_specs=[
                *[pl.BlockSpec((Q, count), lambda c, lens: (back(c), 0)) for count in sets],
                *[piece] * 4,
                *[keep(dims) for dims in accs],
            ],
            scratch_shapes=[
                pltpu.VMEM((wt.shape[0], Q), BF16),
                pltpu.VMEM((inner, states2 // 2), F32),
                pltpu.VMEM((inner, HALF), F32),
                pltpu.VMEM((states2, HALF), F32),
                pltpu.VMEM((3, HALF, HALF), F32),
                pltpu.VMEM((inner, Q), BF16),
                pltpu.VMEM((inner, Q), BF16),
            ],
        ),
        compiler_params=params(1),
        name="mixer_backward",
    )(lengths, *xs, *consts, *saved, squares, stat)


def exchange(a, axis, bit):
    return lax.ppermute(a, axis, [(i, i ^ bit) for i in range(lax.axis_size(axis))])


def exchange_sum(a, axis):
    bit = 1
    while bit < lax.axis_size(axis):
        a = a + exchange(a, axis, bit)
        bit *= 2
    return a


def gather_pieces(a):
    across = exchange(a, "tensor", 2)
    beside = exchange(a, "tensor", 1)
    return a, beside, across, exchange(across, "tensor", 1)


def reduce_pieces(pieces, kind=BF16):
    own, beside, across, corner = pieces
    got_corner = exchange(corner.astype(kind), "tensor", 1)
    got_beside = exchange(beside.astype(kind), "tensor", 1)
    onward = (across.astype(F32) + got_corner.astype(F32)).astype(kind)
    here = own.astype(F32) + got_beside.astype(F32)
    return here + exchange(onward, "tensor", 2).astype(F32)


def place():
    index = lax.axis_index("dp")
    return index // 2, index % 2


def take(a, index, dim):
    return lax.dynamic_index_in_dim(a, index, dim, keepdims=False)


def round_to(count, tile):
    return count // tile * tile


def side_by_side(pick, extra):
    _, x = place()
    out = []
    for m in range(4):
        mine, other = pick(m)
        zero = [jnp.zeros((extra, mine.shape[1]), BF16)] if extra else []
        for side in (0, 1):
            out.append(jnp.concatenate([jnp.where(x == side, mine, other)] + zero, 0))
    return jnp.concatenate(out, 1)


def gather_other_way(a):
    tensor = lax.axis_index("tensor")
    whole = jnp.transpose(lax.all_gather(jnp.transpose(a), "dp", axis=0, tiled=True))
    blocks = whole.reshape(a.shape[0], 4, -1)
    return jnp.concatenate([take(blocks, tensor ^ m, 1) for m in range(4)], 1)


def z_stack(a):
    return jnp.stack([a] + [exchange(a, "dp", 2 * j) for j in (3, 2, 1)])


def slot_of(m):
    z, _ = place()
    return (4 - ((lax.axis_index("tensor") ^ m) ^ z)) % 4


def weight_columns(a, extra, ready):
    if lax.axis_size("dp") != 8:
        return jnp.pad(gather_other_way(a), ((0, extra), (0, 0))), ready
    cut = round_to(a.shape[0] * 7 // 10, 16)
    first, second = a[:cut], a[cut:]
    beside = exchange(second, "dp", 1)
    beside, ready = lax.optimization_barrier((beside, ready))
    mine = z_stack(first)
    other = exchange(first, "dp", 1)
    both = z_stack(jnp.stack([second, beside]))
    other = jnp.concatenate([other[None], exchange(mine[1:], "dp", 1)], 0)

    def pick(m):
        slot = slot_of(m)
        low = take(both, slot, 0)
        return (
            jnp.concatenate([take(mine, slot, 0), low[0]], 0),
            jnp.concatenate([take(other, slot, 0), low[1]], 0),
        )

    return side_by_side(pick, extra), ready


def hidden_columns(a):
    if lax.axis_size("dp") != 8:
        return gather_other_way(a)
    both = z_stack(jnp.stack([a, exchange(a, "dp", 1)]))

    def pick(m):
        low = take(both, slot_of(m), 0)
        return low[0], low[1]

    return side_by_side(pick, 0)


def along_z(pick):
    z, _ = place()
    total = pick(z)
    for j in (3, 2, 1):
        total = total + exchange(pick(z ^ j).astype(BF16), "dp", 2 * j).astype(F32)
    return total


def reduce_other_way(a):
    tensor = lax.axis_index("tensor")
    blocks = a.reshape(4, -1, a.shape[1])
    ordered = jnp.concatenate([take(blocks, tensor ^ m, 0) for m in range(4)], 0)
    return lax.psum_scatter(ordered, "dp", scatter_dimension=0, tiled=True)


def rows_pair_first(a):
    if lax.axis_size("dp") != 8:
        return reduce_other_way(a)
    tensor = lax.axis_index("tensor")
    _, x = place()
    blocks = a.reshape(4, 2, a.shape[0] // 8, a.shape[1])
    got = exchange(take(blocks, 1 - x, 1).astype(BF16), "dp", 1).astype(F32)
    halves = take(blocks, x, 1) + got
    return along_z(lambda z: take(halves, z ^ tensor, 0))


def rows_line_first(a):
    if lax.axis_size("dp") != 8:
        return reduce_other_way(a)
    tensor = lax.axis_index("tensor")
    _, x = place()
    blocks = a.reshape(4, 2, a.shape[0] // 8, a.shape[1])
    pairs = along_z(lambda z: take(blocks, z ^ tensor, 0))
    late = exchange(take(pairs, 1 - x, 0).astype(BF16), "dp", 1).astype(F32)
    return take(pairs, x, 0) + late


def direct_sum(a, axis, bits):
    total = a
    for bit in bits:
        total = total + exchange(a, axis, bit)
    return total


def over_rows(left, right):
    return lax.dot_general(
        left, right, (((0,), (0,)), ((), ())), preferred_element_type=F32
    )


def lanes(a):
    return jnp.broadcast_to(a[..., None], a.shape + (HALF,))


def small_constants(conv_x, conv_bc, dt_bias, a_log, skip_d, gate_gain):
    per = conv_x.shape[1] // skip_d.shape[0]
    chan = lanes(jnp.concatenate([conv_x, gate_gain[None], jnp.repeat(skip_d, per)[None]], 0))
    return chan, lanes(conv_bc), lanes(jnp.stack([dt_bias, -jnp.exp(a_log)], 0))


def per_device(
    tokens,
    lengths,
    grad_out,
    norm_gain,
    w_gate,
    w_value,
    w_bc,
    w_dt,
    conv_x,
    conv_bc,
    dt_bias,
    a_log,
    skip_d,
    gate_gain,
    w_out,
):
    tensor_count = lax.axis_size("tensor")
    tensor = lax.axis_index("tensor")
    rows, _ = tokens.shape
    seqs = rows // SEQ_LEN
    inner = w_gate.shape[1]
    inner_all = inner * tensor_count
    heads = w_dt.shape[1]
    states2 = w_bc.shape[1]
    base = 2 * inner + states2

    local = jnp.concatenate(
        [
            w_gate,
            w_value,
            w_bc,
            w_dt,
            norm_gain[:, None],
            jnp.zeros((w_gate.shape[0], 15 - heads), BF16),
        ],
        1,
    )
    xs = [gather_pieces(tokens[q * SEQ_LEN : (q + 1) * SEQ_LEN]) for q in range(seqs)]
    cots = gather_pieces(grad_out)
    ready = small_constants(conv_x, conv_bc, dt_bias, a_log, skip_d, gate_gain)
    turned = jnp.transpose(w_out)
    wt, (turned, *ready) = weight_columns(jnp.transpose(local), HALF - 16, (turned, *ready))
    turned, wt = lax.optimization_barrier((turned, wt))
    wo = hidden_columns(turned)
    chan, bcc, headc = ready

    saved, squares = [], []
    for q in range(seqs):
        *saved, here = run_forward(q, seqs, lengths, xs[q], wt, chan, bcc, headc, saved)
        squares.append(exchange_sum(here, "tensor"))
    squares = jnp.concatenate(squares, 1)
    normed, gate, val, z, y, m, *shared = saved
    nout, *branch, gno, stat, gain_acc = run_middle(lengths, cots, wo, chan, m, squares, inner_all)
    stat = exchange_sum(stat, "tensor")
    g_out = jnp.concatenate([over_rows(cot, nout) for cot in cots], 0)
    branch = reduce_pieces(branch)
    out_rows = (tokens.astype(F32) + branch).astype(BF16)
    grad_out_rows = rows_line_first(g_out)

    grad_rows, accs, sums = [], None, None
    kept = (gate, val, z, y, gno, *shared)
    for q in range(seqs):
        low_a, low_b, *rest = run_backward(
            q, lengths, xs[q], wt, chan, bcc, headc, kept, squares, stat, inner_all
        )
        gin, here = rest[:4], rest[4:]
        accs = here if accs is None else [a + b for a, b in zip(accs, here)]
        grad_rows.append(reduce_pieces(gin))
        here = normed[q * SEQ_LEN : (q + 1) * SEQ_LEN]
        part_b = over_rows(here, low_b)
        part_a = over_rows(here, low_a)
        if sums is None:
            sums = lax.optimization_barrier((part_a, part_b))
        else:
            part_b = sums[1] + part_b
            part_a = sums[0] + part_a
            sums = (part_a, part_b)
    valid = (jnp.arange(SEQ_LEN)[None] < lengths[:, None]).reshape(rows)[:, None]
    grad_rows = jnp.concatenate(grad_rows, 0) + jnp.where(valid, grad_out.astype(F32), 0.0)

    chan_acc, bc_acc, head_acc, norm_acc = accs
    cut = sums[0].shape[1]
    column = jnp.arange(sums[1].shape[1]) == base + heads - cut
    norm_column = jnp.sum(norm_acc, 0)[:, None]
    sum_b = jnp.where(column[None], norm_column, sums[1])
    grads = jnp.concatenate([rows_pair_first(sums[0]), rows_line_first(sum_b)], 1)
    rest = grads[:, 2 * inner :].reshape(tensor_count, -1, states2 + HALF)
    rest = reduce_pieces([take(rest, tensor ^ i, 0) for i in range(4)], F32)
    sizes = [5 * inner, inner, inner, 2 * heads, 5 * states2]
    flat = jnp.concatenate(
        [
            jnp.sum(chan_acc, -1).reshape(-1),
            jnp.sum(gain_acc, -1),
            jnp.sum(head_acc, -1).reshape(-1),
            jnp.sum(bc_acc, -1).reshape(-1),
        ]
    )
    if lax.axis_size("dp") == 8:
        flat = direct_sum(flat, "dp", (1,))
        flat = direct_sum(flat, "dp", (2, 4, 6))
    else:
        flat = exchange_sum(flat, "dp")
    cuts = [sum(sizes[: i + 1]) for i in range(4)]
    g_conv, g_skip, g_gain, g_head, g_conv_bc = jnp.split(flat, cuts)
    g_conv_bc = direct_sum(g_conv_bc, "tensor", (1, 2, 3))
    return (
        out_rows,
        grad_rows,
        rest[:, states2 + heads],
        grads[:, :inner],
        grads[:, inner : 2 * inner],
        rest[:, :states2],
        grads[:, base : base + heads],
        g_conv.reshape(5, inner),
        g_conv_bc.reshape(5, states2),
        g_head[:heads],
        g_head[heads:] * -jnp.exp(a_log),
        jnp.sum(g_skip.reshape(heads, -1), -1),
        g_gain,
        grad_out_rows,
    )


def solution(mesh):
    return mapped(mesh)


def mapped(mesh):
    both = ("dp", "tensor")
    return jax.shard_map(
        per_device,
        mesh=mesh,
        in_specs=(
            P("dp", "tensor"),
            P("dp"),
            P("dp", "tensor"),
            P("dp"),
            P("dp", "tensor"),
            P("dp", "tensor"),
            P("dp", None),
            P("dp", "tensor"),
            P(None, "tensor"),
            P(),
            P("tensor"),
            P("tensor"),
            P("tensor"),
            P("tensor"),
            P("dp", "tensor"),
        ),
        out_specs=(
            P("dp", "tensor"),
            P("dp", "tensor"),
            P(both),
            P("dp", "tensor"),
            P("dp", "tensor"),
            P(both, None),
            P("dp", "tensor"),
            P(None, "tensor"),
            P(),
            P("tensor"),
            P("tensor"),
            P("tensor"),
            P("tensor"),
            P("dp", "tensor"),
        ),
        check_vma=False,
    )
```

```python
import functools

import jax
import jax.numpy as jnp
from jax import lax
from jax.experimental import pallas as pl
from jax.experimental.pallas import tpu as pltpu
from jax.sharding import PartitionSpec as P


SEQ_LEN = 2048
Q = 256
HALF = 128
F32 = jnp.float32
BF16 = jnp.bfloat16
epsilon = 1e-05
NEG = -1e30


def nn(a, b):
    return lax.dot_general(a, b, (((1,), (0,)), ((), ())), preferred_element_type=F32)


def nt(a, b):
    return lax.dot_general(a, b, (((1,), (1,)), ((), ())), preferred_element_type=F32)


def split3(a):
    high = a.astype(BF16)
    rest = a - high.astype(F32)
    mid = rest.astype(BF16)
    low = (rest - mid.astype(F32)).astype(BF16)
    return high, mid, low


def times_ones(a, ones):
    rows = a.shape[0]
    got = nn(jnp.concatenate(split3(a), 0), ones)
    return got[:rows] + got[rows : 2 * rows] + got[2 * rows :]


def twice(a):
    return jnp.concatenate([a, a], 1)


def fold(a):
    return a[:, :HALF] + a[:, HALF:]


def triangle(keep):
    row = lax.broadcasted_iota(jnp.int32, (Q, Q), 0)
    col = lax.broadcasted_iota(jnp.int32, (Q, Q), 1)
    return jnp.where(keep(row, col), 1.0, 0.0).astype(BF16)


def conv(raw, tail, taps):
    ext = jnp.concatenate([tail, raw], 1)
    total = twice(taps[4]) + twice(taps[3]) * raw
    for k in range(1, 4):
        total = total + twice(taps[3 - k]) * pltpu.roll(ext, k, 1)[:, HALF:]
    return total


def conv_back(grad, head, taps):
    ext = jnp.concatenate([grad, head], 1)
    shifted = [grad] + [pltpu.roll(ext, 3 * HALF - k, 1)[:, :Q] for k in range(1, 4)]
    total = twice(taps[3]) * grad
    for k in range(1, 4):
        total = total + twice(taps[3 - k]) * shifted[k]
    return total, shifted


def decay_blocks(run_row, run_col, upper):
    early, late = run_row[:, :HALF], run_row[:, HALF:]
    col_early = jnp.broadcast_to(run_col[:HALF], (HALF, HALF))
    col_late = jnp.broadcast_to(run_col[HALF:], (HALF, HALF))
    first = jnp.exp(jnp.where(upper, early - col_early, NEG))
    cross = jnp.exp(late - col_early)
    second = jnp.exp(jnp.where(upper, late - col_late, NEG))
    return first, cross, second


def stack_blocks(first, cross, second):
    zero = jnp.zeros((HALF, HALF), first.dtype)
    return jnp.concatenate(
        [jnp.concatenate([first, cross], 1), jnp.concatenate([zero, second], 1)], 0
    )


def intersection(b_rows, c_rows):
    b_time = jnp.transpose(b_rows)
    b_high = b_time.astype(BF16)
    b_low = (b_time - b_high.astype(F32)).astype(BF16)
    c_high = c_rows.astype(BF16)
    c_low = (c_rows - c_high.astype(F32)).astype(BF16)
    full = nn(
        jnp.concatenate([b_high, b_low, b_high], 1), jnp.concatenate([c_high, c_high, c_low], 0)
    )
    return (full[:HALF, :HALF], full[:HALF, HALF:], full[HALF:, HALF:]), b_high


def rms_scale(xs, width):
    total = xs[0] * xs[0]
    for x in xs[1:]:
        total = total + x * x
    return lax.rsqrt(jnp.sum(total, -1, keepdims=True) / width + epsilon)


def gain_row(wt_ref, base, heads):
    return wt_ref[base : base + 16, :].astype(F32)[heads : heads + 1]


def softplus(a):
    return jnp.maximum(a, 0.0) + jnp.log1p(jnp.exp(-jnp.abs(a)))


def upper_half():
    row = lax.broadcasted_iota(jnp.int32, (HALF, HALF), 0)
    return row <= lax.broadcasted_iota(jnp.int32, (HALF, HALF), 1)


def valid_row(block, length):
    pos = block * Q + lax.broadcasted_iota(jnp.int32, (1, Q), 1)
    return jnp.where(pos < length, 1.0, 0.0)


def forward_kernel(len_ref, *refs, seq, inner, heads, width, aliased):
    x_refs, (wt_ref, chan_ref, bcc_ref, headc_ref) = refs[:4], refs[4:8]
    refs = refs[8 + aliased :]
    (norm_ref, gate_ref, val_ref, z_ref, y_ref, m_ref, bc_ref, bcz_ref) = refs[:8]
    (step_ref, run_ref, state_ref, stat_ref, proj, vtail, btail, state, carried, wdec) = refs[8:]
    block = pl.program_id(0)
    length = len_ref[seq]
    per = inner // heads
    part = width // 4
    states = bc_ref.shape[0] // 2

    @pl.when(block == 0)
    def _():
        vtail[...] = jnp.zeros_like(vtail)
        btail[...] = jnp.zeros_like(btail)
        state[...] = jnp.zeros_like(state)

    @pl.when(block * Q >= length)
    def _():
        norm_ref[...] = jnp.zeros_like(norm_ref)
        stat_ref[...] = jnp.zeros_like(stat_ref)

    @pl.when(block * Q < length)
    def _():
        base = 2 * inner + 2 * states
        gain = gain_row(wt_ref, base, heads)
        xs = [ref[...].astype(F32) for ref in x_refs]
        inv = rms_scale(xs, width)
        for k in range(4):
            cols = slice(k * part, (k + 1) * part)
            norm_ref[:, cols] = (xs[k] * inv * gain[:, cols]).astype(BF16)
        proj[...] = nt(wt_ref[: base + 16, :], norm_ref[...])

        raw = proj[2 * inner : base, :]
        bc_ref[...] = raw
        bcz = conv(raw, btail[...], [bcc_ref[j] for j in range(5)])
        btail[...] = raw[:, HALF:]
        bcz_ref[...] = bcz
        shared = bcz * jax.nn.sigmoid(bcz)
        b_rows, c_rows = shared[:states], shared[states:]
        cb_blocks, b_time = intersection(b_rows, c_rows)
        c_low = c_rows.astype(BF16)

        step_raw = proj[base : base + heads, :] + twice(headc_ref[0])
        step_ref[...] = step_raw
        steps = softplus(step_raw)
        running = times_ones(steps * twice(headc_ref[1]), triangle(lambda s, t: s <= t))
        run_ref[...] = running
        run_cols = jnp.transpose(running)
        ends = running[:, Q - 1 :]
        grow = jnp.exp(running)
        to_end = jnp.exp(ends - running)
        whole = jnp.exp(ends)
        upper = upper_half()

        state_ref[...] = state[...]
        carried[...] = nn(state[...].astype(BF16), c_low)
        squares = jnp.zeros((1, Q), F32)
        for h in range(heads):
            rows = slice(h * per, (h + 1) * per)
            raw_v = proj[inner + h * per : inner + (h + 1) * per, :]
            gate = proj[rows, :]
            val_ref[rows, :] = raw_v
            gate_ref[rows, :] = gate
            z = conv(raw_v, vtail[rows, :], [chan_ref[j, rows, :] for j in range(5)])
            vtail[rows, :] = raw_v[:, HALF:]
            z_ref[rows, :] = z
            v = z * jax.nn.sigmoid(z)
            w = v * steps[h : h + 1]
            decays = decay_blocks(running[h : h + 1], run_cols[:, h : h + 1], upper)
            grid = stack_blocks(*[(d * g).astype(BF16) for d, g in zip(decays, cb_blocks)])
            y = nn(w.astype(BF16), grid) + carried[rows, :] * grow[h : h + 1]
            y_ref[rows, :] = y
            wdec[rows, :] = (w * to_end[h : h + 1]).astype(BF16)
            u = y + twice(chan_ref[6, rows, :]) * v
            m = u * gate * jax.nn.sigmoid(gate)
            m_ref[rows, :] = m
            squares = squares + jnp.sum(m * m, 0, keepdims=True)
        stat_ref[...] = squares
        fresh = nn(wdec[...], b_time)
        for h in range(heads):
            rows = slice(h * per, (h + 1) * per)
            state[rows, :] = state[rows, :] * whole[h : h + 1] + fresh[rows]


def middle_kernel(len_ref, *refs, seq, inner, inner_all, width, aliased):
    c0, c1, c2, c3, wo_ref, chan_ref, m_ref, sq_ref = refs[:8]
    nout_ref, b0, b1, b2, b3, gno_ref, stat_ref, gain_acc, nout = refs[8 + aliased :]
    block = pl.program_id(0)
    length = len_ref[seq]
    part = width // 4

    @pl.when(block == 0)
    def _():
        gain_acc[...] = jnp.zeros_like(gain_acc)

    @pl.when(block * Q >= length)
    def _():
        nout_ref[...] = jnp.zeros_like(nout_ref)
        stat_ref[...] = jnp.zeros_like(stat_ref)
        for ref in (b0, b1, b2, b3):
            ref[...] = jnp.zeros_like(ref)

    @pl.when(block * Q < length)
    def _():
        valid = valid_row(block, length)
        scale = lax.rsqrt(sq_ref[...] / inner_all + epsilon) * valid
        cot = jnp.concatenate([ref[...] for ref in (c0, c1, c2, c3)], 1)
        gno_ref[...] = nt(wo_ref[...], cot) * valid
        inners = jnp.zeros((1, Q), F32)
        for lo in range(0, inner, 64):
            rows = slice(lo, lo + 64)
            gain = twice(chan_ref[5, rows, :])
            m = m_ref[rows, :]
            gno = gno_ref[rows, :]
            nout[rows, :] = (m * scale * gain).astype(BF16)
            inners = inners + jnp.sum(gno * gain * m, 0, keepdims=True)
            gain_acc[rows, :] += fold(gno * m * scale)
        stat_ref[...] = inners
        nout_time = jnp.transpose(nout[...])
        nout_ref[...] = nout_time
        branch = nn(nout_time, wo_ref[...])
        for k, ref in enumerate((b0, b1, b2, b3)):
            ref[...] = branch[:, k * part : (k + 1) * part].astype(BF16)


def backward_kernel(len_ref, *refs, seq, inner, inner_all, heads, width, blocks):
    x_refs, (wt_ref, chan_ref, bcc_ref, headc_ref) = refs[:4], refs[4:8]
    (gate_ref, val_ref, z_ref, y_ref, gno_ref, bc_ref, bcz_ref) = refs[8:15]
    (step_ref, run_ref, state_ref, sq_ref, stat_ref) = refs[15:20]
    low_refs, g_refs, (chan_acc, bc_acc, head_acc, norm_acc) = refs[20:22], refs[22:26], refs[26:30]
    low, gstate, vhead, bhead, dcb, wdec, gudec, sent = refs[30:]
    step = pl.program_id(0)
    block = blocks - 1 - step
    length = len_ref[seq]
    per = inner // heads
    part = width // 4
    states = bc_ref.shape[0] // 2
    base = 2 * inner + 2 * states

    @pl.when(step == 0)
    def _():
        chan_acc[...] = jnp.zeros_like(chan_acc)
        bc_acc[...] = jnp.zeros_like(bc_acc)
        head_acc[...] = jnp.zeros_like(head_acc)
        norm_acc[...] = jnp.zeros_like(norm_acc)
        low[base:, :] = jnp.zeros_like(low[base:, :])
        gstate[...] = jnp.zeros_like(gstate)
        vhead[...] = jnp.zeros_like(vhead)
        bhead[...] = jnp.zeros_like(bhead)

    @pl.when(block * Q >= length)
    def _():
        for ref in (*low_refs, *g_refs):
            ref[...] = jnp.zeros_like(ref)

    @pl.when(block * Q < length)
    def _():
        inv_gate = lax.rsqrt(sq_ref[...] / inner_all + epsilon)
        pull = inv_gate * inv_gate * inv_gate * stat_ref[...] / inner_all

        bcz = bcz_ref[...]
        sig = jax.nn.sigmoid(bcz)
        shared = bcz * sig
        shared_slope = sig * (1.0 + bcz * (1.0 - sig))
        b_rows, c_rows = shared[:states], shared[states:]
        cb_blocks, _ = intersection(b_rows, c_rows)
        b_low, c_low = b_rows.astype(BF16), c_rows.astype(BF16)

        step_raw = step_ref[...]
        steps = softplus(step_raw)
        running = run_ref[...]
        run_cols = jnp.transpose(running)
        ends = running[:, Q - 1 :]
        grow = jnp.exp(running)
        to_end = jnp.exp(ends - running)
        whole = jnp.exp(ends)
        upper = upper_half()

        sent[...] = nn(gstate[...].astype(BF16), b_low)
        direct, both, after, through = [], [], [], []
        for h in range(heads):
            rows = slice(h * per, (h + 1) * per)
            gate, z, y, gno = gate_ref[rows, :], z_ref[rows, :], y_ref[rows, :], gno_ref[rows, :]
            gain = twice(chan_ref[5, rows, :])
            skip = twice(chan_ref[6, rows, :])
            sig_g = jax.nn.sigmoid(gate)
            silu_g = gate * sig_g
            sig_z = jax.nn.sigmoid(z)
            v = z * sig_z
            u = y + skip * v
            m = u * silu_g
            gm = inv_gate * gain * gno - m * pull
            low[rows, :] = (gm * u * (sig_g * (1.0 + gate * (1.0 - sig_g)))).astype(BF16)
            gu = gm * silu_g
            chan_acc[5, rows, :] += fold(gu * v)
            w = v * steps[h : h + 1]
            w_low, gu_low = w.astype(BF16), gu.astype(BF16)
            decays = decay_blocks(running[h : h + 1], run_cols[:, h : h + 1], upper)
            grid = stack_blocks(*[(d * g).astype(BF16) for d, g in zip(decays, cb_blocks)])
            gw_in = nt(gu_low, grid)
            pair = nn(jnp.transpose(w_low), gu_low)
            pieces = (pair[:HALF, :HALF], pair[:HALF, HALF:], pair[HALF:, HALF:])
            for i in range(3):
                if h == 0:
                    dcb[i] = decays[i] * pieces[i]
                else:
                    dcb[i] += decays[i] * pieces[i]
            gs = gstate[rows, :]
            gw_out = sent[rows, :] * to_end[h : h + 1]
            gw = gw_in + gw_out
            direct.append(jnp.sum(gw * v, 0, keepdims=True))
            both.append(
                jnp.sum(gu_low.astype(F32) * y - gw_in * w_low.astype(F32), 0, keepdims=True)
            )
            after.append(jnp.sum(gw_out * w, 0, keepdims=True))
            through.append(
                jnp.sum(gs * state_ref[rows, :], 0, keepdims=True) * whole[h : h + 1]
            )
            gud = (gu * grow[h : h + 1]).astype(BF16)
            gudec[rows, :] = gud
            wdec[rows, :] = (w * to_end[h : h + 1]).astype(BF16)
            gz = (skip * gu + gw * steps[h : h + 1]) * (sig_z * (1.0 + z * (1.0 - sig_z)))
            taps = [chan_ref[j, rows, :] for j in range(4)]
            gv, shifted = conv_back(gz, vhead[rows, :], taps)
            vhead[rows, :] = gz[:, :HALF]
            raw_v = val_ref[rows, :]
            for k in range(4):
                chan_acc[3 - k, rows, :] += fold(shifted[k] * raw_v)
            chan_acc[4, rows, :] += fold(gz)
            low[inner + h * per : inner + (h + 1) * per, :] = gv.astype(BF16)

        direct = jnp.concatenate(direct, 0)
        both = jnp.concatenate(both, 0)
        after = jnp.concatenate(after, 0)
        through = jnp.sum(jnp.concatenate(through, 0), -1, keepdims=True)
        g_decay = (
            times_ones(both, triangle(lambda t, r: t >= r))
            + times_ones(after, triangle(lambda s, r: s < r))
            + through
        )
        head_acc[1] += fold(steps * g_decay)
        g_step = (direct + twice(headc_ref[1]) * g_decay) * jax.nn.sigmoid(step_raw)
        head_acc[0] += fold(g_step)
        low[base : base + 16, :] = jnp.concatenate(
            [g_step, jnp.zeros((16 - heads, Q), F32)], 0
        ).astype(BF16)

        dcb_low = stack_blocks(*[dcb[i].astype(BF16) for i in range(3)])
        gud, wd = gudec[...], wdec[...]
        gs_old = gstate[...]
        g_c = nn(b_low, dcb_low) + nn(jnp.transpose(state_ref[...]).astype(BF16), gud)
        g_b = nt(c_low, dcb_low) + nn(jnp.transpose(gs_old).astype(BF16), wd)
        fresh = nn(gud, jnp.transpose(c_low))
        for h in range(heads):
            rows = slice(h * per, (h + 1) * per)
            gstate[rows, :] = gs_old[rows] * whole[h : h + 1] + fresh[rows]
        gbcz = jnp.concatenate([g_b, g_c], 0) * shared_slope
        gbc, shifted = conv_back(gbcz, bhead[...], [bcc_ref[j] for j in range(4)])
        bhead[...] = gbcz[:, :HALF]
        raw = bc_ref[...]
        for k in range(4):
            bc_acc[3 - k] += fold(shifted[k] * raw)
        bc_acc[4] += fold(gbcz)
        low[2 * inner : base, :] = gbc.astype(BF16)

        lows = jnp.transpose(low[...])
        cut = low_refs[0].shape[1]
        low_refs[0][...] = lows[:, :cut]
        low_refs[1][...] = lows[:, cut:]
        g_norm = nn(lows, wt_ref[...])
        gain = gain_row(wt_ref, base, heads)
        xs = [ref[...].astype(F32) for ref in x_refs]
        inv = rms_scale(xs, width)
        prod = None
        for k in range(4):
            cols = slice(k * part, (k + 1) * part)
            here = g_norm[:, cols] * xs[k]
            norm_acc[:, cols] += jnp.sum((here * inv).reshape(Q // 8, 8, part), 0)
            weighted = here * gain[:, cols]
            prod = weighted if prod is None else prod + weighted
        pull_x = inv * inv * inv * (jnp.sum(prod, -1, keepdims=True) / width)
        for k in range(4):
            cols = slice(k * part, (k + 1) * part)
            g_refs[k][...] = (inv * gain[:, cols] * g_norm[:, cols] - xs[k] * pull_x).astype(BF16)


def shape(dims, kind=F32):
    return jax.ShapeDtypeStruct(dims, kind)


def params(count):
    return pltpu.CompilerParams(
        dimension_semantics=("arbitrary",) * count, vmem_limit_bytes=44 << 20
    )


def fixed(array):
    rank = array.ndim
    return pl.BlockSpec(array.shape, lambda *_: (0,) * rank, pipeline_mode=pl.Buffered(1))


def run_forward(seq, seqs, lengths, xs, wt, chan, bcc, headc, before):
    part = xs[0].shape[1]
    width = 4 * part
    inner, heads, states2 = chan.shape[1], headc.shape[1], bcc.shape[1]
    blocks = SEQ_LEN // Q
    rows = seqs * SEQ_LEN
    at = lambda c: seq * blocks + c
    col = lambda n: pl.BlockSpec((n, Q), lambda c, lens: (0, at(c)))
    out_shape = [
        shape((rows, width), BF16),
        *[shape((inner, rows))] * 5,
        *[shape((states2, rows))] * 2,
        *[shape((heads, rows))] * 2,
        shape((seqs * blocks * inner, states2 // 2)),
        shape((1, SEQ_LEN)),
    ]
    out_specs = [
        pl.BlockSpec((Q, width), lambda c, lens: (at(c), 0)),
        *[col(inner)] * 5,
        *[col(states2)] * 2,
        *[col(heads)] * 2,
        pl.BlockSpec((inner, states2 // 2), lambda c, lens: (at(c), 0)),
        pl.BlockSpec((1, Q), lambda c, lens: (0, c)),
    ]
    consts = (wt, chan, bcc, headc)
    return pl.pallas_call(
        functools.partial(
            forward_kernel,
            seq=seq,
            inner=inner,
            heads=heads,
            width=width,
            aliased=len(before),
        ),
        out_shape=out_shape,
        grid_spec=pltpu.PrefetchScalarGridSpec(
            num_scalar_prefetch=1,
            grid=(blocks,),
            in_specs=[
                *[pl.BlockSpec((Q, part), lambda c, lens: (c, 0))] * 4,
                *[fixed(array) for array in consts],
                *[pl.BlockSpec(memory_space=pl.ANY)] * len(before),
            ],
            out_specs=out_specs,
            scratch_shapes=[
                pltpu.VMEM((2 * inner + states2 + 16, Q), F32),
                pltpu.VMEM((inner, HALF), F32),
                pltpu.VMEM((states2, HALF), F32),
                pltpu.VMEM((inner, states2 // 2), F32),
                pltpu.VMEM((inner, Q), F32),
                pltpu.VMEM((inner, Q), BF16),
            ],
        ),
        input_output_aliases={9 + i: i for i in range(len(before))},
        compiler_params=params(1),
        name="mixer_forward",
    )(lengths, *xs, *consts, *before)


def run_middle(seq, lengths, cots, wo, chan, m, squares, inner_all, before):
    rows, part = cots[0].shape
    width = 4 * part
    inner = wo.shape[0]
    blocks = SEQ_LEN // Q
    at = lambda c: seq * blocks + c
    piece = pl.BlockSpec((Q, part), lambda c, lens: (at(c), 0))
    col = pl.BlockSpec((inner, Q), lambda c, lens: (0, at(c)))
    stat = pl.BlockSpec((1, Q), lambda c, lens: (0, c))
    return pl.pallas_call(
        functools.partial(
            middle_kernel,
            seq=seq,
            inner=inner,
            inner_all=inner_all,
            width=width,
            aliased=len(before),
        ),
        out_shape=[
            shape((rows, inner), BF16),
            *[shape((rows, part), BF16)] * 4,
            shape((inner, rows)),
            shape((1, SEQ_LEN)),
            shape((inner, HALF)),
        ],
        grid_spec=pltpu.PrefetchScalarGridSpec(
            num_scalar_prefetch=1,
            grid=(blocks,),
            in_specs=[
                *[piece] * 4,
                fixed(wo),
                fixed(chan),
                col,
                stat,
                *[pl.BlockSpec(memory_space=pl.ANY)] * len(before),
            ],
            out_specs=[
                pl.BlockSpec((Q, inner), lambda c, lens: (at(c), 0)),
                *[piece] * 4,
                col,
                stat,
                pl.BlockSpec((inner, HALF), lambda c, lens: (0, 0)),
            ],
            scratch_shapes=[pltpu.VMEM((inner, Q), BF16)],
        ),
        input_output_aliases={9 + i: i for i in range(len(before))},
        compiler_params=params(1),
        name="mixer_middle",
    )(lengths, *cots, wo, chan, m, squares, *before)


def run_backward(seq, lengths, xs, wt, chan, bcc, headc, saved, squares, stat, inner_all):
    part = xs[0].shape[1]
    width = 4 * part
    inner, heads, states2 = chan.shape[1], headc.shape[1], bcc.shape[1]
    blocks = SEQ_LEN // Q
    back = lambda c: blocks - 1 - c
    at = lambda c: seq * blocks + back(c)
    col = lambda n: pl.BlockSpec((n, Q), lambda c, lens: (0, at(c)))
    piece = pl.BlockSpec((Q, part), lambda c, lens: (back(c), 0))
    consts = (wt, chan, bcc, headc)
    cut = inner + inner // 2
    sets = (cut, wt.shape[0] - cut)
    accs = [(6, inner, HALF), (5, states2, HALF), (2, heads, HALF), (8, width)]
    keep = lambda dims: pl.BlockSpec(dims, lambda c, lens: (0,) * len(dims))
    return pl.pallas_call(
        functools.partial(
            backward_kernel,
            seq=seq,
            inner=inner,
            inner_all=inner_all,
            heads=heads,
            width=width,
            blocks=blocks,
        ),
        out_shape=[
            *[shape((SEQ_LEN, count), BF16) for count in sets],
            *[shape((SEQ_LEN, part), BF16)] * 4,
            *[shape(dims) for dims in accs],
        ],
        grid_spec=pltpu.PrefetchScalarGridSpec(
            num_scalar_prefetch=1,
            grid=(blocks,),
            in_specs=[
                *[piece] * 4,
                *[fixed(array) for array in consts],
                *[col(inner)] * 5,
                *[col(states2)] * 2,
                *[col(heads)] * 2,
                pl.BlockSpec((inner, states2 // 2), lambda c, lens: (at(c), 0)),
                *[pl.BlockSpec((1, Q), lambda c, lens: (0, back(c)))] * 2,
            ],
            out_specs=[
                *[pl.BlockSpec((Q, count), lambda c, lens: (back(c), 0)) for count in sets],
                *[piece] * 4,
                *[keep(dims) for dims in accs],
            ],
            scratch_shapes=[
                pltpu.VMEM((wt.shape[0], Q), BF16),
                pltpu.VMEM((inner, states2 // 2), F32),
                pltpu.VMEM((inner, HALF), F32),
                pltpu.VMEM((states2, HALF), F32),
                pltpu.VMEM((3, HALF, HALF), F32),
                pltpu.VMEM((inner, Q), BF16),
                pltpu.VMEM((inner, Q), BF16),
                pltpu.VMEM((inner, Q), F32),
            ],
        ),
        compiler_params=params(1),
        name="mixer_backward",
    )(lengths, *xs, *consts, *saved, squares, stat)


def exchange(a, axis, bit):
    return lax.ppermute(a, axis, [(i, i ^ bit) for i in range(lax.axis_size(axis))])


def exchange_sum(a, axis):
    bit = 1
    while bit < lax.axis_size(axis):
        a = a + exchange(a, axis, bit)
        bit *= 2
    return a


def gather_pieces(a):
    across = exchange(a, "tensor", 2)
    beside = exchange(a, "tensor", 1)
    return a, beside, across, exchange(across, "tensor", 1)


def reduce_pieces(pieces, kind=BF16):
    own, beside, across, corner = pieces
    got_corner = exchange(corner.astype(kind), "tensor", 1)
    got_beside = exchange(beside.astype(kind), "tensor", 1)
    onward = (across.astype(F32) + got_corner.astype(F32)).astype(kind)
    last = exchange(onward, "tensor", 2).astype(F32)
    return own.astype(F32) + got_beside.astype(F32) + last


def place():
    index = lax.axis_index("dp")
    return index // 2, index % 2


def take(a, index, dim):
    return lax.dynamic_index_in_dim(a, index, dim, keepdims=False)


def round_to(count, tile):
    return count // tile * tile


def side_by_side(pick, extra):
    _, x = place()
    out = []
    for m in range(4):
        mine, other = pick(m)
        zero = [jnp.zeros((extra, mine.shape[1]), BF16)] if extra else []
        for side in (0, 1):
            out.append(jnp.concatenate([jnp.where(x == side, mine, other)] + zero, 0))
    return jnp.concatenate(out, 1)


def gather_other_way(a):
    tensor = lax.axis_index("tensor")
    whole = jnp.transpose(lax.all_gather(jnp.transpose(a), "dp", axis=0, tiled=True))
    blocks = whole.reshape(a.shape[0], 4, -1)
    return jnp.concatenate([take(blocks, tensor ^ m, 1) for m in range(4)], 1)


ROUNDS = ((3, 2, 1), (1, 3, 2))


def exchange_z(a, turn):
    count, tensor_count = lax.axis_size("dp"), lax.axis_size("tensor")
    pairs = [
        (d * tensor_count + t, (d ^ (2 * ROUNDS[t % 2][turn])) * tensor_count + t)
        for d in range(count)
        for t in range(tensor_count)
    ]
    return lax.ppermute(a, ("dp", "tensor"), pairs)


def even_core():
    return lax.axis_index("tensor") % 2 == 0


def distance(turn):
    return jnp.where(even_core(), ROUNDS[0][turn], ROUNDS[1][turn])


def z_stack(a):
    return jnp.stack([a] + [exchange_z(a, turn) for turn in range(3)])


def slot_of(m):
    z, _ = place()
    j = (lax.axis_index("tensor") ^ m) ^ z
    return jnp.where(even_core(), (4 - j) % 4, jnp.where(j >= 2, 5 - j, j))


def weight_columns(a, extra, ready):
    if lax.axis_size("dp") != 8:
        return jnp.pad(gather_other_way(a), ((0, extra), (0, 0))), ready
    cut = round_to(a.shape[0] * 6 // 10, 16)
    first, second = a[:cut], a[cut:]
    beside = exchange(second, "dp", 1)
    beside, ready = lax.optimization_barrier((beside, ready))
    mine = z_stack(first)
    other = exchange(first, "dp", 1)
    pair = jnp.stack([second, beside])
    both = z_stack(pair)
    other = jnp.concatenate([other[None], exchange(mine[1:], "dp", 1)], 0)

    def pick(m):
        slot = slot_of(m)
        low = take(both, slot, 0)
        return (
            jnp.concatenate([take(mine, slot, 0), low[0]], 0),
            jnp.concatenate([take(other, slot, 0), low[1]], 0),
        )

    return side_by_side(pick, extra), ready


def hidden_columns(a):
    if lax.axis_size("dp") != 8:
        return gather_other_way(a)
    both = z_stack(jnp.stack([a, exchange(a, "dp", 1)]))

    def pick(m):
        low = take(both, slot_of(m), 0)
        return low[0], low[1]

    return side_by_side(pick, 0)


def along_z(pick):
    z, _ = place()
    total = pick(z)
    for turn in range(3):
        send = pick(z ^ distance(turn)).astype(BF16)
        total = total + exchange_z(send, turn).astype(F32)
    return total


def reduce_other_way(a):
    tensor = lax.axis_index("tensor")
    blocks = a.reshape(4, -1, a.shape[1])
    ordered = jnp.concatenate([take(blocks, tensor ^ m, 0) for m in range(4)], 0)
    return lax.psum_scatter(ordered, "dp", scatter_dimension=0, tiled=True)


def rows_pair_first(a):
    if lax.axis_size("dp") != 8:
        return reduce_other_way(a)
    tensor = lax.axis_index("tensor")
    _, x = place()
    blocks = a.reshape(4, 2, a.shape[0] // 8, a.shape[1])
    got = exchange(take(blocks, 1 - x, 1).astype(BF16), "dp", 1).astype(F32)
    halves = take(blocks, x, 1) + got
    return along_z(lambda z: take(halves, z ^ tensor, 0))


def rows_line_first(a):
    if lax.axis_size("dp") != 8:
        return reduce_other_way(a)
    tensor = lax.axis_index("tensor")
    _, x = place()
    blocks = a.reshape(4, 2, a.shape[0] // 8, a.shape[1])
    pairs = along_z(lambda z: take(blocks, z ^ tensor, 0))
    late = exchange(take(pairs, 1 - x, 0).astype(BF16), "dp", 1).astype(F32)
    return take(pairs, x, 0) + late


def direct_sum(a, axis, bits):
    total = a
    for bit in bits:
        total = total + exchange(a, axis, bit)
    return total


def over_rows(left, right):
    return lax.dot_general(
        left, right, (((0,), (0,)), ((), ())), preferred_element_type=F32
    )


def lanes(a):
    return jnp.broadcast_to(a[..., None], a.shape + (HALF,))


def small_constants(conv_x, conv_bc, dt_bias, a_log, skip_d, gate_gain):
    per = conv_x.shape[1] // skip_d.shape[0]
    chan = lanes(jnp.concatenate([conv_x, gate_gain[None], jnp.repeat(skip_d, per)[None]], 0))
    return chan, lanes(conv_bc), lanes(jnp.stack([dt_bias, -jnp.exp(a_log)], 0))


def per_device(
    tokens,
    lengths,
    grad_out,
    norm_gain,
    w_gate,
    w_value,
    w_bc,
    w_dt,
    conv_x,
    conv_bc,
    dt_bias,
    a_log,
    skip_d,
    gate_gain,
    w_out,
):
    tensor_count = lax.axis_size("tensor")
    tensor = lax.axis_index("tensor")
    rows, _ = tokens.shape
    seqs = rows // SEQ_LEN
    inner = w_gate.shape[1]
    inner_all = inner * tensor_count
    heads = w_dt.shape[1]
    states2 = w_bc.shape[1]
    base = 2 * inner + states2

    local = jnp.concatenate(
        [
            w_gate,
            w_value,
            w_bc,
            w_dt,
            norm_gain[:, None],
            jnp.zeros((w_gate.shape[0], 15 - heads), BF16),
        ],
        1,
    )
    xs = [gather_pieces(tokens[q * SEQ_LEN : (q + 1) * SEQ_LEN]) for q in range(seqs)]
    cots = gather_pieces(grad_out)
    ready = small_constants(conv_x, conv_bc, dt_bias, a_log, skip_d, gate_gain)
    wt, (turned, *ready) = weight_columns(
        jnp.transpose(local), HALF - 16, (jnp.transpose(w_out), *ready)
    )
    wo = hidden_columns(turned)
    chan, bcc, headc = ready

    saved, squares = [], []
    for q in range(seqs):
        *saved, here = run_forward(q, seqs, lengths, xs[q], wt, chan, bcc, headc, saved)
        squares.append(direct_sum(here, "tensor", (1, 2, 3)))
    normed, gate, val, z, y, m, *shared = saved
    middle, stats, gain_acc = [], [], None
    for q in range(seqs):
        *middle, stat, here = run_middle(
            q, lengths, cots, wo, chan, m, squares[q], inner_all, middle
        )
        stats.append(direct_sum(stat, "tensor", (1, 2, 3)))
        gain_acc = here if gain_acc is None else gain_acc + here
    nout, *branch, gno = middle
    g_out = jnp.concatenate([over_rows(cot, nout) for cot in cots], 0)
    branch = reduce_pieces(branch)
    out_rows = (tokens.astype(F32) + branch).astype(BF16)
    grad_out_rows = rows_line_first(g_out)

    grad_rows, accs, sums = [], None, None
    kept = (gate, val, z, y, gno, *shared)
    for q in range(seqs):
        low_a, low_b, *rest = run_backward(
            q, lengths, xs[q], wt, chan, bcc, headc, kept, squares[q], stats[q], inner_all
        )
        gin, here = rest[:4], rest[4:]
        accs = here if accs is None else [a + b for a, b in zip(accs, here)]
        grad_rows.append(reduce_pieces(gin))
        here = normed[q * SEQ_LEN : (q + 1) * SEQ_LEN]
        part_b = over_rows(here, low_b)
        part_a = over_rows(here, low_a)
        if sums is None:
            sums = lax.optimization_barrier((part_a, part_b))
        else:
            part_b = sums[1] + part_b
            part_a = sums[0] + part_a
            sums = (part_a, part_b)
    valid = (jnp.arange(SEQ_LEN)[None] < lengths[:, None]).reshape(rows)[:, None]
    grad_rows = jnp.concatenate(grad_rows, 0) + jnp.where(valid, grad_out.astype(F32), 0.0)

    chan_acc, bc_acc, head_acc, norm_acc = accs
    cut = sums[0].shape[1]
    column = jnp.arange(sums[1].shape[1]) == base + heads - cut
    norm_column = jnp.sum(norm_acc, 0)[:, None]
    sum_b = jnp.where(column[None], norm_column, sums[1])
    grads = jnp.concatenate([rows_pair_first(sums[0]), rows_line_first(sum_b)], 1)
    rest = grads[:, 2 * inner :].reshape(tensor_count, -1, states2 + HALF)
    rest = reduce_pieces([take(rest, tensor ^ i, 0) for i in range(4)], F32)
    sizes = [5 * inner, inner, inner, 2 * heads, 5 * states2]
    flat = jnp.concatenate(
        [
            jnp.sum(chan_acc, -1).reshape(-1),
            jnp.sum(gain_acc, -1),
            jnp.sum(head_acc, -1).reshape(-1),
            jnp.sum(bc_acc, -1).reshape(-1),
        ]
    )
    if lax.axis_size("dp") == 8:
        flat = direct_sum(flat, "dp", (1,))
        flat = direct_sum(flat, "dp", (2, 4, 6))
    else:
        flat = exchange_sum(flat, "dp")
    cuts = [sum(sizes[: i + 1]) for i in range(4)]
    g_conv, g_skip, g_gain, g_head, g_conv_bc = jnp.split(flat, cuts)
    g_conv_bc = direct_sum(g_conv_bc, "tensor", (1, 2, 3))
    return (
        out_rows,
        grad_rows,
        rest[:, states2 + heads],
        grads[:, :inner],
        grads[:, inner : 2 * inner],
        rest[:, :states2],
        grads[:, base : base + heads],
        g_conv.reshape(5, inner),
        g_conv_bc.reshape(5, states2),
        g_head[:heads],
        g_head[heads:] * -jnp.exp(a_log),
        jnp.sum(g_skip.reshape(heads, -1), -1),
        g_gain,
        grad_out_rows,
    )


def solution(mesh):
    return mapped(mesh)


def mapped(mesh):
    both = ("dp", "tensor")
    return jax.shard_map(
        per_device,
        mesh=mesh,
        in_specs=(
            P("dp", "tensor"),
            P("dp"),
            P("dp", "tensor"),
            P("dp"),
            P("dp", "tensor"),
            P("dp", "tensor"),
            P("dp", None),
            P("dp", "tensor"),
            P(None, "tensor"),
            P(),
            P("tensor"),
            P("tensor"),
            P("tensor"),
            P("tensor"),
            P("dp", "tensor"),
        ),
        out_specs=(
            P("dp", "tensor"),
            P("dp", "tensor"),
            P(both),
            P("dp", "tensor"),
            P("dp", "tensor"),
            P(both, None),
            P("dp", "tensor"),
            P(None, "tensor"),
            P(),
            P("tensor"),
            P("tensor"),
            P("tensor"),
            P("tensor"),
            P("dp", "tensor"),
        ),
        check_vma=False,
    )
```

```python
import functools

import jax
import jax.numpy as jnp
from jax import lax
from jax.experimental import pallas as pl
from jax.experimental.pallas import tpu as pltpu
from jax.sharding import PartitionSpec as P


SEQ_LEN = 2048
Q = 256
HALF = 128
F32 = jnp.float32
BF16 = jnp.bfloat16
epsilon = 1e-05
NEG = -1e30
LOG2E = 1.4426950408889634


def nn(a, b):
    return lax.dot_general(a, b, (((1,), (0,)), ((), ())), preferred_element_type=F32)


def nt(a, b):
    return lax.dot_general(a, b, (((1,), (1,)), ((), ())), preferred_element_type=F32)


def split3(a):
    high = a.astype(BF16)
    rest = a - high.astype(F32)
    mid = rest.astype(BF16)
    low = (rest - mid.astype(F32)).astype(BF16)
    return high, mid, low


def times_ones(a, ones):
    rows = a.shape[0]
    got = nn(jnp.concatenate(split3(a), 0), ones)
    return got[:rows] + got[rows : 2 * rows] + got[2 * rows :]


def twice(a):
    return jnp.concatenate([a, a], 1)


def fold(a):
    return a[:, :HALF] + a[:, HALF:]


def triangle(keep):
    row = lax.broadcasted_iota(jnp.int32, (Q, Q), 0)
    col = lax.broadcasted_iota(jnp.int32, (Q, Q), 1)
    return jnp.where(keep(row, col), 1.0, 0.0).astype(BF16)


def conv(raw, tail, taps):
    ext = jnp.concatenate([tail, raw], 1)
    total = twice(taps[4]) + twice(taps[3]) * raw
    for k in range(1, 4):
        total = total + twice(taps[3 - k]) * pltpu.roll(ext, k, 1)[:, HALF:]
    return total


def conv_back(grad, head, taps):
    ext = jnp.concatenate([grad, head], 1)
    shifted = [grad] + [pltpu.roll(ext, 3 * HALF - k, 1)[:, :Q] for k in range(1, 4)]
    total = twice(taps[3]) * grad
    for k in range(1, 4):
        total = total + twice(taps[3 - k]) * shifted[k]
    return total, shifted


def decay_blocks(run_row, run_col, upper):
    early, late = run_row[:, :HALF], run_row[:, HALF:]
    col_early = jnp.broadcast_to(run_col[:HALF], (HALF, HALF))
    col_late = jnp.broadcast_to(run_col[HALF:], (HALF, HALF))
    first = jnp.exp2(jnp.where(upper, early - col_early, NEG))
    cross = jnp.exp2(late - col_early)
    second = jnp.exp2(jnp.where(upper, late - col_late, NEG))
    return first, cross, second


def stack_blocks(first, cross, second):
    zero = jnp.zeros((HALF, HALF), first.dtype)
    return jnp.concatenate(
        [jnp.concatenate([first, cross], 1), jnp.concatenate([zero, second], 1)], 0
    )


def intersection(b_rows, c_rows):
    b_time = jnp.transpose(b_rows)
    b_high = b_time.astype(BF16)
    b_low = (b_time - b_high.astype(F32)).astype(BF16)
    c_high = c_rows.astype(BF16)
    c_low = (c_rows - c_high.astype(F32)).astype(BF16)
    full = nn(
        jnp.concatenate([b_high, b_low, b_high], 1), jnp.concatenate([c_high, c_high, c_low], 0)
    )
    return (full[:HALF, :HALF], full[:HALF, HALF:], full[HALF:, HALF:]), b_high


def rms_scale(xs, width):
    total = xs[0] * xs[0]
    for x in xs[1:]:
        total = total + x * x
    return lax.rsqrt(jnp.sum(total, -1, keepdims=True) / width + epsilon)


def gain_row(wt_ref, base, heads):
    return wt_ref[base : base + 16, :].astype(F32)[heads : heads + 1]


def softplus(a):
    return jnp.maximum(a, 0.0) + jnp.log1p(jnp.exp(-jnp.abs(a)))


def upper_half():
    row = lax.broadcasted_iota(jnp.int32, (HALF, HALF), 0)
    return row <= lax.broadcasted_iota(jnp.int32, (HALF, HALF), 1)


def valid_row(block, length):
    pos = block * Q + lax.broadcasted_iota(jnp.int32, (1, Q), 1)
    return jnp.where(pos < length, 1.0, 0.0)


def forward_kernel(len_ref, *refs, seq, inner, heads, width, aliased):
    x_refs, (wt_ref, chan_ref, bcc_ref, headc_ref) = refs[:4], refs[4:8]
    refs = refs[8 + aliased :]
    (norm_ref, gate_ref, val_ref, z_ref, y_ref, m_ref, bc_ref, bcz_ref) = refs[:8]
    (step_ref, run_ref, state_ref, stat_ref, proj, vtail, btail, state, carried, wdec) = refs[8:]
    block = pl.program_id(0)
    length = len_ref[seq]
    per = inner // heads
    part = width // 4
    states = bc_ref.shape[0] // 2

    @pl.when(block == 0)
    def _():
        vtail[...] = jnp.zeros_like(vtail)
        btail[...] = jnp.zeros_like(btail)
        state[...] = jnp.zeros_like(state)

    @pl.when(block * Q >= length)
    def _():
        norm_ref[...] = jnp.zeros_like(norm_ref)
        stat_ref[...] = jnp.zeros_like(stat_ref)

    @pl.when(block * Q < length)
    def _():
        base = 2 * inner + 2 * states
        gain = gain_row(wt_ref, base, heads)
        xs = [ref[...].astype(F32) for ref in x_refs]
        inv = rms_scale(xs, width)
        for k in range(4):
            cols = slice(k * part, (k + 1) * part)
            norm_ref[:, cols] = (xs[k] * inv * gain[:, cols]).astype(BF16)
        proj[...] = nt(wt_ref[: base + 16, :], norm_ref[...])

        raw = proj[2 * inner : base, :]
        bc_ref[...] = raw
        bcz = conv(raw, btail[...], [bcc_ref[j] for j in range(5)])
        btail[...] = raw[:, HALF:]
        bcz_ref[...] = bcz
        shared = bcz * jax.nn.sigmoid(bcz)
        b_rows, c_rows = shared[:states], shared[states:]
        cb_blocks, b_time = intersection(b_rows, c_rows)
        c_low = c_rows.astype(BF16)

        step_raw = proj[base : base + heads, :] + twice(headc_ref[0])
        step_ref[...] = step_raw
        steps = softplus(step_raw)
        running = times_ones(
            steps * (twice(headc_ref[1]) * LOG2E), triangle(lambda s, t: s <= t)
        )
        run_ref[...] = running
        run_cols = jnp.transpose(running)
        ends = running[:, Q - 1 :]
        grow = jnp.exp2(running)
        to_end = jnp.exp2(ends - running)
        whole = jnp.exp2(ends)
        upper = upper_half()

        state_ref[...] = state[...]
        carried[...] = nn(state[...].astype(BF16), c_low)
        squares = jnp.zeros((1, Q), F32)
        for h in range(heads):
            rows = slice(h * per, (h + 1) * per)
            raw_v = proj[inner + h * per : inner + (h + 1) * per, :]
            gate = proj[rows, :]
            val_ref[rows, :] = raw_v
            gate_ref[rows, :] = gate
            z = conv(raw_v, vtail[rows, :], [chan_ref[j, rows, :] for j in range(5)])
            vtail[rows, :] = raw_v[:, HALF:]
            z_ref[rows, :] = z
            v = z * jax.nn.sigmoid(z)
            w = v * steps[h : h + 1]
            decays = decay_blocks(running[h : h + 1], run_cols[:, h : h + 1], upper)
            grid = stack_blocks(*[(d * g).astype(BF16) for d, g in zip(decays, cb_blocks)])
            y = nn(w.astype(BF16), grid) + carried[rows, :] * grow[h : h + 1]
            y_ref[rows, :] = y
            wdec[rows, :] = (w * to_end[h : h + 1]).astype(BF16)
            u = y + twice(chan_ref[6, rows, :]) * v
            m = u * gate * jax.nn.sigmoid(gate)
            m_ref[rows, :] = m
            squares = squares + jnp.sum(m * m, 0, keepdims=True)
        stat_ref[...] = squares
        fresh = nn(wdec[...], b_time)
        for h in range(heads):
            rows = slice(h * per, (h + 1) * per)
            state[rows, :] = state[rows, :] * whole[h : h + 1] + fresh[rows]


def middle_kernel(len_ref, *refs, seq, inner, inner_all, width, aliased):
    c0, c1, c2, c3, wo_ref, chan_ref, m_ref, sq_ref = refs[:8]
    nout_ref, gno_ref, b0, b1, b2, b3, stat_ref, gain_acc, nout = refs[8 + aliased :]
    block = pl.program_id(0)
    length = len_ref[seq]
    part = width // 4

    @pl.when(block == 0)
    def _():
        gain_acc[...] = jnp.zeros_like(gain_acc)

    @pl.when(block * Q >= length)
    def _():
        nout_ref[...] = jnp.zeros_like(nout_ref)
        stat_ref[...] = jnp.zeros_like(stat_ref)
        for ref in (b0, b1, b2, b3):
            ref[...] = jnp.zeros_like(ref)

    @pl.when(block * Q < length)
    def _():
        valid = valid_row(block, length)
        scale = lax.rsqrt(sq_ref[...] / inner_all + epsilon) * valid
        cot = jnp.concatenate([ref[...] for ref in (c0, c1, c2, c3)], 1)
        gno_ref[...] = nt(wo_ref[...], cot) * valid
        inners = jnp.zeros((1, Q), F32)
        for lo in range(0, inner, 64):
            rows = slice(lo, lo + 64)
            gain = twice(chan_ref[5, rows, :])
            m = m_ref[rows, :]
            gno = gno_ref[rows, :]
            nout[rows, :] = (m * scale * gain).astype(BF16)
            inners = inners + jnp.sum(gno * gain * m, 0, keepdims=True)
            gain_acc[rows, :] += fold(gno * m * scale)
        stat_ref[...] = inners
        nout_time = jnp.transpose(nout[...])
        nout_ref[...] = nout_time
        branch = nn(nout_time, wo_ref[...])
        for k, ref in enumerate((b0, b1, b2, b3)):
            ref[...] = branch[:, k * part : (k + 1) * part].astype(BF16)


def backward_kernel(len_ref, *refs, seq, inner, inner_all, heads, width, blocks, aliased):
    x_refs, (wt_ref, chan_ref, bcc_ref, headc_ref) = refs[:4], refs[4:8]
    (gate_ref, val_ref, z_ref, y_ref, gno_ref, bc_ref, bcz_ref) = refs[8:15]
    (step_ref, run_ref, state_ref, sq_ref, stat_ref) = refs[15:20]
    refs = refs[:20] + refs[20 + aliased :]
    low_refs, g_refs, (chan_acc, bc_acc, head_acc, norm_acc) = refs[20:22], refs[22:26], refs[26:30]
    low, gstate, vhead, bhead, dcb, wdec, gudec, sent = refs[30:]
    step = pl.program_id(0)
    block = blocks - 1 - step
    length = len_ref[seq]
    per = inner // heads
    part = width // 4
    states = bc_ref.shape[0] // 2
    base = 2 * inner + 2 * states

    @pl.when(step == 0)
    def _():
        chan_acc[...] = jnp.zeros_like(chan_acc)
        bc_acc[...] = jnp.zeros_like(bc_acc)
        head_acc[...] = jnp.zeros_like(head_acc)
        norm_acc[...] = jnp.zeros_like(norm_acc)
        low[base:, :] = jnp.zeros_like(low[base:, :])
        gstate[...] = jnp.zeros_like(gstate)
        vhead[...] = jnp.zeros_like(vhead)
        bhead[...] = jnp.zeros_like(bhead)

    @pl.when(block * Q >= length)
    def _():
        for ref in (*low_refs, *g_refs):
            ref[...] = jnp.zeros_like(ref)

    @pl.when(block * Q < length)
    def _():
        inv_gate = lax.rsqrt(sq_ref[...] / inner_all + epsilon)
        pull = inv_gate * inv_gate * inv_gate * stat_ref[...] / inner_all

        bcz = bcz_ref[...]
        sig = jax.nn.sigmoid(bcz)
        shared = bcz * sig
        shared_slope = sig + shared * (1.0 - sig)
        b_rows, c_rows = shared[:states], shared[states:]
        cb_blocks, _ = intersection(b_rows, c_rows)
        b_low, c_low = b_rows.astype(BF16), c_rows.astype(BF16)

        step_raw = step_ref[...]
        steps = softplus(step_raw)
        running = run_ref[...]
        run_cols = jnp.transpose(running)
        ends = running[:, Q - 1 :]
        grow = jnp.exp2(running)
        to_end = jnp.exp2(ends - running)
        whole = jnp.exp2(ends)
        upper = upper_half()

        sent[...] = nn(gstate[...].astype(BF16), b_low)
        direct, both, after, through = [], [], [], []
        for h in range(heads):
            rows = slice(h * per, (h + 1) * per)
            gate, z, y, gno = gate_ref[rows, :], z_ref[rows, :], y_ref[rows, :], gno_ref[rows, :]
            gain = twice(chan_ref[5, rows, :])
            skip = twice(chan_ref[6, rows, :])
            sig_g = jax.nn.sigmoid(gate)
            silu_g = gate * sig_g
            sig_z = jax.nn.sigmoid(z)
            v = z * sig_z
            u = y + skip * v
            m = u * silu_g
            gm = inv_gate * gain * gno - m * pull
            low[rows, :] = (gm * u * (sig_g + silu_g * (1.0 - sig_g))).astype(BF16)
            gu = gm * silu_g
            chan_acc[5, rows, :] += fold(gu * v)
            w = v * steps[h : h + 1]
            w_low, gu_low = w.astype(BF16), gu.astype(BF16)
            decays = decay_blocks(running[h : h + 1], run_cols[:, h : h + 1], upper)
            grid = stack_blocks(*[(d * g).astype(BF16) for d, g in zip(decays, cb_blocks)])
            gw_in = nt(gu_low, grid)
            pair = nn(jnp.transpose(w_low), gu_low)
            pieces = (pair[:HALF, :HALF], pair[:HALF, HALF:], pair[HALF:, HALF:])
            for i in range(3):
                if h == 0:
                    dcb[i] = decays[i] * pieces[i]
                else:
                    dcb[i] += decays[i] * pieces[i]
            gs = gstate[rows, :]
            gw_out = sent[rows, :] * to_end[h : h + 1]
            gw = gw_in + gw_out
            direct.append(jnp.sum(gw * v, 0, keepdims=True))
            both.append(
                jnp.sum(gu_low.astype(F32) * y - gw_in * w_low.astype(F32), 0, keepdims=True)
            )
            after.append(jnp.sum(gw_out * w, 0, keepdims=True))
            through.append(
                jnp.sum(gs * state_ref[rows, :], 0, keepdims=True) * whole[h : h + 1]
            )
            gud = (gu * grow[h : h + 1]).astype(BF16)
            gudec[rows, :] = gud
            wdec[rows, :] = (w * to_end[h : h + 1]).astype(BF16)
            gz = (skip * gu + gw * steps[h : h + 1]) * (sig_z + v * (1.0 - sig_z))
            taps = [chan_ref[j, rows, :] for j in range(4)]
            gv, shifted = conv_back(gz, vhead[rows, :], taps)
            vhead[rows, :] = gz[:, :HALF]
            raw_v = val_ref[rows, :]
            for k in range(4):
                chan_acc[3 - k, rows, :] += fold(shifted[k] * raw_v)
            chan_acc[4, rows, :] += fold(gz)
            low[inner + h * per : inner + (h + 1) * per, :] = gv.astype(BF16)

        direct = jnp.concatenate(direct, 0)
        both = jnp.concatenate(both, 0)
        after = jnp.concatenate(after, 0)
        through = jnp.sum(jnp.concatenate(through, 0), -1, keepdims=True)
        g_decay = (
            times_ones(both, triangle(lambda t, r: t >= r))
            + times_ones(after, triangle(lambda s, r: s < r))
            + through
        )
        head_acc[1] += fold(steps * g_decay)
        g_step = (direct + twice(headc_ref[1]) * g_decay) * jax.nn.sigmoid(step_raw)
        head_acc[0] += fold(g_step)
        low[base : base + 16, :] = jnp.concatenate(
            [g_step, jnp.zeros((16 - heads, Q), F32)], 0
        ).astype(BF16)

        dcb_low = stack_blocks(*[dcb[i].astype(BF16) for i in range(3)])
        gud, wd = gudec[...], wdec[...]
        gs_old = gstate[...]
        g_c = nn(b_low, dcb_low) + nn(jnp.transpose(state_ref[...]).astype(BF16), gud)
        g_b = nt(c_low, dcb_low) + nn(jnp.transpose(gs_old).astype(BF16), wd)
        fresh = nn(gud, jnp.transpose(c_low))
        for h in range(heads):
            rows = slice(h * per, (h + 1) * per)
            gstate[rows, :] = gs_old[rows] * whole[h : h + 1] + fresh[rows]
        gbcz = jnp.concatenate([g_b, g_c], 0) * shared_slope
        gbc, shifted = conv_back(gbcz, bhead[...], [bcc_ref[j] for j in range(4)])
        bhead[...] = gbcz[:, :HALF]
        raw = bc_ref[...]
        for k in range(4):
            bc_acc[3 - k] += fold(shifted[k] * raw)
        bc_acc[4] += fold(gbcz)
        low[2 * inner : base, :] = gbc.astype(BF16)

        lows = jnp.transpose(low[...])
        cut = low_refs[0].shape[1]
        low_refs[0][...] = lows[:, :cut]
        low_refs[1][...] = lows[:, cut:]
        g_norm = nn(lows, wt_ref[...])
        gain = gain_row(wt_ref, base, heads)
        xs = [ref[...].astype(F32) for ref in x_refs]
        inv = rms_scale(xs, width)
        prod = None
        for k in range(4):
            cols = slice(k * part, (k + 1) * part)
            here = g_norm[:, cols] * xs[k]
            norm_acc[:, cols] += jnp.sum((here * inv).reshape(Q // 8, 8, part), 0)
            weighted = here * gain[:, cols]
            prod = weighted if prod is None else prod + weighted
        pull_x = inv * inv * inv * (jnp.sum(prod, -1, keepdims=True) / width)
        for k in range(4):
            cols = slice(k * part, (k + 1) * part)
            g_refs[k][...] = (inv * gain[:, cols] * g_norm[:, cols] - xs[k] * pull_x).astype(BF16)


def shape(dims, kind=F32):
    return jax.ShapeDtypeStruct(dims, kind)


def params(count):
    return pltpu.CompilerParams(
        dimension_semantics=("arbitrary",) * count, vmem_limit_bytes=52 << 20
    )


def fixed(array):
    rank = array.ndim
    return pl.BlockSpec(array.shape, lambda *_: (0,) * rank, pipeline_mode=pl.Buffered(1))


def run_forward(seq, seqs, lengths, xs, wt, chan, bcc, headc, before):
    part = xs[0].shape[1]
    width = 4 * part
    inner, heads, states2 = chan.shape[1], headc.shape[1], bcc.shape[1]
    blocks = SEQ_LEN // Q
    rows = seqs * SEQ_LEN
    at = lambda c: seq * blocks + c
    col = lambda n: pl.BlockSpec((n, Q), lambda c, lens: (0, at(c)))
    out_shape = [
        shape((rows, width), BF16),
        *[shape((inner, rows))] * 5,
        *[shape((states2, rows))] * 2,
        *[shape((heads, rows))] * 2,
        shape((seqs * blocks * inner, states2 // 2)),
        shape((1, SEQ_LEN)),
    ]
    out_specs = [
        pl.BlockSpec((Q, width), lambda c, lens: (at(c), 0)),
        *[col(inner)] * 5,
        *[col(states2)] * 2,
        *[col(heads)] * 2,
        pl.BlockSpec((inner, states2 // 2), lambda c, lens: (at(c), 0)),
        pl.BlockSpec((1, Q), lambda c, lens: (0, c)),
    ]
    consts = (wt, chan, bcc, headc)
    return pl.pallas_call(
        functools.partial(
            forward_kernel,
            seq=seq,
            inner=inner,
            heads=heads,
            width=width,
            aliased=len(before),
        ),
        out_shape=out_shape,
        grid_spec=pltpu.PrefetchScalarGridSpec(
            num_scalar_prefetch=1,
            grid=(blocks,),
            in_specs=[
                *[pl.BlockSpec((Q, part), lambda c, lens: (c, 0))] * 4,
                *[fixed(array) for array in consts],
                *[pl.BlockSpec(memory_space=pl.ANY)] * len(before),
            ],
            out_specs=out_specs,
            scratch_shapes=[
                pltpu.VMEM((2 * inner + states2 + 16, Q), F32),
                pltpu.VMEM((inner, HALF), F32),
                pltpu.VMEM((states2, HALF), F32),
                pltpu.VMEM((inner, states2 // 2), F32),
                pltpu.VMEM((inner, Q), F32),
                pltpu.VMEM((inner, Q), BF16),
            ],
        ),
        input_output_aliases={9 + i: i for i in range(len(before))},
        compiler_params=params(1),
        name="mixer_forward",
    )(lengths, *xs, *consts, *before)


def run_middle(seq, lengths, cots, wo, chan, m, squares, inner_all, before):
    rows, part = cots[0].shape
    width = 4 * part
    inner = wo.shape[0]
    blocks = SEQ_LEN // Q
    at = lambda c: seq * blocks + c
    piece = pl.BlockSpec((Q, part), lambda c, lens: (at(c), 0))
    col = pl.BlockSpec((inner, Q), lambda c, lens: (0, at(c)))
    stat = pl.BlockSpec((1, Q), lambda c, lens: (0, c))
    return pl.pallas_call(
        functools.partial(
            middle_kernel,
            seq=seq,
            inner=inner,
            inner_all=inner_all,
            width=width,
            aliased=len(before),
        ),
        out_shape=[
            shape((rows, inner), BF16),
            shape((inner, rows)),
            *[shape((SEQ_LEN, part), BF16)] * 4,
            shape((1, SEQ_LEN)),
            shape((inner, HALF)),
        ],
        grid_spec=pltpu.PrefetchScalarGridSpec(
            num_scalar_prefetch=1,
            grid=(blocks,),
            in_specs=[
                *[piece] * 4,
                fixed(wo),
                fixed(chan),
                col,
                stat,
                *[pl.BlockSpec(memory_space=pl.ANY)] * len(before),
            ],
            out_specs=[
                pl.BlockSpec((Q, inner), lambda c, lens: (at(c), 0)),
                col,
                *[pl.BlockSpec((Q, part), lambda c, lens: (c, 0))] * 4,
                stat,
                pl.BlockSpec((inner, HALF), lambda c, lens: (0, 0)),
            ],
            scratch_shapes=[pltpu.VMEM((inner, Q), BF16)],
        ),
        input_output_aliases={9 + i: i for i in range(len(before))},
        compiler_params=params(1),
        name="mixer_middle",
    )(lengths, *cots, wo, chan, m, squares, *before)


def run_backward(
    seq, lengths, xs, wt, chan, bcc, headc, saved, squares, stat, inner_all, before
):
    part = xs[0].shape[1]
    width = 4 * part
    inner, heads, states2 = chan.shape[1], headc.shape[1], bcc.shape[1]
    blocks = SEQ_LEN // Q
    back = lambda c: blocks - 1 - c
    at = lambda c: seq * blocks + back(c)
    col = lambda n: pl.BlockSpec((n, Q), lambda c, lens: (0, at(c)))
    piece = pl.BlockSpec((Q, part), lambda c, lens: (back(c), 0))
    consts = (wt, chan, bcc, headc)
    cut = inner + inner // 2
    sets = (cut, wt.shape[0] - cut)
    accs = [(6, inner, HALF), (5, states2, HALF), (2, heads, HALF), (8, width)]
    keep = lambda dims: pl.BlockSpec(dims, lambda c, lens: (0,) * len(dims))
    return pl.pallas_call(
        functools.partial(
            backward_kernel,
            seq=seq,
            inner=inner,
            inner_all=inner_all,
            heads=heads,
            width=width,
            blocks=blocks,
            aliased=len(before),
        ),
        out_shape=[
            *[shape((saved[0].shape[1], count), BF16) for count in sets],
            *[shape((SEQ_LEN, part), BF16)] * 4,
            *[shape(dims) for dims in accs],
        ],
        grid_spec=pltpu.PrefetchScalarGridSpec(
            num_scalar_prefetch=1,
            grid=(blocks,),
            in_specs=[
                *[piece] * 4,
                *[fixed(array) for array in consts],
                *[col(inner)] * 5,
                *[col(states2)] * 2,
                *[col(heads)] * 2,
                pl.BlockSpec((inner, states2 // 2), lambda c, lens: (at(c), 0)),
                *[pl.BlockSpec((1, Q), lambda c, lens: (0, back(c)))] * 2,
                *[pl.BlockSpec(memory_space=pl.ANY)] * len(before),
            ],
            out_specs=[
                *[pl.BlockSpec((Q, count), lambda c, lens: (at(c), 0)) for count in sets],
                *[piece] * 4,
                *[keep(dims) for dims in accs],
            ],
            scratch_shapes=[
                pltpu.VMEM((wt.shape[0], Q), BF16),
                pltpu.VMEM((inner, states2 // 2), F32),
                pltpu.VMEM((inner, HALF), F32),
                pltpu.VMEM((states2, HALF), F32),
                pltpu.VMEM((3, HALF, HALF), F32),
                pltpu.VMEM((inner, Q), BF16),
                pltpu.VMEM((inner, Q), BF16),
                pltpu.VMEM((inner, Q), F32),
            ],
        ),
        input_output_aliases={21 + i: i for i in range(len(before))},
        compiler_params=params(1),
        name="mixer_backward",
    )(lengths, *xs, *consts, *saved, squares, stat, *before)


def exchange(a, axis, bit):
    return lax.ppermute(a, axis, [(i, i ^ bit) for i in range(lax.axis_size(axis))])


def exchange_sum(a, axis):
    bit = 1
    while bit < lax.axis_size(axis):
        a = a + exchange(a, axis, bit)
        bit *= 2
    return a


def gather_pieces(a):
    across = exchange(a, "tensor", 2)
    beside = exchange(a, "tensor", 1)
    return a, beside, across, exchange(across, "tensor", 1)


def reduce_pieces(pieces, kind=BF16):
    own, beside, across, corner = pieces
    got_corner = exchange(corner.astype(kind), "tensor", 1)
    got_beside = exchange(beside.astype(kind), "tensor", 1)
    onward = (across.astype(F32) + got_corner.astype(F32)).astype(kind)
    last = exchange(onward, "tensor", 2).astype(F32)
    return own.astype(F32) + got_beside.astype(F32) + last


def place():
    index = lax.axis_index("dp")
    return index // 2, index % 2


def take(a, index, dim):
    return lax.dynamic_index_in_dim(a, index, dim, keepdims=False)


def round_to(count, tile):
    return count // tile * tile


def side_by_side(pick, extra):
    _, x = place()
    out = []
    for m in range(4):
        mine, other = pick(m)
        zero = [jnp.zeros((extra, mine.shape[1]), BF16)] if extra else []
        for side in (0, 1):
            out.append(jnp.concatenate([jnp.where(x == side, mine, other)] + zero, 0))
    return jnp.concatenate(out, 1)


def gather_other_way(a):
    tensor = lax.axis_index("tensor")
    whole = jnp.transpose(lax.all_gather(jnp.transpose(a), "dp", axis=0, tiled=True))
    blocks = whole.reshape(a.shape[0], 4, -1)
    return jnp.concatenate([take(blocks, tensor ^ m, 1) for m in range(4)], 1)


ROUNDS = ((3, 2, 1), (1, 3, 2))


def exchange_z(a, turn):
    count, tensor_count = lax.axis_size("dp"), lax.axis_size("tensor")
    pairs = [
        (d * tensor_count + t, (d ^ (2 * ROUNDS[t % 2][turn])) * tensor_count + t)
        for d in range(count)
        for t in range(tensor_count)
    ]
    return lax.ppermute(a, ("dp", "tensor"), pairs)


def even_core():
    return lax.axis_index("tensor") % 2 == 0


def distance(turn):
    return jnp.where(even_core(), ROUNDS[0][turn], ROUNDS[1][turn])


def z_stack(a):
    return jnp.stack([a] + [exchange_z(a, turn) for turn in range(3)])


def slot_of(m):
    z, _ = place()
    j = (lax.axis_index("tensor") ^ m) ^ z
    return jnp.where(even_core(), (4 - j) % 4, jnp.where(j >= 2, 5 - j, j))


def weight_columns(a, extra, ready):
    if lax.axis_size("dp") != 8:
        return jnp.pad(gather_other_way(a), ((0, extra), (0, 0))), ready
    cut = round_to(a.shape[0] * 6 // 10, 16)
    first, second = a[:cut], a[cut:]
    beside = exchange(second, "dp", 1)
    beside, ready = lax.optimization_barrier((beside, ready))
    mine = z_stack(first)
    other = exchange(first, "dp", 1)
    pair = jnp.stack([second, beside])
    both = z_stack(pair)
    other = jnp.concatenate([other[None], exchange(mine[1:], "dp", 1)], 0)

    def pick(m):
        slot = slot_of(m)
        low = take(both, slot, 0)
        return (
            jnp.concatenate([take(mine, slot, 0), low[0]], 0),
            jnp.concatenate([take(other, slot, 0), low[1]], 0),
        )

    return side_by_side(pick, extra), ready


def hidden_columns(a):
    if lax.axis_size("dp") != 8:
        return gather_other_way(a)
    both = z_stack(jnp.stack([a, exchange(a, "dp", 1)]))

    def pick(m):
        low = take(both, slot_of(m), 0)
        return low[0], low[1]

    return side_by_side(pick, 0)


def along_z(pick):
    z, _ = place()
    total = pick(z)
    for turn in range(3):
        send = pick(z ^ distance(turn)).astype(BF16)
        total = total + exchange_z(send, turn).astype(F32)
    return total


def reduce_other_way(a):
    tensor = lax.axis_index("tensor")
    blocks = a.reshape(4, -1, a.shape[1])
    ordered = jnp.concatenate([take(blocks, tensor ^ m, 0) for m in range(4)], 0)
    return lax.psum_scatter(ordered, "dp", scatter_dimension=0, tiled=True)


def rows_pair_first(a):
    if lax.axis_size("dp") != 8:
        return reduce_other_way(a)
    tensor = lax.axis_index("tensor")
    _, x = place()
    blocks = a.reshape(4, 2, a.shape[0] // 8, a.shape[1])
    got = exchange(take(blocks, 1 - x, 1).astype(BF16), "dp", 1).astype(F32)
    halves = take(blocks, x, 1) + got
    return along_z(lambda z: take(halves, z ^ tensor, 0))


def rows_line_first(a):
    if lax.axis_size("dp") != 8:
        return reduce_other_way(a)
    tensor = lax.axis_index("tensor")
    _, x = place()
    blocks = a.reshape(4, 2, a.shape[0] // 8, a.shape[1])
    pairs = along_z(lambda z: take(blocks, z ^ tensor, 0))
    late = exchange(take(pairs, 1 - x, 0).astype(BF16), "dp", 1).astype(F32)
    return take(pairs, x, 0) + late


def direct_sum(a, axis, bits):
    total = a
    for bit in bits:
        total = total + exchange(a, axis, bit)
    return total


def over_rows(left, right):
    return lax.dot_general(
        left, right, (((0,), (0,)), ((), ())), preferred_element_type=F32
    )


def lanes(a):
    return jnp.broadcast_to(a[..., None], a.shape + (HALF,))


def small_constants(conv_x, conv_bc, dt_bias, a_log, skip_d, gate_gain):
    per = conv_x.shape[1] // skip_d.shape[0]
    chan = lanes(jnp.concatenate([conv_x, gate_gain[None], jnp.repeat(skip_d, per)[None]], 0))
    return chan, lanes(conv_bc), lanes(jnp.stack([dt_bias, -jnp.exp(a_log)], 0))


def per_device(
    tokens,
    lengths,
    grad_out,
    norm_gain,
    w_gate,
    w_value,
    w_bc,
    w_dt,
    conv_x,
    conv_bc,
    dt_bias,
    a_log,
    skip_d,
    gate_gain,
    w_out,
):
    tensor_count = lax.axis_size("tensor")
    tensor = lax.axis_index("tensor")
    rows, part = tokens.shape
    seqs = rows // SEQ_LEN
    inner = w_gate.shape[1]
    inner_all = inner * tensor_count
    heads = w_dt.shape[1]
    states2 = w_bc.shape[1]
    base = 2 * inner + states2

    local = jnp.concatenate(
        [
            w_gate,
            w_value,
            w_bc,
            w_dt,
            norm_gain[:, None],
            jnp.zeros((w_gate.shape[0], 15 - heads), BF16),
        ],
        1,
    )
    xs = [gather_pieces(tokens[q * SEQ_LEN : (q + 1) * SEQ_LEN]) for q in range(seqs)]
    cots = gather_pieces(grad_out)
    ready = small_constants(conv_x, conv_bc, dt_bias, a_log, skip_d, gate_gain)
    wt, (turned, *ready) = weight_columns(
        jnp.transpose(local), HALF - 16, (jnp.transpose(w_out), *ready)
    )
    wo = hidden_columns(turned)
    chan, bcc, headc = ready

    saved, squares = [], []
    for q in range(seqs):
        *saved, here = run_forward(q, seqs, lengths, xs[q], wt, chan, bcc, headc, saved)
        squares.append(direct_sum(here, "tensor", (1, 2, 3)))
    normed, gate, val, z, y, m, *shared = saved
    middle, stats, gain_acc, out_rows = [], [], None, []
    for q in range(seqs):
        *middle, stat, here = run_middle(
            q, lengths, cots, wo, chan, m, squares[q], inner_all, middle
        )
        middle, branch = middle[:2], middle[2:]
        stats.append(direct_sum(stat, "tensor", (1, 2, 3)))
        gain_acc = here if gain_acc is None else gain_acc + here
        out_rows.append(reduce_pieces(branch))
    nout, gno = middle
    g_out = jnp.concatenate([over_rows(cot, nout) for cot in cots], 0)
    grad_out_rows = rows_line_first(g_out)
    out_rows = (tokens.astype(F32) + jnp.concatenate(out_rows, 0)).astype(BF16)

    grad_rows, accs, lows = [], None, []
    kept = (gate, val, z, y, gno, *shared)
    for q in range(seqs):
        *lows, g0, g1, g2, g3, a0, a1, a2, a3 = run_backward(
            q, lengths, xs[q], wt, chan, bcc, headc, kept, squares[q], stats[q], inner_all, lows
        )
        here = (a0, a1, a2, a3)
        accs = here if accs is None else [a + b for a, b in zip(accs, here)]
        grad_rows.append(reduce_pieces((g0, g1, g2, g3)))
    sum_b = over_rows(normed, lows[1])
    sum_a = over_rows(normed, lows[0])
    sums = (sum_a, sum_b)
    valid = (jnp.arange(SEQ_LEN)[None] < lengths[:, None]).reshape(rows)[:, None]
    grad_rows = jnp.concatenate(grad_rows, 0) + jnp.where(valid, grad_out.astype(F32), 0.0)

    chan_acc, bc_acc, head_acc, norm_acc = accs
    grads = jnp.concatenate([rows_pair_first(sums[0]), rows_line_first(sums[1])], 1)
    rest = grads[:, 2 * inner :].reshape(tensor_count, -1, states2 + HALF)
    rest = reduce_pieces([take(rest, tensor ^ i, 0) for i in range(4)], F32)
    norm = jnp.sum(norm_acc, 0).reshape(tensor_count, part)
    norm = jnp.concatenate([take(norm, tensor ^ i, 0) for i in range(tensor_count)])
    sizes = [5 * inner, inner, inner, 2 * heads]
    flat = jnp.concatenate(
        [
            jnp.sum(chan_acc, -1).reshape(-1),
            jnp.sum(gain_acc, -1),
            jnp.sum(head_acc, -1).reshape(-1),
            jnp.sum(bc_acc, -1).reshape(-1),
            norm,
        ]
    )
    if lax.axis_size("dp") == 8:
        flat = direct_sum(flat, "dp", (1,))
        flat = direct_sum(flat, "dp", (2, 4, 6))
    else:
        flat = exchange_sum(flat, "dp")
    cuts = [sum(sizes[: i + 1]) for i in range(4)]
    g_conv, g_skip, g_gain, g_head, everywhere = jnp.split(flat, cuts)
    everywhere = direct_sum(everywhere, "tensor", (1, 2, 3))
    g_conv_bc = everywhere[: 5 * states2]
    share = part // lax.axis_size("dp")
    first = 5 * states2 + (lax.axis_index("dp") * tensor_count + tensor) * share
    g_norm = lax.dynamic_slice_in_dim(everywhere, first, share, 0)
    return (
        out_rows,
        grad_rows,
        g_norm,
        grads[:, :inner],
        grads[:, inner : 2 * inner],
        rest[:, :states2],
        grads[:, base : base + heads],
        g_conv.reshape(5, inner),
        g_conv_bc.reshape(5, states2),
        g_head[:heads],
        g_head[heads:] * -jnp.exp(a_log),
        jnp.sum(g_skip.reshape(heads, -1), -1),
        g_gain,
        grad_out_rows,
    )


def solution(mesh):
    return mapped(mesh)


def mapped(mesh):
    both = ("dp", "tensor")
    return jax.shard_map(
        per_device,
        mesh=mesh,
        in_specs=(
            P("dp", "tensor"),
            P("dp"),
            P("dp", "tensor"),
            P("dp"),
            P("dp", "tensor"),
            P("dp", "tensor"),
            P("dp", None),
            P("dp", "tensor"),
            P(None, "tensor"),
            P(),
            P("tensor"),
            P("tensor"),
            P("tensor"),
            P("tensor"),
            P("dp", "tensor"),
        ),
        out_specs=(
            P("dp", "tensor"),
            P("dp", "tensor"),
            P(both),
            P("dp", "tensor"),
            P("dp", "tensor"),
            P(both, None),
            P("dp", "tensor"),
            P(None, "tensor"),
            P(),
            P("tensor"),
            P("tensor"),
            P("tensor"),
            P("tensor"),
            P("dp", "tensor"),
        ),
        check_vma=False,
    )
```

```python
import functools

import jax
import jax.numpy as jnp
from jax import lax
from jax.experimental import pallas as pl
from jax.experimental.pallas import tpu as pltpu
from jax.sharding import PartitionSpec as P


SEQ_LEN = 2048
Q = 256
HALF = 128
F32 = jnp.float32
BF16 = jnp.bfloat16
epsilon = 1e-05
NEG = -1e30
LOG2E = 1.4426950408889634
TENSOR = "tensor"
DP = "dp"


def nn(a, b):
    return lax.dot_general(a, b, (((1,), (0,)), ((), ())), preferred_element_type=F32)


def nt(a, b):
    return lax.dot_general(a, b, (((1,), (1,)), ((), ())), preferred_element_type=F32)


def split3(a):
    high = a.astype(BF16)
    rest = a - high.astype(F32)
    mid = rest.astype(BF16)
    low = (rest - mid.astype(F32)).astype(BF16)
    return high, mid, low


def times_ones(a, ones):
    rows = a.shape[0]
    got = nn(jnp.concatenate(split3(a), 0), ones)
    return got[:rows] + got[rows : 2 * rows] + got[2 * rows :]


def twice(a):
    return jnp.concatenate([a, a], 1)


def fold(a):
    return a[:, :HALF] + a[:, HALF:]


def triangle(keep):
    row = lax.broadcasted_iota(jnp.int32, (Q, Q), 0)
    col = lax.broadcasted_iota(jnp.int32, (Q, Q), 1)
    return jnp.where(keep(row, col), 1.0, 0.0).astype(BF16)


def conv(raw, tail, taps):
    ext = jnp.concatenate([tail, raw], 1)
    total = twice(taps[4]) + twice(taps[3]) * raw
    for k in range(1, 4):
        total = total + twice(taps[3 - k]) * pltpu.roll(ext, k, 1)[:, HALF:]
    return total


def conv_back(grad, head, taps):
    ext = jnp.concatenate([grad, head], 1)
    shifted = [grad] + [pltpu.roll(ext, 3 * HALF - k, 1)[:, :Q] for k in range(1, 4)]
    total = twice(taps[3]) * grad
    for k in range(1, 4):
        total = total + twice(taps[3 - k]) * shifted[k]
    return total, shifted


def decay_blocks(run_row, run_col, upper):
    early, late = run_row[:, :HALF], run_row[:, HALF:]
    col_early = jnp.broadcast_to(run_col[:HALF], (HALF, HALF))
    col_late = jnp.broadcast_to(run_col[HALF:], (HALF, HALF))
    first = jnp.exp2(jnp.where(upper, early - col_early, NEG))
    cross = jnp.exp2(late - col_early)
    second = jnp.exp2(jnp.where(upper, late - col_late, NEG))
    return first, cross, second


def stack_blocks(first, cross, second):
    zero = jnp.zeros((HALF, HALF), first.dtype)
    return jnp.concatenate(
        [jnp.concatenate([first, cross], 1), jnp.concatenate([zero, second], 1)], 0
    )


def intersection(b_rows, c_rows):
    b_time = jnp.transpose(b_rows)
    b_high = b_time.astype(BF16)
    b_low = (b_time - b_high.astype(F32)).astype(BF16)
    c_high = c_rows.astype(BF16)
    c_low = (c_rows - c_high.astype(F32)).astype(BF16)
    full = nn(
        jnp.concatenate([b_high, b_low, b_high], 1), jnp.concatenate([c_high, c_high, c_low], 0)
    )
    return (full[:HALF, :HALF], full[:HALF, HALF:], full[HALF:, HALF:]), b_high


def rms_scale(xs, width):
    total = xs[0] * xs[0]
    for x in xs[1:]:
        total = total + x * x
    return lax.rsqrt(jnp.sum(total, -1, keepdims=True) / width + epsilon)


def gain_row(wt_ref, base, heads):
    return wt_ref[base : base + 16, :].astype(F32)[heads : heads + 1]


def softplus(a):
    return jnp.maximum(a, 0.0) + jnp.log1p(jnp.exp(-jnp.abs(a)))


def upper_half():
    row = lax.broadcasted_iota(jnp.int32, (HALF, HALF), 0)
    return row <= lax.broadcasted_iota(jnp.int32, (HALF, HALF), 1)


def valid_row(block, length):
    pos = block * Q + lax.broadcasted_iota(jnp.int32, (1, Q), 1)
    return jnp.where(pos < length, 1.0, 0.0)


def forward_kernel(len_ref, *refs, seq, inner, heads, width, aliased):
    x_refs, (wt_ref, chan_ref, bcc_ref, headc_ref) = refs[:4], refs[4:8]
    refs = refs[8 + aliased :]
    (norm_ref, gate_ref, val_ref, z_ref, y_ref, m_ref, bc_ref, bcz_ref) = refs[:8]
    (step_ref, run_ref, state_ref, stat_ref, proj, vtail, btail, state, carried, wdec) = refs[8:]
    block = pl.program_id(0)
    length = len_ref[seq]
    per = inner // heads
    part = width // 4
    states = bc_ref.shape[0] // 2

    @pl.when(block == 0)
    def _():
        vtail[...] = jnp.zeros_like(vtail)
        btail[...] = jnp.zeros_like(btail)
        state[...] = jnp.zeros_like(state)

    @pl.when(block * Q >= length)
    def _():
        norm_ref[...] = jnp.zeros_like(norm_ref)
        stat_ref[...] = jnp.zeros_like(stat_ref)

    @pl.when(block * Q < length)
    def _():
        base = 2 * inner + 2 * states
        gain = gain_row(wt_ref, base, heads)
        xs = [ref[...].astype(F32) for ref in x_refs]
        inv = rms_scale(xs, width)
        for k in range(4):
            cols = slice(k * part, (k + 1) * part)
            norm_ref[:, cols] = (xs[k] * inv * gain[:, cols]).astype(BF16)
        proj[...] = nt(wt_ref[: base + 16, :], norm_ref[...])

        raw = proj[2 * inner : base, :]
        bc_ref[...] = raw
        bcz = conv(raw, btail[...], [bcc_ref[j] for j in range(5)])
        btail[...] = raw[:, HALF:]
        bcz_ref[...] = bcz
        shared = bcz * jax.nn.sigmoid(bcz)
        b_rows, c_rows = shared[:states], shared[states:]
        cb_blocks, b_time = intersection(b_rows, c_rows)
        c_low = c_rows.astype(BF16)

        step_raw = proj[base : base + heads, :] + twice(headc_ref[0])
        step_ref[...] = step_raw
        steps = softplus(step_raw)
        running = times_ones(
            steps * (twice(headc_ref[1]) * LOG2E), triangle(lambda s, t: s <= t)
        )
        run_ref[...] = running
        run_cols = jnp.transpose(running)
        ends = running[:, Q - 1 :]
        grow = jnp.exp2(running)
        to_end = jnp.exp2(ends - running)
        whole = jnp.exp2(ends)
        upper = upper_half()

        state_ref[...] = state[...]
        carried[...] = nn(state[...].astype(BF16), c_low)
        squares = jnp.zeros((1, Q), F32)
        for h in range(heads):
            rows = slice(h * per, (h + 1) * per)
            raw_v = proj[inner + h * per : inner + (h + 1) * per, :]
            gate = proj[rows, :]
            val_ref[rows, :] = raw_v
            gate_ref[rows, :] = gate
            z = conv(raw_v, vtail[rows, :], [chan_ref[j, rows, :] for j in range(5)])
            vtail[rows, :] = raw_v[:, HALF:]
            z_ref[rows, :] = z
            v = z * jax.nn.sigmoid(z)
            w = v * steps[h : h + 1]
            decays = decay_blocks(running[h : h + 1], run_cols[:, h : h + 1], upper)
            grid = stack_blocks(*[(d * g).astype(BF16) for d, g in zip(decays, cb_blocks)])
            y = nn(w.astype(BF16), grid) + carried[rows, :] * grow[h : h + 1]
            y_ref[rows, :] = y
            wdec[rows, :] = (w * to_end[h : h + 1]).astype(BF16)
            u = y + twice(chan_ref[6, rows, :]) * v
            m = u * gate * jax.nn.sigmoid(gate)
            m_ref[rows, :] = m
            squares = squares + jnp.sum(m * m, 0, keepdims=True)
        stat_ref[...] = squares
        fresh = nn(wdec[...], b_time)
        for h in range(heads):
            rows = slice(h * per, (h + 1) * per)
            state[rows, :] = state[rows, :] * whole[h : h + 1] + fresh[rows]


def middle_kernel(len_ref, *refs, seq, inner, inner_all, width, aliased):
    c0, c1, c2, c3, wo_ref, chan_ref, m_ref, sq_ref = refs[:8]
    nout_ref, gno_ref, b0, b1, b2, b3, stat_ref, gain_acc, nout = refs[8 + aliased :]
    block = pl.program_id(0)
    length = len_ref[seq]
    part = width // 4

    @pl.when(block == 0)
    def _():
        gain_acc[...] = jnp.zeros_like(gain_acc)

    @pl.when(block * Q >= length)
    def _():
        nout_ref[...] = jnp.zeros_like(nout_ref)
        stat_ref[...] = jnp.zeros_like(stat_ref)
        for ref in (b0, b1, b2, b3):
            ref[...] = jnp.zeros_like(ref)

    @pl.when(block * Q < length)
    def _():
        valid = valid_row(block, length)
        scale = lax.rsqrt(sq_ref[...] / inner_all + epsilon) * valid
        cot = jnp.concatenate([ref[...] for ref in (c0, c1, c2, c3)], 1)
        gno_ref[...] = nt(wo_ref[...], cot) * valid
        inners = jnp.zeros((1, Q), F32)
        for lo in range(0, inner, 64):
            rows = slice(lo, lo + 64)
            gain = twice(chan_ref[5, rows, :])
            m = m_ref[rows, :]
            gno = gno_ref[rows, :]
            nout[rows, :] = (m * scale * gain).astype(BF16)
            inners = inners + jnp.sum(gno * gain * m, 0, keepdims=True)
            gain_acc[rows, :] += fold(gno * m * scale)
        stat_ref[...] = inners
        nout_time = jnp.transpose(nout[...])
        nout_ref[...] = nout_time
        branch = nn(nout_time, wo_ref[...])
        for k, ref in enumerate((b0, b1, b2, b3)):
            ref[...] = branch[:, k * part : (k + 1) * part].astype(BF16)


def backward_kernel(len_ref, *refs, seq, inner, inner_all, heads, width, blocks, aliased):
    x_refs, (wt_ref, chan_ref, bcc_ref, headc_ref) = refs[:4], refs[4:8]
    (gate_ref, val_ref, z_ref, y_ref, gno_ref, bc_ref, bcz_ref) = refs[8:15]
    (step_ref, run_ref, state_ref, sq_ref, stat_ref) = refs[15:20]
    refs = refs[:20] + refs[20 + aliased :]
    low_refs, g_refs, (chan_acc, bc_acc, head_acc, norm_acc) = refs[20:22], refs[22:26], refs[26:30]
    low, gstate, vhead, bhead, dcb, wdec, gudec, sent = refs[30:]
    step = pl.program_id(0)
    block = blocks - 1 - step
    length = len_ref[seq]
    per = inner // heads
    part = width // 4
    states = bc_ref.shape[0] // 2
    base = 2 * inner + 2 * states

    @pl.when(step == 0)
    def _():
        chan_acc[...] = jnp.zeros_like(chan_acc)
        bc_acc[...] = jnp.zeros_like(bc_acc)
        head_acc[...] = jnp.zeros_like(head_acc)
        norm_acc[...] = jnp.zeros_like(norm_acc)
        low[base:, :] = jnp.zeros_like(low[base:, :])
        gstate[...] = jnp.zeros_like(gstate)
        vhead[...] = jnp.zeros_like(vhead)
        bhead[...] = jnp.zeros_like(bhead)

    @pl.when(block * Q >= length)
    def _():
        for ref in (*low_refs, *g_refs):
            ref[...] = jnp.zeros_like(ref)

    @pl.when(block * Q < length)
    def _():
        inv_gate = lax.rsqrt(sq_ref[...] / inner_all + epsilon)
        pull = inv_gate * inv_gate * inv_gate * stat_ref[...] / inner_all

        bcz = bcz_ref[...]
        sig = jax.nn.sigmoid(bcz)
        shared = bcz * sig
        shared_slope = sig + shared * (1.0 - sig)
        b_rows, c_rows = shared[:states], shared[states:]
        cb_blocks, _ = intersection(b_rows, c_rows)
        b_low, c_low = b_rows.astype(BF16), c_rows.astype(BF16)

        step_raw = step_ref[...]
        steps = softplus(step_raw)
        running = run_ref[...]
        run_cols = jnp.transpose(running)
        ends = running[:, Q - 1 :]
        grow = jnp.exp2(running)
        to_end = jnp.exp2(ends - running)
        whole = jnp.exp2(ends)
        upper = upper_half()

        sent[...] = nn(gstate[...].astype(BF16), b_low)
        direct, both, after, through = [], [], [], []
        for h in range(heads):
            rows = slice(h * per, (h + 1) * per)
            gate, z, y, gno = gate_ref[rows, :], z_ref[rows, :], y_ref[rows, :], gno_ref[rows, :]
            gain = twice(chan_ref[5, rows, :])
            skip = twice(chan_ref[6, rows, :])
            sig_g = jax.nn.sigmoid(gate)
            silu_g = gate * sig_g
            sig_z = jax.nn.sigmoid(z)
            v = z * sig_z
            u = y + skip * v
            m = u * silu_g
            gm = inv_gate * gain * gno - m * pull
            low[rows, :] = (gm * u * (sig_g + silu_g * (1.0 - sig_g))).astype(BF16)
            gu = gm * silu_g
            chan_acc[5, rows, :] += fold(gu * v)
            w = v * steps[h : h + 1]
            w_low, gu_low = w.astype(BF16), gu.astype(BF16)
            decays = decay_blocks(running[h : h + 1], run_cols[:, h : h + 1], upper)
            grid = stack_blocks(*[(d * g).astype(BF16) for d, g in zip(decays, cb_blocks)])
            gw_in = nt(gu_low, grid)
            pair = nn(jnp.transpose(w_low), gu_low)
            pieces = (pair[:HALF, :HALF], pair[:HALF, HALF:], pair[HALF:, HALF:])
            for i in range(3):
                if h == 0:
                    dcb[i] = decays[i] * pieces[i]
                else:
                    dcb[i] += decays[i] * pieces[i]
            gs = gstate[rows, :]
            gw_out = sent[rows, :] * to_end[h : h + 1]
            gw = gw_in + gw_out
            direct.append(jnp.sum(gw * v, 0, keepdims=True))
            both.append(
                jnp.sum(gu_low.astype(F32) * y - gw_in * w_low.astype(F32), 0, keepdims=True)
            )
            after.append(jnp.sum(gw_out * w, 0, keepdims=True))
            through.append(
                jnp.sum(gs * state_ref[rows, :], 0, keepdims=True) * whole[h : h + 1]
            )
            gud = (gu * grow[h : h + 1]).astype(BF16)
            gudec[rows, :] = gud
            wdec[rows, :] = (w * to_end[h : h + 1]).astype(BF16)
            gz = (skip * gu + gw * steps[h : h + 1]) * (sig_z + v * (1.0 - sig_z))
            taps = [chan_ref[j, rows, :] for j in range(4)]
            gv, shifted = conv_back(gz, vhead[rows, :], taps)
            vhead[rows, :] = gz[:, :HALF]
            raw_v = val_ref[rows, :]
            for k in range(4):
                chan_acc[3 - k, rows, :] += fold(shifted[k] * raw_v)
            chan_acc[4, rows, :] += fold(gz)
            low[inner + h * per : inner + (h + 1) * per, :] = gv.astype(BF16)

        direct = jnp.concatenate(direct, 0)
        both = jnp.concatenate(both, 0)
        after = jnp.concatenate(after, 0)
        through = jnp.sum(jnp.concatenate(through, 0), -1, keepdims=True)
        g_decay = (
            times_ones(both, triangle(lambda t, r: t >= r))
            + times_ones(after, triangle(lambda s, r: s < r))
            + through
        )
        head_acc[1] += fold(steps * g_decay)
        g_step = (direct + twice(headc_ref[1]) * g_decay) * jax.nn.sigmoid(step_raw)
        head_acc[0] += fold(g_step)
        low[base : base + 16, :] = jnp.concatenate(
            [g_step, jnp.zeros((16 - heads, Q), F32)], 0
        ).astype(BF16)

        dcb_low = stack_blocks(*[dcb[i].astype(BF16) for i in range(3)])
        gud, wd = gudec[...], wdec[...]
        gs_old = gstate[...]
        g_c = nn(b_low, dcb_low) + nn(jnp.transpose(state_ref[...]).astype(BF16), gud)
        g_b = nt(c_low, dcb_low) + nn(jnp.transpose(gs_old).astype(BF16), wd)
        fresh = nn(gud, jnp.transpose(c_low))
        for h in range(heads):
            rows = slice(h * per, (h + 1) * per)
            gstate[rows, :] = gs_old[rows] * whole[h : h + 1] + fresh[rows]
        gbcz = jnp.concatenate([g_b, g_c], 0) * shared_slope
        gbc, shifted = conv_back(gbcz, bhead[...], [bcc_ref[j] for j in range(4)])
        bhead[...] = gbcz[:, :HALF]
        raw = bc_ref[...]
        for k in range(4):
            bc_acc[3 - k] += fold(shifted[k] * raw)
        bc_acc[4] += fold(gbcz)
        low[2 * inner : base, :] = gbc.astype(BF16)

        lows = jnp.transpose(low[...])
        cut = low_refs[0].shape[1]
        low_refs[0][...] = lows[:, :cut]
        low_refs[1][...] = lows[:, cut:]
        g_norm = nn(lows, wt_ref[...])
        gain = gain_row(wt_ref, base, heads)
        xs = [ref[...].astype(F32) for ref in x_refs]
        inv = rms_scale(xs, width)
        prod = None
        for k in range(4):
            cols = slice(k * part, (k + 1) * part)
            here = g_norm[:, cols] * xs[k]
            norm_acc[:, cols] += jnp.sum((here * inv).reshape(Q // 8, 8, part), 0)
            weighted = here * gain[:, cols]
            prod = weighted if prod is None else prod + weighted
        pull_x = inv * inv * inv * (jnp.sum(prod, -1, keepdims=True) / width)
        for k in range(4):
            cols = slice(k * part, (k + 1) * part)
            g_refs[k][...] = (inv * gain[:, cols] * g_norm[:, cols] - xs[k] * pull_x).astype(BF16)


def shape(dims, kind=F32):
    return jax.ShapeDtypeStruct(dims, kind)


def params(count):
    return pltpu.CompilerParams(
        dimension_semantics=("arbitrary",) * count, vmem_limit_bytes=52 << 20
    )


def fixed(array):
    rank = array.ndim
    return pl.BlockSpec(array.shape, lambda *_: (0,) * rank, pipeline_mode=pl.Buffered(1))


def run_forward(seq, seqs, lengths, xs, wt, chan, bcc, headc, before):
    part = xs[0].shape[1]
    width = 4 * part
    inner, heads, states2 = chan.shape[1], headc.shape[1], bcc.shape[1]
    blocks = SEQ_LEN // Q
    rows = seqs * SEQ_LEN
    at = lambda c: seq * blocks + c
    col = lambda n: pl.BlockSpec((n, Q), lambda c, lens: (0, at(c)))
    out_shape = [
        shape((rows, width), BF16),
        *[shape((inner, rows))] * 5,
        *[shape((states2, rows))] * 2,
        *[shape((heads, rows))] * 2,
        shape((seqs * blocks * inner, states2 // 2)),
        shape((1, SEQ_LEN)),
    ]
    out_specs = [
        pl.BlockSpec((Q, width), lambda c, lens: (at(c), 0)),
        *[col(inner)] * 5,
        *[col(states2)] * 2,
        *[col(heads)] * 2,
        pl.BlockSpec((inner, states2 // 2), lambda c, lens: (at(c), 0)),
        pl.BlockSpec((1, Q), lambda c, lens: (0, c)),
    ]
    consts = (wt, chan, bcc, headc)
    return pl.pallas_call(
        functools.partial(
            forward_kernel,
            seq=seq,
            inner=inner,
            heads=heads,
            width=width,
            aliased=len(before),
        ),
        out_shape=out_shape,
        grid_spec=pltpu.PrefetchScalarGridSpec(
            num_scalar_prefetch=1,
            grid=(blocks,),
            in_specs=[
                *[pl.BlockSpec((Q, part), lambda c, lens: (c, 0))] * 4,
                *[fixed(array) for array in consts],
                *[pl.BlockSpec(memory_space=pl.ANY)] * len(before),
            ],
            out_specs=out_specs,
            scratch_shapes=[
                pltpu.VMEM((2 * inner + states2 + 16, Q), F32),
                pltpu.VMEM((inner, HALF), F32),
                pltpu.VMEM((states2, HALF), F32),
                pltpu.VMEM((inner, states2 // 2), F32),
                pltpu.VMEM((inner, Q), F32),
                pltpu.VMEM((inner, Q), BF16),
            ],
        ),
        input_output_aliases={9 + i: i for i in range(len(before))},
        compiler_params=params(1),
        name="mixer_forward",
    )(lengths, *xs, *consts, *before)


def run_middle(seq, lengths, cots, wo, chan, m, squares, inner_all, before):
    rows, part = cots[0].shape
    width = 4 * part
    inner = wo.shape[0]
    blocks = SEQ_LEN // Q
    at = lambda c: seq * blocks + c
    piece = pl.BlockSpec((Q, part), lambda c, lens: (at(c), 0))
    col = pl.BlockSpec((inner, Q), lambda c, lens: (0, at(c)))
    stat = pl.BlockSpec((1, Q), lambda c, lens: (0, c))
    return pl.pallas_call(
        functools.partial(
            middle_kernel,
            seq=seq,
            inner=inner,
            inner_all=inner_all,
            width=width,
            aliased=len(before),
        ),
        out_shape=[
            shape((rows, inner), BF16),
            shape((inner, rows)),
            *[shape((SEQ_LEN, part), BF16)] * 4,
            shape((1, SEQ_LEN)),
            shape((inner, HALF)),
        ],
        grid_spec=pltpu.PrefetchScalarGridSpec(
            num_scalar_prefetch=1,
            grid=(blocks,),
            in_specs=[
                *[piece] * 4,
                fixed(wo),
                fixed(chan),
                col,
                stat,
                *[pl.BlockSpec(memory_space=pl.ANY)] * len(before),
            ],
            out_specs=[
                pl.BlockSpec((Q, inner), lambda c, lens: (at(c), 0)),
                col,
                *[pl.BlockSpec((Q, part), lambda c, lens: (c, 0))] * 4,
                stat,
                pl.BlockSpec((inner, HALF), lambda c, lens: (0, 0)),
            ],
            scratch_shapes=[pltpu.VMEM((inner, Q), BF16)],
        ),
        input_output_aliases={9 + i: i for i in range(len(before))},
        compiler_params=params(1),
        name="mixer_middle",
    )(lengths, *cots, wo, chan, m, squares, *before)


def run_backward(
    seq, lengths, xs, wt, chan, bcc, headc, saved, squares, stat, inner_all, before
):
    part = xs[0].shape[1]
    width = 4 * part
    inner, heads, states2 = chan.shape[1], headc.shape[1], bcc.shape[1]
    blocks = SEQ_LEN // Q
    back = lambda c: blocks - 1 - c
    at = lambda c: seq * blocks + back(c)
    col = lambda n: pl.BlockSpec((n, Q), lambda c, lens: (0, at(c)))
    piece = pl.BlockSpec((Q, part), lambda c, lens: (back(c), 0))
    consts = (wt, chan, bcc, headc)
    cut = inner + inner // 2
    sets = (cut, wt.shape[0] - cut)
    accs = [(6, inner, HALF), (5, states2, HALF), (2, heads, HALF), (8, width)]
    keep = lambda dims: pl.BlockSpec(dims, lambda c, lens: (0,) * len(dims))
    return pl.pallas_call(
        functools.partial(
            backward_kernel,
            seq=seq,
            inner=inner,
            inner_all=inner_all,
            heads=heads,
            width=width,
            blocks=blocks,
            aliased=len(before),
        ),
        out_shape=[
            *[shape((saved[0].shape[1], count), BF16) for count in sets],
            *[shape((SEQ_LEN, part), BF16)] * 4,
            *[shape(dims) for dims in accs],
        ],
        grid_spec=pltpu.PrefetchScalarGridSpec(
            num_scalar_prefetch=1,
            grid=(blocks,),
            in_specs=[
                *[piece] * 4,
                *[fixed(array) for array in consts],
                *[col(inner)] * 5,
                *[col(states2)] * 2,
                *[col(heads)] * 2,
                pl.BlockSpec((inner, states2 // 2), lambda c, lens: (at(c), 0)),
                *[pl.BlockSpec((1, Q), lambda c, lens: (0, back(c)))] * 2,
                *[pl.BlockSpec(memory_space=pl.ANY)] * len(before),
            ],
            out_specs=[
                *[pl.BlockSpec((Q, count), lambda c, lens: (at(c), 0)) for count in sets],
                *[piece] * 4,
                *[keep(dims) for dims in accs],
            ],
            scratch_shapes=[
                pltpu.VMEM((wt.shape[0], Q), BF16),
                pltpu.VMEM((inner, states2 // 2), F32),
                pltpu.VMEM((inner, HALF), F32),
                pltpu.VMEM((states2, HALF), F32),
                pltpu.VMEM((3, HALF, HALF), F32),
                pltpu.VMEM((inner, Q), BF16),
                pltpu.VMEM((inner, Q), BF16),
                pltpu.VMEM((inner, Q), F32),
            ],
        ),
        input_output_aliases={21 + i: i for i in range(len(before))},
        compiler_params=params(1),
        name="mixer_backward",
    )(lengths, *xs, *consts, *saved, squares, stat, *before)


def finish_kernel(len_ref, base_ref, own_ref, beside_ref, last_ref, *refs, seq, masked):
    total = own_ref[...].astype(F32) + beside_ref[...].astype(F32) + last_ref[...].astype(F32)
    base = base_ref[...].astype(F32)
    if masked:
        count = base.shape[0]
        row = pl.program_id(0) * count + lax.broadcasted_iota(jnp.int32, (count, 1), 0)
        base = jnp.where(row < len_ref[seq], base, 0.0)
    refs[-1][...] = (base + total).astype(refs[-1].dtype)


def run_finish(seq, lengths, base, parts, kind, before):
    rows, part = base.shape
    count = SEQ_LEN // 2
    joint = pl.BlockSpec((count, part), lambda c, lens: (seq * 2 + c, 0))
    alone = pl.BlockSpec((count, part), lambda c, lens: (c, 0))
    return pl.pallas_call(
        functools.partial(finish_kernel, seq=seq, masked=kind == F32),
        out_shape=[shape((rows, part), kind)],
        grid_spec=pltpu.PrefetchScalarGridSpec(
            num_scalar_prefetch=1,
            grid=(2,),
            in_specs=[joint, *[alone] * 3, *[pl.BlockSpec(memory_space=pl.ANY)] * len(before)],
            out_specs=[joint],
        ),
        input_output_aliases={5 + i: i for i in range(len(before))},
        compiler_params=pltpu.CompilerParams(vmem_limit_bytes=16 << 20),
        name="finish",
    )(lengths, base, *parts, *before)


def exchange(a, axis, bit):
    return lax.ppermute(a, axis, [(i, i ^ bit) for i in range(lax.axis_size(axis))])


def exchange_sum(a, axis):
    bit = 1
    while bit < lax.axis_size(axis):
        a = a + exchange(a, axis, bit)
        bit *= 2
    return a


def gather_pieces(a):
    across = exchange(a, TENSOR, 2)
    beside = exchange(a, TENSOR, 1)
    return a, beside, across, exchange(across, TENSOR, 1)


def reduce_pieces(pieces, kind=BF16):
    own, beside, across, corner = pieces
    got_corner = exchange(corner.astype(kind), TENSOR, 1)
    got_beside = exchange(beside.astype(kind), TENSOR, 1)
    onward = (across.astype(F32) + got_corner.astype(F32)).astype(kind)
    return own, got_beside, exchange(onward, TENSOR, 2)


def place():
    index = lax.axis_index(DP)
    return index // 2, index % 2


def take(a, index, dim):
    return lax.dynamic_index_in_dim(a, index, dim, keepdims=False)


def round_to(count, tile):
    return count // tile * tile


def side_by_side(pick, extra):
    _, x = place()
    out = []
    for m in range(4):
        mine, other = pick(m)
        zero = [jnp.zeros((extra, mine.shape[1]), BF16)] if extra else []
        for side in (0, 1):
            out.append(jnp.concatenate([jnp.where(x == side, mine, other)] + zero, 0))
    return jnp.concatenate(out, 1)


def gather_other_way(a):
    tensor = lax.axis_index(TENSOR)
    whole = jnp.transpose(lax.all_gather(jnp.transpose(a), DP, axis=0, tiled=True))
    blocks = whole.reshape(a.shape[0], 4, -1)
    return jnp.concatenate([take(blocks, tensor ^ m, 1) for m in range(4)], 1)


ROUNDS = ((3, 2, 1), (1, 3, 2))


def exchange_z(a, turn):
    count, tensor_count = lax.axis_size(DP), lax.axis_size(TENSOR)
    pairs = [
        (d * tensor_count + t, (d ^ (2 * ROUNDS[t % 2][turn])) * tensor_count + t)
        for d in range(count)
        for t in range(tensor_count)
    ]
    return lax.ppermute(a, (DP, TENSOR), pairs)


def even_core():
    return lax.axis_index(TENSOR) % 2 == 0


def distance(turn):
    return jnp.where(even_core(), ROUNDS[0][turn], ROUNDS[1][turn])


def z_stack(a):
    return jnp.stack([a] + [exchange_z(a, turn) for turn in range(3)])


def slot_of(m):
    z, _ = place()
    j = (lax.axis_index(TENSOR) ^ m) ^ z
    return jnp.where(even_core(), (4 - j) % 4, jnp.where(j >= 2, 5 - j, j))


def weight_columns(a, extra, ready):
    if lax.axis_size(DP) != 8:
        return jnp.pad(gather_other_way(a), ((0, extra), (0, 0))), ready
    cut = round_to(a.shape[0] * 6 // 10, 16)
    first, second = a[:cut], a[cut:]
    beside = exchange(second, DP, 1)
    beside, ready = lax.optimization_barrier((beside, ready))
    mine = z_stack(first)
    other = exchange(first, DP, 1)
    pair = jnp.stack([second, beside])
    both = z_stack(pair)
    other = jnp.concatenate([other[None], exchange(mine[1:], DP, 1)], 0)

    def pick(m):
        slot = slot_of(m)
        low = take(both, slot, 0)
        return (
            jnp.concatenate([take(mine, slot, 0), low[0]], 0),
            jnp.concatenate([take(other, slot, 0), low[1]], 0),
        )

    return side_by_side(pick, extra), ready


def hidden_columns(a):
    if lax.axis_size(DP) != 8:
        return gather_other_way(a)
    both = z_stack(jnp.stack([a, exchange(a, DP, 1)]))

    def pick(m):
        low = take(both, slot_of(m), 0)
        return low[0], low[1]

    return side_by_side(pick, 0)


def along_z(pick):
    z, _ = place()
    total = pick(z).astype(F32)
    for turn in range(3):
        send = pick(z ^ distance(turn)).astype(BF16)
        total = total + exchange_z(send, turn).astype(F32)
    return total


def reduce_other_way(a):
    tensor = lax.axis_index(TENSOR)
    blocks = a.reshape(4, -1, a.shape[1])
    ordered = jnp.concatenate([take(blocks, tensor ^ m, 0) for m in range(4)], 0)
    return lax.psum_scatter(ordered.astype(F32), DP, scatter_dimension=0, tiled=True)


def rows_pair_first(a):
    if lax.axis_size(DP) != 8:
        return reduce_other_way(a)
    tensor = lax.axis_index(TENSOR)
    _, x = place()
    blocks = a.reshape(4, 2, a.shape[0] // 8, a.shape[1])
    got = exchange(take(blocks, 1 - x, 1), DP, 1).astype(F32)
    halves = take(blocks, x, 1).astype(F32) + got
    return along_z(lambda z: take(halves, z ^ tensor, 0))


def rows_line_first(a):
    if lax.axis_size(DP) != 8:
        return reduce_other_way(a)
    tensor = lax.axis_index(TENSOR)
    _, x = place()
    blocks = a.reshape(4, 2, a.shape[0] // 8, a.shape[1])
    pairs = along_z(lambda z: take(blocks, z ^ tensor, 0))
    late = exchange(take(pairs, 1 - x, 0).astype(BF16), DP, 1).astype(F32)
    return take(pairs, x, 0) + late


def direct_sum(a, axis, bits):
    total = a
    for bit in bits:
        total = total + exchange(a, axis, bit)
    return total


def over_rows(left, right):
    return lax.dot_general(
        left, right, (((0,), (0,)), ((), ())), preferred_element_type=BF16
    )


def lanes(a):
    return jnp.broadcast_to(a[..., None], a.shape + (HALF,))


def small_constants(conv_x, conv_bc, dt_bias, a_log, skip_d, gate_gain):
    per = conv_x.shape[1] // skip_d.shape[0]
    chan = lanes(jnp.concatenate([conv_x, gate_gain[None], jnp.repeat(skip_d, per)[None]], 0))
    return chan, lanes(conv_bc), lanes(jnp.stack([dt_bias, -jnp.exp(a_log)], 0))


def per_device(
    tokens,
    lengths,
    grad_out,
    norm_gain,
    w_gate,
    w_value,
    w_bc,
    w_dt,
    conv_x,
    conv_bc,
    dt_bias,
    a_log,
    skip_d,
    gate_gain,
    w_out,
):
    tensor_count = lax.axis_size(TENSOR)
    tensor = lax.axis_index(TENSOR)
    rows, part = tokens.shape
    seqs = rows // SEQ_LEN
    inner = w_gate.shape[1]
    inner_all = inner * tensor_count
    heads = w_dt.shape[1]
    states2 = w_bc.shape[1]
    base = 2 * inner + states2

    local = jnp.concatenate(
        [
            w_gate,
            w_value,
            w_bc,
            w_dt,
            norm_gain[:, None],
            jnp.zeros((w_gate.shape[0], 15 - heads), BF16),
        ],
        1,
    )
    xs = [gather_pieces(tokens[q * SEQ_LEN : (q + 1) * SEQ_LEN]) for q in range(seqs)]
    cots = gather_pieces(grad_out)
    ready = small_constants(conv_x, conv_bc, dt_bias, a_log, skip_d, gate_gain)
    wt, (turned, *ready) = weight_columns(
        jnp.transpose(local), HALF - 16, (jnp.transpose(w_out), *ready)
    )
    wo = hidden_columns(turned)
    chan, bcc, headc = ready

    saved, squares = [], []
    for q in range(seqs):
        *saved, here = run_forward(q, seqs, lengths, xs[q], wt, chan, bcc, headc, saved)
        squares.append(direct_sum(here, TENSOR, (1, 2, 3)))
    normed, gate, val, z, y, m, *shared = saved
    middle, stats, gain_acc, branches = [], [], None, []
    for q in range(seqs):
        *middle, stat, here = run_middle(
            q, lengths, cots, wo, chan, m, squares[q], inner_all, middle
        )
        middle, branch = middle[:2], middle[2:]
        stats.append(direct_sum(stat, TENSOR, (1, 2, 3)))
        gain_acc = here if gain_acc is None else gain_acc + here
        branches.append(reduce_pieces(branch))
    nout, gno = middle
    g_out = jnp.concatenate([over_rows(cot, nout) for cot in cots], 0)
    grad_out_rows = rows_line_first(g_out)
    out_rows = []
    for q in range(seqs):
        out_rows = run_finish(q, lengths, tokens, branches[q], BF16, out_rows)

    grad_rows, accs, lows = [], None, []
    kept = (gate, val, z, y, gno, *shared)
    for q in range(seqs):
        *lows, g0, g1, g2, g3, a0, a1, a2, a3 = run_backward(
            q, lengths, xs[q], wt, chan, bcc, headc, kept, squares[q], stats[q], inner_all, lows
        )
        here = (a0, a1, a2, a3)
        accs = here if accs is None else [a + b for a, b in zip(accs, here)]
        grad_rows.append(reduce_pieces((g0, g1, g2, g3)))
    sum_b = over_rows(normed, lows[1])
    sum_a = over_rows(normed, lows[0])
    sums = (sum_a, sum_b)
    inputs, grad_rows = grad_rows, []
    for q in range(seqs):
        grad_rows = run_finish(q, lengths, grad_out, inputs[q], F32, grad_rows)

    chan_acc, bc_acc, head_acc, norm_acc = accs
    grads = jnp.concatenate([rows_pair_first(sums[0]), rows_line_first(sums[1])], 1)
    rest = grads[:, 2 * inner :].reshape(tensor_count, -1, states2 + HALF)
    rest = sum(reduce_pieces([take(rest, tensor ^ i, 0) for i in range(4)], F32))
    norm = jnp.sum(norm_acc, 0).reshape(tensor_count, part)
    norm = jnp.concatenate([take(norm, tensor ^ i, 0) for i in range(tensor_count)])
    sizes = [5 * inner, inner, inner, 2 * heads]
    flat = jnp.concatenate(
        [
            jnp.sum(chan_acc, -1).reshape(-1),
            jnp.sum(gain_acc, -1),
            jnp.sum(head_acc, -1).reshape(-1),
            jnp.sum(bc_acc, -1).reshape(-1),
            norm,
        ]
    )
    if lax.axis_size(DP) == 8:
        flat = direct_sum(flat, DP, (1,))
        flat = direct_sum(flat, DP, (2, 4, 6))
    else:
        flat = exchange_sum(flat, DP)
    cuts = [sum(sizes[: i + 1]) for i in range(4)]
    g_conv, g_skip, g_gain, g_head, everywhere = jnp.split(flat, cuts)
    everywhere = direct_sum(everywhere, TENSOR, (1, 2, 3))
    g_conv_bc = everywhere[: 5 * states2]
    share = part // lax.axis_size(DP)
    first = 5 * states2 + (lax.axis_index(DP) * tensor_count + tensor) * share
    g_norm = lax.dynamic_slice_in_dim(everywhere, first, share, 0)
    return (
        out_rows[0],
        grad_rows[0],
        g_norm,
        grads[:, :inner],
        grads[:, inner : 2 * inner],
        rest[:, :states2],
        grads[:, base : base + heads],
        g_conv.reshape(5, inner),
        g_conv_bc.reshape(5, states2),
        g_head[:heads],
        g_head[heads:] * -jnp.exp(a_log),
        jnp.sum(g_skip.reshape(heads, -1), -1),
        g_gain,
        grad_out_rows,
    )


def solution(mesh):
    return mapped(mesh)


def mapped(mesh):
    both = (DP, TENSOR)
    return jax.shard_map(
        per_device,
        mesh=mesh,
        in_specs=(
            P(DP, TENSOR),
            P(DP),
            P(DP, TENSOR),
            P(DP),
            P(DP, TENSOR),
            P(DP, TENSOR),
            P(DP, None),
            P(DP, TENSOR),
            P(None, TENSOR),
            P(),
            P(TENSOR),
            P(TENSOR),
            P(TENSOR),
            P(TENSOR),
            P(DP, TENSOR),
        ),
        out_specs=(
            P(DP, TENSOR),
            P(DP, TENSOR),
            P(both),
            P(DP, TENSOR),
            P(DP, TENSOR),
            P(both, None),
            P(DP, TENSOR),
            P(None, TENSOR),
            P(),
            P(TENSOR),
            P(TENSOR),
            P(TENSOR),
            P(TENSOR),
            P(DP, TENSOR),
        ),
        check_vma=False,
    )
```

```python
import functools

import jax
import jax.numpy as jnp
from jax import lax
from jax.experimental import pallas as pl
from jax.experimental.pallas import tpu as pltpu
from jax.sharding import PartitionSpec as P


SEQ_LEN = 2048
Q = 256
HALF = 128
F32 = jnp.float32
BF16 = jnp.bfloat16
epsilon = 1e-05
NEG = -1e30
LOG2E = 1.4426950408889634
TENSOR = "tensor"
DP = "dp"


def nn(a, b):
    return lax.dot_general(a, b, (((1,), (0,)), ((), ())), preferred_element_type=F32)


def nt(a, b):
    return lax.dot_general(a, b, (((1,), (1,)), ((), ())), preferred_element_type=F32)


def split3(a):
    high = a.astype(BF16)
    rest = a - high.astype(F32)
    mid = rest.astype(BF16)
    low = (rest - mid.astype(F32)).astype(BF16)
    return high, mid, low


def times_ones(a, ones):
    rows = a.shape[0]
    got = nn(jnp.concatenate(split3(a), 0), ones)
    return got[:rows] + got[rows : 2 * rows] + got[2 * rows :]


def twice(a):
    return jnp.concatenate([a, a], 1)


def fold(a):
    return a[:, :HALF] + a[:, HALF:]


def triangle(keep):
    row = lax.broadcasted_iota(jnp.int32, (Q, Q), 0)
    col = lax.broadcasted_iota(jnp.int32, (Q, Q), 1)
    return jnp.where(keep(row, col), 1.0, 0.0).astype(BF16)


def conv(raw, tail, taps):
    ext = jnp.concatenate([tail, raw], 1)
    total = twice(taps[4]) + twice(taps[3]) * raw
    for k in range(1, 4):
        total = total + twice(taps[3 - k]) * pltpu.roll(ext, k, 1)[:, HALF:]
    return total


def conv_back(grad, head, taps):
    ext = jnp.concatenate([grad, head], 1)
    shifted = [grad] + [pltpu.roll(ext, 3 * HALF - k, 1)[:, :Q] for k in range(1, 4)]
    total = twice(taps[3]) * grad
    for k in range(1, 4):
        total = total + twice(taps[3 - k]) * shifted[k]
    return total, shifted


def decay_blocks(run_row, run_col, upper):
    early, late = run_row[:, :HALF], run_row[:, HALF:]
    col_early = jnp.broadcast_to(run_col[:HALF], (HALF, HALF))
    col_late = jnp.broadcast_to(run_col[HALF:], (HALF, HALF))
    first = jnp.exp2(jnp.where(upper, early - col_early, NEG))
    cross = jnp.exp2(late - col_early)
    second = jnp.exp2(jnp.where(upper, late - col_late, NEG))
    return first, cross, second


def stack_blocks(first, cross, second):
    zero = jnp.zeros((HALF, HALF), first.dtype)
    return jnp.concatenate(
        [jnp.concatenate([first, cross], 1), jnp.concatenate([zero, second], 1)], 0
    )


def intersection(b_rows, c_rows):
    b_time = jnp.transpose(b_rows)
    b_high = b_time.astype(BF16)
    b_low = (b_time - b_high.astype(F32)).astype(BF16)
    c_high = c_rows.astype(BF16)
    c_low = (c_rows - c_high.astype(F32)).astype(BF16)
    full = nn(
        jnp.concatenate([b_high, b_low, b_high], 1), jnp.concatenate([c_high, c_high, c_low], 0)
    )
    return (full[:HALF, :HALF], full[:HALF, HALF:], full[HALF:, HALF:]), b_high


def rms_scale(xs, width):
    total = xs[0] * xs[0]
    for x in xs[1:]:
        total = total + x * x
    return lax.rsqrt(jnp.sum(total, -1, keepdims=True) / width + epsilon)


def gain_row(wt_ref, base, heads):
    return wt_ref[base : base + 16, :].astype(F32)[heads : heads + 1]


def softplus(a):
    return jnp.maximum(a, 0.0) + jnp.log1p(jnp.exp(-jnp.abs(a)))


def upper_half():
    row = lax.broadcasted_iota(jnp.int32, (HALF, HALF), 0)
    return row <= lax.broadcasted_iota(jnp.int32, (HALF, HALF), 1)


def valid_row(block, length):
    pos = block * Q + lax.broadcasted_iota(jnp.int32, (1, Q), 1)
    return jnp.where(pos < length, 1.0, 0.0)


def forward_kernel(len_ref, *refs, seq, inner, heads, width, aliased):
    x_refs, (wt_ref, chan_ref, bcc_ref, headc_ref) = refs[:4], refs[4:8]
    refs = refs[8 + aliased :]
    (norm_ref, gate_ref, val_ref, z_ref, y_ref, m_ref, bc_ref, bcz_ref) = refs[:8]
    (step_ref, run_ref, state_ref, stat_ref, proj, vtail, btail, state, carried, wdec) = refs[8:]
    block = pl.program_id(0)
    length = len_ref[seq]
    per = inner // heads
    part = width // 4
    states = bc_ref.shape[0] // 2

    @pl.when(block == 0)
    def _():
        vtail[...] = jnp.zeros_like(vtail)
        btail[...] = jnp.zeros_like(btail)
        state[...] = jnp.zeros_like(state)

    @pl.when(block * Q >= length)
    def _():
        norm_ref[...] = jnp.zeros_like(norm_ref)
        stat_ref[...] = jnp.zeros_like(stat_ref)

    @pl.when(block * Q < length)
    def _():
        base = 2 * inner + 2 * states
        gain = gain_row(wt_ref, base, heads)
        xs = [ref[...].astype(F32) for ref in x_refs]
        inv = rms_scale(xs, width)
        for k in range(4):
            cols = slice(k * part, (k + 1) * part)
            norm_ref[:, cols] = (xs[k] * inv * gain[:, cols]).astype(BF16)
        half = inner // 2
        for lo, hi in ((2 * inner, base + 16), (inner, inner + half), (0, half)):
            proj[lo:hi, :] = nt(wt_ref[lo:hi, :], norm_ref[...])

        raw = proj[2 * inner : base, :]
        bc_ref[...] = raw
        bcz = conv(raw, btail[...], [bcc_ref[j] for j in range(5)])
        btail[...] = raw[:, HALF:]
        bcz_ref[...] = bcz
        shared = bcz * jax.nn.sigmoid(bcz)
        b_rows, c_rows = shared[:states], shared[states:]
        cb_blocks, b_time = intersection(b_rows, c_rows)
        c_low = c_rows.astype(BF16)

        step_raw = proj[base : base + heads, :] + twice(headc_ref[0])
        step_ref[...] = step_raw
        steps = softplus(step_raw)
        running = times_ones(
            steps * (twice(headc_ref[1]) * LOG2E), triangle(lambda s, t: s <= t)
        )
        run_ref[...] = running
        run_cols = jnp.transpose(running)
        ends = running[:, Q - 1 :]
        grow = jnp.exp2(running)
        to_end = jnp.exp2(ends - running)
        whole = jnp.exp2(ends)
        upper = upper_half()

        state_ref[...] = state[...]
        carried[...] = nn(state[...].astype(BF16), c_low)
        squares = jnp.zeros((1, Q), F32)
        for h in range(heads):
            if h == 0:
                for lo in (half, inner + half):
                    proj[lo : lo + half, :] = nt(wt_ref[lo : lo + half, :], norm_ref[...])
            rows = slice(h * per, (h + 1) * per)
            raw_v = proj[inner + h * per : inner + (h + 1) * per, :]
            gate = proj[rows, :]
            val_ref[rows, :] = raw_v
            gate_ref[rows, :] = gate
            z = conv(raw_v, vtail[rows, :], [chan_ref[j, rows, :] for j in range(5)])
            vtail[rows, :] = raw_v[:, HALF:]
            z_ref[rows, :] = z
            v = z * jax.nn.sigmoid(z)
            w = v * steps[h : h + 1]
            decays = decay_blocks(running[h : h + 1], run_cols[:, h : h + 1], upper)
            grid = stack_blocks(*[(d * g).astype(BF16) for d, g in zip(decays, cb_blocks)])
            y = nn(w.astype(BF16), grid) + carried[rows, :] * grow[h : h + 1]
            y_ref[rows, :] = y
            wdec[rows, :] = (w * to_end[h : h + 1]).astype(BF16)
            u = y + twice(chan_ref[6, rows, :]) * v
            m = u * gate * jax.nn.sigmoid(gate)
            m_ref[rows, :] = m.astype(BF16)
            squares = squares + jnp.sum(m * m, 0, keepdims=True)
        stat_ref[...] = squares
        fresh = nn(wdec[...], b_time)
        for h in range(heads):
            rows = slice(h * per, (h + 1) * per)
            state[rows, :] = state[rows, :] * whole[h : h + 1] + fresh[rows]


def middle_kernel(len_ref, *refs, seq, inner, inner_all, width, aliased):
    c0, c1, c2, c3, wo_ref, chan_ref, m_ref, sq_ref = refs[:8]
    nout_ref, gno_ref, b0, b1, b2, b3, stat_ref, gain_acc, nout = refs[8 + aliased :]
    block = pl.program_id(0)
    length = len_ref[seq]
    part = width // 4

    @pl.when(block == 0)
    def _():
        gain_acc[...] = jnp.zeros_like(gain_acc)

    @pl.when(block * Q >= length)
    def _():
        nout_ref[...] = jnp.zeros_like(nout_ref)
        stat_ref[...] = jnp.zeros_like(stat_ref)
        for ref in (b0, b1, b2, b3):
            ref[...] = jnp.zeros_like(ref)

    @pl.when(block * Q < length)
    def _():
        valid = valid_row(block, length)
        scale = lax.rsqrt(sq_ref[...] / inner_all + epsilon) * valid
        cot = jnp.concatenate([ref[...] for ref in (c0, c1, c2, c3)], 1)
        gno_ref[...] = (nt(wo_ref[...], cot) * valid).astype(BF16)
        inners = jnp.zeros((1, Q), F32)
        for lo in range(0, inner, 64):
            rows = slice(lo, lo + 64)
            gain = twice(chan_ref[5, rows, :])
            m = m_ref[rows, :].astype(F32)
            gno = gno_ref[rows, :].astype(F32)
            nout[rows, :] = (m * scale * gain).astype(BF16)
            inners = inners + jnp.sum(gno * gain * m, 0, keepdims=True)
            gain_acc[rows, :] += fold(gno * m * scale)
        stat_ref[...] = inners
        nout_time = jnp.transpose(nout[...])
        nout_ref[...] = nout_time
        branch = nn(nout_time, wo_ref[...])
        for k, ref in enumerate((b0, b1, b2, b3)):
            ref[...] = branch[:, k * part : (k + 1) * part].astype(BF16)


def backward_kernel(len_ref, *refs, seq, inner, inner_all, heads, width, blocks, aliased):
    x_refs, (wt_ref, chan_ref, bcc_ref, headc_ref) = refs[:4], refs[4:8]
    (gate_ref, val_ref, z_ref, y_ref, gno_ref, bc_ref, bcz_ref) = refs[8:15]
    (step_ref, run_ref, state_ref, sq_ref, stat_ref) = refs[15:20]
    refs = refs[:20] + refs[20 + aliased :]
    low_refs, g_refs, (chan_acc, bc_acc, head_acc, norm_acc) = refs[20:22], refs[22:26], refs[26:30]
    low, gstate, vhead, bhead, dcb, wdec, gudec, sent = refs[30:]
    step = pl.program_id(0)
    block = blocks - 1 - step
    length = len_ref[seq]
    per = inner // heads
    part = width // 4
    states = bc_ref.shape[0] // 2
    base = 2 * inner + 2 * states

    @pl.when(step == 0)
    def _():
        chan_acc[...] = jnp.zeros_like(chan_acc)
        bc_acc[...] = jnp.zeros_like(bc_acc)
        head_acc[...] = jnp.zeros_like(head_acc)
        norm_acc[...] = jnp.zeros_like(norm_acc)
        low[base:, :] = jnp.zeros_like(low[base:, :])
        gstate[...] = jnp.zeros_like(gstate)
        vhead[...] = jnp.zeros_like(vhead)
        bhead[...] = jnp.zeros_like(bhead)

    @pl.when(block * Q >= length)
    def _():
        for ref in (*low_refs, *g_refs):
            ref[...] = jnp.zeros_like(ref)

    @pl.when(block * Q < length)
    def _():
        inv_gate = lax.rsqrt(sq_ref[...] / inner_all + epsilon)
        pull = inv_gate * inv_gate * inv_gate * stat_ref[...] / inner_all

        bcz = bcz_ref[...]
        sig = jax.nn.sigmoid(bcz)
        shared = bcz * sig
        shared_slope = sig + shared * (1.0 - sig)
        b_rows, c_rows = shared[:states], shared[states:]
        cb_blocks, _ = intersection(b_rows, c_rows)
        b_low, c_low = b_rows.astype(BF16), c_rows.astype(BF16)

        step_raw = step_ref[...]
        steps = softplus(step_raw)
        running = run_ref[...]
        run_cols = jnp.transpose(running)
        ends = running[:, Q - 1 :]
        grow = jnp.exp2(running)
        to_end = jnp.exp2(ends - running)
        whole = jnp.exp2(ends)
        upper = upper_half()

        sent[...] = nn(gstate[...].astype(BF16), b_low)
        direct, both, after, through = [], [], [], []
        for h in range(heads):
            rows = slice(h * per, (h + 1) * per)
            gate, z, y = gate_ref[rows, :], z_ref[rows, :], y_ref[rows, :]
            gno = gno_ref[rows, :].astype(F32)
            gain = twice(chan_ref[5, rows, :])
            skip = twice(chan_ref[6, rows, :])
            sig_g = jax.nn.sigmoid(gate)
            silu_g = gate * sig_g
            sig_z = jax.nn.sigmoid(z)
            v = z * sig_z
            u = y + skip * v
            m = u * silu_g
            gm = inv_gate * gain * gno - m * pull
            low[rows, :] = (gm * u * (sig_g + silu_g * (1.0 - sig_g))).astype(BF16)
            gu = gm * silu_g
            chan_acc[5, rows, :] += fold(gu * v)
            w = v * steps[h : h + 1]
            w_low, gu_low = w.astype(BF16), gu.astype(BF16)
            decays = decay_blocks(running[h : h + 1], run_cols[:, h : h + 1], upper)
            grid = stack_blocks(*[(d * g).astype(BF16) for d, g in zip(decays, cb_blocks)])
            gw_in = nt(gu_low, grid)
            pair = nn(jnp.transpose(w_low), gu_low)
            pieces = (pair[:HALF, :HALF], pair[:HALF, HALF:], pair[HALF:, HALF:])
            for i in range(3):
                if h == 0:
                    dcb[i] = decays[i] * pieces[i]
                else:
                    dcb[i] += decays[i] * pieces[i]
            gs = gstate[rows, :]
            gw_out = sent[rows, :] * to_end[h : h + 1]
            gw = gw_in + gw_out
            direct.append(jnp.sum(gw * v, 0, keepdims=True))
            both.append(
                jnp.sum(gu_low.astype(F32) * y - gw_in * w_low.astype(F32), 0, keepdims=True)
            )
            after.append(jnp.sum(gw_out * w, 0, keepdims=True))
            through.append(
                jnp.sum(gs * state_ref[rows, :], 0, keepdims=True) * whole[h : h + 1]
            )
            gud = (gu * grow[h : h + 1]).astype(BF16)
            gudec[rows, :] = gud
            wdec[rows, :] = (w * to_end[h : h + 1]).astype(BF16)
            gz = (skip * gu + gw * steps[h : h + 1]) * (sig_z + v * (1.0 - sig_z))
            taps = [chan_ref[j, rows, :] for j in range(4)]
            gv, shifted = conv_back(gz, vhead[rows, :], taps)
            vhead[rows, :] = gz[:, :HALF]
            raw_v = val_ref[rows, :]
            for k in range(4):
                chan_acc[3 - k, rows, :] += fold(shifted[k] * raw_v)
            chan_acc[4, rows, :] += fold(gz)
            low[inner + h * per : inner + (h + 1) * per, :] = gv.astype(BF16)

        direct = jnp.concatenate(direct, 0)
        both = jnp.concatenate(both, 0)
        after = jnp.concatenate(after, 0)
        through = jnp.sum(jnp.concatenate(through, 0), -1, keepdims=True)
        g_decay = (
            times_ones(both, triangle(lambda t, r: t >= r))
            + times_ones(after, triangle(lambda s, r: s < r))
            + through
        )
        head_acc[1] += fold(steps * g_decay)
        g_step = (direct + twice(headc_ref[1]) * g_decay) * jax.nn.sigmoid(step_raw)
        head_acc[0] += fold(g_step)
        low[base : base + 16, :] = jnp.concatenate(
            [g_step, jnp.zeros((16 - heads, Q), F32)], 0
        ).astype(BF16)

        dcb_low = stack_blocks(*[dcb[i].astype(BF16) for i in range(3)])
        gud, wd = gudec[...], wdec[...]
        gs_old = gstate[...]
        g_c = nn(b_low, dcb_low) + nn(jnp.transpose(state_ref[...]).astype(BF16), gud)
        g_b = nt(c_low, dcb_low) + nn(jnp.transpose(gs_old).astype(BF16), wd)
        fresh = nn(gud, jnp.transpose(c_low))
        for h in range(heads):
            rows = slice(h * per, (h + 1) * per)
            gstate[rows, :] = gs_old[rows] * whole[h : h + 1] + fresh[rows]
        gbcz = jnp.concatenate([g_b, g_c], 0) * shared_slope
        gbc, shifted = conv_back(gbcz, bhead[...], [bcc_ref[j] for j in range(4)])
        bhead[...] = gbcz[:, :HALF]
        raw = bc_ref[...]
        for k in range(4):
            bc_acc[3 - k] += fold(shifted[k] * raw)
        bc_acc[4] += fold(gbcz)
        low[2 * inner : base, :] = gbc.astype(BF16)

        lows = jnp.transpose(low[...])
        cut = low_refs[0].shape[1]
        low_refs[0][...] = lows[:, :cut]
        low_refs[1][...] = lows[:, cut:]
        g_norm = nn(lows, wt_ref[...])
        gain = gain_row(wt_ref, base, heads)
        xs = [ref[...].astype(F32) for ref in x_refs]
        inv = rms_scale(xs, width)
        prod = None
        for k in range(4):
            cols = slice(k * part, (k + 1) * part)
            here = g_norm[:, cols] * xs[k]
            norm_acc[:, cols] += jnp.sum((here * inv).reshape(Q // 8, 8, part), 0)
            weighted = here * gain[:, cols]
            prod = weighted if prod is None else prod + weighted
        pull_x = inv * inv * inv * (jnp.sum(prod, -1, keepdims=True) / width)
        for k in range(4):
            cols = slice(k * part, (k + 1) * part)
            g_refs[k][...] = (inv * gain[:, cols] * g_norm[:, cols] - xs[k] * pull_x).astype(BF16)


def shape(dims, kind=F32):
    return jax.ShapeDtypeStruct(dims, kind)


def params(count):
    return pltpu.CompilerParams(
        dimension_semantics=("arbitrary",) * count, vmem_limit_bytes=52 << 20
    )


def fixed(array):
    rank = array.ndim
    return pl.BlockSpec(array.shape, lambda *_: (0,) * rank, pipeline_mode=pl.Buffered(1))


def run_forward(seq, seqs, lengths, xs, wt, chan, bcc, headc, before):
    part = xs[0].shape[1]
    width = 4 * part
    inner, heads, states2 = chan.shape[1], headc.shape[1], bcc.shape[1]
    blocks = SEQ_LEN // Q
    rows = seqs * SEQ_LEN
    at = lambda c: seq * blocks + c
    col = lambda n: pl.BlockSpec((n, Q), lambda c, lens: (0, at(c)))
    out_shape = [
        shape((rows, width), BF16),
        *[shape((inner, rows))] * 4,
        shape((inner, rows), BF16),
        *[shape((states2, rows))] * 2,
        *[shape((heads, rows))] * 2,
        shape((seqs * blocks * inner, states2 // 2)),
        shape((1, SEQ_LEN)),
    ]
    out_specs = [
        pl.BlockSpec((Q, width), lambda c, lens: (at(c), 0)),
        *[col(inner)] * 5,
        *[col(states2)] * 2,
        *[col(heads)] * 2,
        pl.BlockSpec((inner, states2 // 2), lambda c, lens: (at(c), 0)),
        pl.BlockSpec((1, Q), lambda c, lens: (0, c)),
    ]
    consts = (wt, chan, bcc, headc)
    return pl.pallas_call(
        functools.partial(
            forward_kernel,
            seq=seq,
            inner=inner,
            heads=heads,
            width=width,
            aliased=len(before),
        ),
        out_shape=out_shape,
        grid_spec=pltpu.PrefetchScalarGridSpec(
            num_scalar_prefetch=1,
            grid=(blocks,),
            in_specs=[
                *[pl.BlockSpec((Q, part), lambda c, lens: (c, 0))] * 4,
                *[fixed(array) for array in consts],
                *[pl.BlockSpec(memory_space=pl.ANY)] * len(before),
            ],
            out_specs=out_specs,
            scratch_shapes=[
                pltpu.VMEM((2 * inner + states2 + 16, Q), F32),
                pltpu.VMEM((inner, HALF), F32),
                pltpu.VMEM((states2, HALF), F32),
                pltpu.VMEM((inner, states2 // 2), F32),
                pltpu.VMEM((inner, Q), F32),
                pltpu.VMEM((inner, Q), BF16),
            ],
        ),
        input_output_aliases={9 + i: i for i in range(len(before))},
        compiler_params=params(1),
        name="mixer_forward",
    )(lengths, *xs, *consts, *before)


def run_middle(seq, lengths, cots, wo, chan, m, squares, inner_all, before):
    rows, part = cots[0].shape
    width = 4 * part
    inner = wo.shape[0]
    blocks = SEQ_LEN // Q
    at = lambda c: seq * blocks + c
    piece = pl.BlockSpec((Q, part), lambda c, lens: (at(c), 0))
    col = pl.BlockSpec((inner, Q), lambda c, lens: (0, at(c)))
    stat = pl.BlockSpec((1, Q), lambda c, lens: (0, c))
    return pl.pallas_call(
        functools.partial(
            middle_kernel,
            seq=seq,
            inner=inner,
            inner_all=inner_all,
            width=width,
            aliased=len(before),
        ),
        out_shape=[
            shape((rows, inner), BF16),
            shape((inner, rows), BF16),
            *[shape((SEQ_LEN, part), BF16)] * 4,
            shape((1, SEQ_LEN)),
            shape((inner, HALF)),
        ],
        grid_spec=pltpu.PrefetchScalarGridSpec(
            num_scalar_prefetch=1,
            grid=(blocks,),
            in_specs=[
                *[piece] * 4,
                fixed(wo),
                fixed(chan),
                col,
                stat,
                *[pl.BlockSpec(memory_space=pl.ANY)] * len(before),
            ],
            out_specs=[
                pl.BlockSpec((Q, inner), lambda c, lens: (at(c), 0)),
                col,
                *[pl.BlockSpec((Q, part), lambda c, lens: (c, 0))] * 4,
                stat,
                pl.BlockSpec((inner, HALF), lambda c, lens: (0, 0)),
            ],
            scratch_shapes=[pltpu.VMEM((inner, Q), BF16)],
        ),
        input_output_aliases={9 + i: i for i in range(len(before))},
        compiler_params=params(1),
        name="mixer_middle",
    )(lengths, *cots, wo, chan, m, squares, *before)


def run_backward(
    seq, lengths, xs, wt, chan, bcc, headc, saved, squares, stat, inner_all, before
):
    part = xs[0].shape[1]
    width = 4 * part
    inner, heads, states2 = chan.shape[1], headc.shape[1], bcc.shape[1]
    blocks = SEQ_LEN // Q
    back = lambda c: blocks - 1 - c
    at = lambda c: seq * blocks + back(c)
    col = lambda n: pl.BlockSpec((n, Q), lambda c, lens: (0, at(c)))
    piece = pl.BlockSpec((Q, part), lambda c, lens: (back(c), 0))
    consts = (wt, chan, bcc, headc)
    cut = inner + inner // 2
    sets = (cut, wt.shape[0] - cut)
    accs = [(6, inner, HALF), (5, states2, HALF), (2, heads, HALF), (8, width)]
    keep = lambda dims: pl.BlockSpec(dims, lambda c, lens: (0,) * len(dims))
    return pl.pallas_call(
        functools.partial(
            backward_kernel,
            seq=seq,
            inner=inner,
            inner_all=inner_all,
            heads=heads,
            width=width,
            blocks=blocks,
            aliased=len(before),
        ),
        out_shape=[
            *[shape((saved[0].shape[1], count), BF16) for count in sets],
            *[shape((SEQ_LEN, part), BF16)] * 4,
            *[shape(dims) for dims in accs],
        ],
        grid_spec=pltpu.PrefetchScalarGridSpec(
            num_scalar_prefetch=1,
            grid=(blocks,),
            in_specs=[
                *[piece] * 4,
                *[fixed(array) for array in consts],
                *[col(inner)] * 5,
                *[col(states2)] * 2,
                *[col(heads)] * 2,
                pl.BlockSpec((inner, states2 // 2), lambda c, lens: (at(c), 0)),
                *[pl.BlockSpec((1, Q), lambda c, lens: (0, back(c)))] * 2,
                *[pl.BlockSpec(memory_space=pl.ANY)] * len(before),
            ],
            out_specs=[
                *[pl.BlockSpec((Q, count), lambda c, lens: (at(c), 0)) for count in sets],
                *[piece] * 4,
                *[keep(dims) for dims in accs],
            ],
            scratch_shapes=[
                pltpu.VMEM((wt.shape[0], Q), BF16),
                pltpu.VMEM((inner, states2 // 2), F32),
                pltpu.VMEM((inner, HALF), F32),
                pltpu.VMEM((states2, HALF), F32),
                pltpu.VMEM((3, HALF, HALF), F32),
                pltpu.VMEM((inner, Q), BF16),
                pltpu.VMEM((inner, Q), BF16),
                pltpu.VMEM((inner, Q), F32),
            ],
        ),
        input_output_aliases={21 + i: i for i in range(len(before))},
        compiler_params=params(1),
        name="mixer_backward",
    )(lengths, *xs, *consts, *saved, squares, stat, *before)


def finish_kernel(len_ref, base_ref, own_ref, beside_ref, last_ref, *refs, seq, masked):
    total = own_ref[...].astype(F32) + beside_ref[...].astype(F32) + last_ref[...].astype(F32)
    base = base_ref[...].astype(F32)
    if masked:
        count = base.shape[0]
        row = pl.program_id(0) * count + lax.broadcasted_iota(jnp.int32, (count, 1), 0)
        base = jnp.where(row < len_ref[seq], base, 0.0)
    refs[-1][...] = (base + total).astype(refs[-1].dtype)


def run_finish(seq, lengths, base, parts, kind, before):
    rows, part = base.shape
    count = SEQ_LEN // 2
    joint = pl.BlockSpec((count, part), lambda c, lens: (seq * 2 + c, 0))
    alone = pl.BlockSpec((count, part), lambda c, lens: (c, 0))
    return pl.pallas_call(
        functools.partial(finish_kernel, seq=seq, masked=kind == F32),
        out_shape=[shape((rows, part), kind)],
        grid_spec=pltpu.PrefetchScalarGridSpec(
            num_scalar_prefetch=1,
            grid=(2,),
            in_specs=[joint, *[alone] * 3, *[pl.BlockSpec(memory_space=pl.ANY)] * len(before)],
            out_specs=[joint],
        ),
        input_output_aliases={5 + i: i for i in range(len(before))},
        compiler_params=pltpu.CompilerParams(vmem_limit_bytes=16 << 20),
        name="finish",
    )(lengths, base, *parts, *before)


def exchange(a, axis, bit):
    return lax.ppermute(a, axis, [(i, i ^ bit) for i in range(lax.axis_size(axis))])


def exchange_sum(a, axis):
    bit = 1
    while bit < lax.axis_size(axis):
        a = a + exchange(a, axis, bit)
        bit *= 2
    return a


def gather_pieces(a):
    across = exchange(a, TENSOR, 2)
    beside = exchange(a, TENSOR, 1)
    return a, beside, across, exchange(across, TENSOR, 1)


def reduce_pieces(pieces, kind=BF16):
    own, beside, across, corner = pieces
    got_corner = exchange(corner.astype(kind), TENSOR, 1)
    got_beside = exchange(beside.astype(kind), TENSOR, 1)
    onward = (across.astype(F32) + got_corner.astype(F32)).astype(kind)
    return own, got_beside, exchange(onward, TENSOR, 2)


def place():
    index = lax.axis_index(DP)
    return index // 2, index % 2


def take(a, index, dim):
    return lax.dynamic_index_in_dim(a, index, dim, keepdims=False)


def round_to(count, tile):
    return count // tile * tile


def side_by_side(pick, extra):
    _, x = place()
    out = []
    for m in range(4):
        mine, other = pick(m)
        zero = [jnp.zeros((extra, mine.shape[1]), BF16)] if extra else []
        for side in (0, 1):
            out.append(jnp.concatenate([jnp.where(x == side, mine, other)] + zero, 0))
    return jnp.concatenate(out, 1)


def gather_other_way(a):
    tensor = lax.axis_index(TENSOR)
    whole = jnp.transpose(lax.all_gather(jnp.transpose(a), DP, axis=0, tiled=True))
    blocks = whole.reshape(a.shape[0], 4, -1)
    return jnp.concatenate([take(blocks, tensor ^ m, 1) for m in range(4)], 1)


ROUNDS = ((3, 2, 1), (1, 3, 2))


def exchange_z(a, turn):
    count, tensor_count = lax.axis_size(DP), lax.axis_size(TENSOR)
    pairs = [
        (d * tensor_count + t, (d ^ (2 * ROUNDS[t % 2][turn])) * tensor_count + t)
        for d in range(count)
        for t in range(tensor_count)
    ]
    return lax.ppermute(a, (DP, TENSOR), pairs)


def even_core():
    return lax.axis_index(TENSOR) % 2 == 0


def distance(turn):
    return jnp.where(even_core(), ROUNDS[0][turn], ROUNDS[1][turn])


def z_stack(a):
    return jnp.stack([a] + [exchange_z(a, turn) for turn in range(3)])


def slot_of(m):
    z, _ = place()
    j = (lax.axis_index(TENSOR) ^ m) ^ z
    return jnp.where(even_core(), (4 - j) % 4, jnp.where(j >= 2, 5 - j, j))


def weight_columns(a, extra, ready):
    if lax.axis_size(DP) != 8:
        return jnp.pad(gather_other_way(a), ((0, extra), (0, 0))), ready
    cut = round_to(a.shape[0] * 6 // 10, 16)
    first, second = a[:cut], a[cut:]
    beside = exchange(second, DP, 1)
    beside, ready = lax.optimization_barrier((beside, ready))
    mine = z_stack(first)
    other = exchange(first, DP, 1)
    pair = jnp.stack([second, beside])
    both = z_stack(pair)
    other = jnp.concatenate([other[None], exchange(mine[1:], DP, 1)], 0)

    def pick(m):
        slot = slot_of(m)
        low = take(both, slot, 0)
        return (
            jnp.concatenate([take(mine, slot, 0), low[0]], 0),
            jnp.concatenate([take(other, slot, 0), low[1]], 0),
        )

    return side_by_side(pick, extra), ready


def hidden_columns(a):
    if lax.axis_size(DP) != 8:
        return gather_other_way(a)
    both = z_stack(jnp.stack([a, exchange(a, DP, 1)]))

    def pick(m):
        low = take(both, slot_of(m), 0)
        return low[0], low[1]

    return side_by_side(pick, 0)


def along_z(pick):
    z, _ = place()
    total = pick(z).astype(F32)
    for turn in range(3):
        send = pick(z ^ distance(turn)).astype(BF16)
        total = total + exchange_z(send, turn).astype(F32)
    return total


def reduce_other_way(a):
    tensor = lax.axis_index(TENSOR)
    blocks = a.reshape(4, -1, a.shape[1])
    ordered = jnp.concatenate([take(blocks, tensor ^ m, 0) for m in range(4)], 0)
    return lax.psum_scatter(ordered.astype(F32), DP, scatter_dimension=0, tiled=True)


def rows_pair_first(a):
    if lax.axis_size(DP) != 8:
        return reduce_other_way(a)
    tensor = lax.axis_index(TENSOR)
    _, x = place()
    blocks = a.reshape(4, 2, a.shape[0] // 8, a.shape[1])
    got = exchange(take(blocks, 1 - x, 1), DP, 1).astype(F32)
    halves = take(blocks, x, 1).astype(F32) + got
    return along_z(lambda z: take(halves, z ^ tensor, 0))


def rows_line_first(a):
    if lax.axis_size(DP) != 8:
        return reduce_other_way(a)
    tensor = lax.axis_index(TENSOR)
    _, x = place()
    blocks = a.reshape(4, 2, a.shape[0] // 8, a.shape[1])
    pairs = along_z(lambda z: take(blocks, z ^ tensor, 0))
    late = exchange(take(pairs, 1 - x, 0).astype(BF16), DP, 1).astype(F32)
    return take(pairs, x, 0) + late


def direct_sum(a, axis, bits):
    total = a
    for bit in bits:
        total = total + exchange(a, axis, bit)
    return total


def over_rows(left, right):
    return lax.dot_general(
        left, right, (((0,), (0,)), ((), ())), preferred_element_type=BF16
    )


def lanes(a):
    return jnp.broadcast_to(a[..., None], a.shape + (HALF,))


def small_constants(conv_x, conv_bc, dt_bias, a_log, skip_d, gate_gain):
    per = conv_x.shape[1] // skip_d.shape[0]
    chan = lanes(jnp.concatenate([conv_x, gate_gain[None], jnp.repeat(skip_d, per)[None]], 0))
    return chan, lanes(conv_bc), lanes(jnp.stack([dt_bias, -jnp.exp(a_log)], 0))


def per_device(
    tokens,
    lengths,
    grad_out,
    norm_gain,
    w_gate,
    w_value,
    w_bc,
    w_dt,
    conv_x,
    conv_bc,
    dt_bias,
    a_log,
    skip_d,
    gate_gain,
    w_out,
):
    tensor_count = lax.axis_size(TENSOR)
    tensor = lax.axis_index(TENSOR)
    rows, part = tokens.shape
    seqs = rows // SEQ_LEN
    inner = w_gate.shape[1]
    inner_all = inner * tensor_count
    heads = w_dt.shape[1]
    states2 = w_bc.shape[1]
    base = 2 * inner + states2

    local = jnp.concatenate(
        [
            w_gate,
            w_value,
            w_bc,
            w_dt,
            norm_gain[:, None],
            jnp.zeros((w_gate.shape[0], 15 - heads), BF16),
        ],
        1,
    )
    xs = [gather_pieces(tokens[q * SEQ_LEN : (q + 1) * SEQ_LEN]) for q in range(seqs)]
    cots = gather_pieces(grad_out)
    ready = small_constants(conv_x, conv_bc, dt_bias, a_log, skip_d, gate_gain)
    wt, (turned, *ready) = weight_columns(
        jnp.transpose(local), HALF - 16, (jnp.transpose(w_out), *ready)
    )
    wo = hidden_columns(turned)
    chan, bcc, headc = ready

    saved, squares = [], []
    for q in range(seqs):
        *saved, here = run_forward(q, seqs, lengths, xs[q], wt, chan, bcc, headc, saved)
        squares.append(direct_sum(here, TENSOR, (1, 2, 3)))
    normed, gate, val, z, y, m, *shared = saved
    middle, stats, gain_acc, branches = [], [], None, []
    for q in range(seqs):
        *middle, stat, here = run_middle(
            q, lengths, cots, wo, chan, m, squares[q], inner_all, middle
        )
        middle, branch = middle[:2], middle[2:]
        stats.append(direct_sum(stat, TENSOR, (1, 2, 3)))
        gain_acc = here if gain_acc is None else gain_acc + here
        branches.append(reduce_pieces(branch))
    nout, gno = middle
    g_out = jnp.concatenate([over_rows(cot, nout) for cot in cots], 0)
    grad_out_rows = rows_line_first(g_out)
    out_rows = []
    for q in range(seqs):
        out_rows = run_finish(q, lengths, tokens, branches[q], BF16, out_rows)

    grad_rows, accs, lows = [], None, []
    kept = (gate, val, z, y, gno, *shared)
    for q in range(seqs):
        *lows, g0, g1, g2, g3, a0, a1, a2, a3 = run_backward(
            q, lengths, xs[q], wt, chan, bcc, headc, kept, squares[q], stats[q], inner_all, lows
        )
        here = (a0, a1, a2, a3)
        accs = here if accs is None else [a + b for a, b in zip(accs, here)]
        grad_rows.append(reduce_pieces((g0, g1, g2, g3)))
    sum_b = over_rows(normed, lows[1])
    sum_a = over_rows(normed, lows[0])
    sums = (sum_a, sum_b)
    inputs, grad_rows = grad_rows, []
    for q in range(seqs):
        grad_rows = run_finish(q, lengths, grad_out, inputs[q], F32, grad_rows)

    chan_acc, bc_acc, head_acc, norm_acc = accs
    grads = jnp.concatenate([rows_pair_first(sums[0]), rows_line_first(sums[1])], 1)
    rest = grads[:, 2 * inner :].reshape(tensor_count, -1, states2 + HALF)
    rest = sum(reduce_pieces([take(rest, tensor ^ i, 0) for i in range(4)], F32))
    norm = jnp.sum(norm_acc, 0).reshape(tensor_count, part)
    norm = jnp.concatenate([take(norm, tensor ^ i, 0) for i in range(tensor_count)])
    sizes = [5 * inner, inner, inner, 2 * heads]
    flat = jnp.concatenate(
        [
            jnp.sum(chan_acc, -1).reshape(-1),
            jnp.sum(gain_acc, -1),
            jnp.sum(head_acc, -1).reshape(-1),
            jnp.sum(bc_acc, -1).reshape(-1),
            norm,
        ]
    )
    if lax.axis_size(DP) == 8:
        flat = direct_sum(flat, DP, (1,))
        flat = direct_sum(flat, DP, (2, 4, 6))
    else:
        flat = exchange_sum(flat, DP)
    cuts = [sum(sizes[: i + 1]) for i in range(4)]
    g_conv, g_skip, g_gain, g_head, everywhere = jnp.split(flat, cuts)
    everywhere = direct_sum(everywhere, TENSOR, (1, 2, 3))
    g_conv_bc = everywhere[: 5 * states2]
    share = part // lax.axis_size(DP)
    first = 5 * states2 + (lax.axis_index(DP) * tensor_count + tensor) * share
    g_norm = lax.dynamic_slice_in_dim(everywhere, first, share, 0)
    return (
        out_rows[0],
        grad_rows[0],
        g_norm,
        grads[:, :inner],
        grads[:, inner : 2 * inner],
        rest[:, :states2],
        grads[:, base : base + heads],
        g_conv.reshape(5, inner),
        g_conv_bc.reshape(5, states2),
        g_head[:heads],
        g_head[heads:] * -jnp.exp(a_log),
        jnp.sum(g_skip.reshape(heads, -1), -1),
        g_gain,
        grad_out_rows,
    )


def solution(mesh):
    return mapped(mesh)


def mapped(mesh):
    both = (DP, TENSOR)
    return jax.shard_map(
        per_device,
        mesh=mesh,
        in_specs=(
            P(DP, TENSOR),
            P(DP),
            P(DP, TENSOR),
            P(DP),
            P(DP, TENSOR),
            P(DP, TENSOR),
            P(DP, None),
            P(DP, TENSOR),
            P(None, TENSOR),
            P(),
            P(TENSOR),
            P(TENSOR),
            P(TENSOR),
            P(TENSOR),
            P(DP, TENSOR),
        ),
        out_specs=(
            P(DP, TENSOR),
            P(DP, TENSOR),
            P(both),
            P(DP, TENSOR),
            P(DP, TENSOR),
            P(both, None),
            P(DP, TENSOR),
            P(None, TENSOR),
            P(),
            P(TENSOR),
            P(TENSOR),
            P(TENSOR),
            P(TENSOR),
            P(DP, TENSOR),
        ),
        check_vma=False,
    )
```
